128 devices in a mesh: tile: 32 (over x, y, core), slab: 4 (over z).
Axes of the slice: x: 4, y: 4, z: 4, core: 2. Of those that a mesh axis runs over, the one named last changes fastest.
Arguments:
- stored: float32 [128, 8, 256, 1024], P('tile', 'slab'), may hold values from -6 to 6
- offsets: int32 [2, 2, 128], P(None, None, ('tile', 'slab')), may hold values from 0 to 128
Outputs:
- surface: float32 [2, 128, 128, 1024], P(None, ('tile', 'slab'))
- peak: float32 [2, 128], P(None, ('tile', 'slab'))
The draws below stay inside these ranges and needn't reach their ends.
All inputs are finite; a program needn't handle non-finite values.
Results may differ from the reference program's by a relative error of at most 0.0003.
Values sent between devices are 32-bit elements; how exact they have to be, the bound alone decides.
No kernel may reach another device: no remote copies, remote signals or barrier semaphores. Data moves between devices by JAX's collectives and lax.ppermute only.
A program may use at most 192 MiB of HBM per device.

```python
import jax
import jax.numpy as jnp
from jax import lax

Z = 8
A = 128
L = 1024
BAND = 256
GC = 7
ROUNDS = 2
TILES = 128


def plant(drawn, own_key, smallest, high):
    place = [jax.random.randint(jax.random.fold_in(own_key, axis), (), 0, length) for axis, length in enumerate(drawn.shape)]
    widest = drawn.shape.index(max(drawn.shape))
    next_to = place[:widest] + [(place[widest] + 1) % drawn.shape[widest]] + place[widest + 1:]
    return drawn.at[tuple(place)].set(smallest).at[tuple(next_to)].set(high)


def block_levels(rng, dims, shards, smallest, largest):
    gain = 1.0
    for dim, shards_of in shards:
        steps = jax.random.uniform(jax.random.fold_in(jax.random.fold_in(rng, 6), dim), (shards_of,), jnp.float32, smallest / len(shards), largest / len(shards))
        gain = gain * jnp.repeat(jnp.exp(steps), dims[dim] // shards_of).reshape((-1,) + (1,) * (len(dims) - 1 - dim))
    return gain


def noise(own_key, dims, deviation, limit, shards=(), kind=jnp.bfloat16):
    drawn = jax.random.normal(own_key, dims, jnp.float32) * deviation
    if len(shards) > 0:
        drawn = block_levels(own_key, dims, shards, -0.22, 0.18) * drawn
    return jnp.clip(drawn, min=-limit, max=limit).astype(kind)


def setup_inputs(seed: int = 0) -> dict:
    arg_keys = jax.random.split(jax.random.key(seed), 3)
    return {
        "stored": noise(arg_keys[0], (TILES, Z, BAND, L), 1.0, 6.0, ((0, 32), (1, 4)), jnp.float32),
        "offsets": plant(jax.random.randint(arg_keys[1], (ROUNDS, 2, TILES), 0, BAND - A + 1), jax.random.fold_in(arg_keys[1], 1), 0, BAND - A).astype(jnp.int32),
    }


FLOOR = 0.25


def correlate(own_strip, partner_strip):
    spec_own = jnp.fft.fftn(own_strip, norm="ortho")
    spec_partner = jnp.fft.fftn(partner_strip, norm="ortho")
    cross = spec_own * jnp.conj(spec_partner)
    denom = jnp.maximum(jnp.abs(cross), FLOOR)
    field = jnp.real(jnp.fft.ifftn(cross / denom, norm="ortho"))
    return jnp.max(field, axis=0)


def reference(stored, offsets):
    tile_ids = jnp.arange(TILES, dtype=jnp.int32)
    zero = jnp.int32(0)
    surfaces = []
    for rnd in range(ROUNDS):
        stride = 1 if rnd == 0 else GC

        def one_pair(tile):
            partner = jnp.minimum(tile + stride, TILES - 1).astype(jnp.int32)
            if rnd == 0:
                valid = jnp.logical_and((tile % GC) != (GC - 1), (tile + 1) < TILES)
            else:
                valid = (tile + GC) < TILES
            own_strip = lax.dynamic_slice(stored[tile], (zero, offsets[rnd, 0, tile].astype(jnp.int32), zero), (Z, A, L))
            partner_strip = lax.dynamic_slice(stored[partner], (zero, offsets[rnd, 1, partner].astype(jnp.int32), zero), (Z, A, L))
            partner_strip = partner_strip * valid.astype(stored.dtype)
            return correlate(own_strip, partner_strip)

        surfaces.append(lax.map(one_pair, tile_ids))
    surface = jnp.stack(surfaces)
    peak = jnp.max(surface, axis=(2, 3))
    return surface, peak
```

```python
import functools
import math

import jax
import jax.numpy as jnp
from jax import lax
from jax.experimental import pallas as pl
from jax.experimental.pallas import tpu as pltpu
from jax.sharding import PartitionSpec as P

GC = 7
ROUNDS = 2
A = 128
L = 1024
Z = 8
FLOOR = 0.25
BF = jnp.bfloat16
F32 = jnp.float32
HALF = math.sqrt(0.5)


def split(x):
    hi = x.astype(BF)
    lo = (x - hi.astype(F32)).astype(BF)
    return hi, lo


def split_table(x):
    hi = lax.reduce_precision(x, exponent_bits=8, mantissa_bits=7)
    return hi.astype(BF), (x - hi).astype(BF)


def three_rows(x):
    hi, lo = split_table(x)
    return jnp.concatenate((hi, hi, lo), axis=0)


def three_cols(x):
    hi, lo = split_table(x)
    return jnp.concatenate((hi, hi, lo), axis=1)


def trig(index, total):
    angle = (index % total).astype(F32) * (2.0 * math.pi / total)
    return jnp.cos(angle), jnp.sin(angle)


def iota(length):
    return lax.optimization_barrier(jnp.arange(length, dtype=jnp.int32))


def along_tables():
    rows = iota(512)[:, None]
    m = iota(256)[None, :]
    n4 = rows[:256]
    m4 = m[:, :128]
    nyquist = (1 - 2 * (n4 % 2)).astype(F32)
    first = m4 == 0
    c0, s0 = trig(n4 * (4 * m4), L)
    c2, s2 = trig(n4 * (4 * m4 + 2), L)
    c1, s1 = trig(rows * (2 * m + 1), L)
    im0 = jnp.where(first, nyquist, -s0)
    scale = 1.0 / L
    fwd = (
        three_rows(scale * jnp.concatenate((c0, im0), axis=1)),
        three_rows(scale * jnp.concatenate((c2, -s2), axis=1)),
        three_rows(scale * jnp.concatenate((c1, -s1), axis=1)),
    )
    return fwd


def back_tables():
    cols = iota(512)[None, :]
    m = iota(256)[:, None]
    n4 = cols[:, :256]
    m4 = m[:128]
    nyquist = (1 - 2 * (n4 % 2)).astype(F32)
    first = m4 == 0
    c0, s0 = trig(n4 * (4 * m4), L)
    c2, s2 = trig(n4 * (4 * m4 + 2), L)
    c1, s1 = trig(cols * (2 * m + 1), L)
    scale = 1.0 / L
    re0 = jnp.where(first, scale, 2.0 * scale * c0)
    im0 = jnp.where(first, scale * nyquist, -2.0 * scale * s0)
    odd = 2.0 * scale * jnp.concatenate((c1[:128], -s1[:128], c1[128:], -s1[128:]), axis=0)
    return (
        three_rows(jnp.concatenate((re0, im0), axis=0)),
        three_rows(2.0 * scale * jnp.concatenate((c2, -s2), axis=0)),
        three_rows(odd),
    )


def across_forward(offset):
    v = iota(A)[:, None]
    r = iota(A)[None, :]
    c, s = trig((r - offset + A) * v, A)
    top = jnp.concatenate((c, s), axis=1)
    low = jnp.concatenate((-s, c), axis=1)
    return three_cols(jnp.concatenate((top, low), axis=0))


def across_back():
    v = iota(A)[None, :]
    a = iota(A)[:, None]
    c, s = trig(a * v, A)
    top = jnp.concatenate((c, -s), axis=1)
    low = jnp.concatenate((s, c), axis=1)
    return three_cols(jnp.concatenate((top, low), axis=0))


def edge_tables():
    lane = iota(A)
    i = lane[:, None]
    j = lane[None, :]
    inside = jnp.logical_and(i < Z, j < Z)
    c, s = trig(i * j, Z)
    c = jnp.where(inside, c, 0.0)
    s = jnp.where(inside, s, 0.0)
    fwd = jnp.concatenate(
        (jnp.concatenate((c, -s), axis=1), jnp.concatenate((s, c), axis=1)), axis=0
    )
    rev = jnp.concatenate(
        (jnp.concatenate((c, s), axis=1), jnp.concatenate((-s, c), axis=1)), axis=0
    )
    flip = ((i + j) % A == 0).astype(F32)
    return fwd, rev, flip


def dot3_left(x, table):
    hi, lo = split(x)
    return jnp.dot(jnp.concatenate((hi, lo, hi), axis=1), table, preferred_element_type=F32)


def dot3_right(table, x):
    hi, lo = split(x)
    return jnp.dot(table, jnp.concatenate((hi, lo, hi), axis=0), preferred_element_type=F32)


def choose(y_ref, offset):
    row = lax.broadcasted_iota(jnp.int32, (A, 512), 0)
    later = row >= offset
    real = jnp.where(later, y_ref[0, :A, :], y_ref[0, A:, :])
    imag = jnp.where(later, y_ref[1, :A, :], y_ref[1, A:, :])
    return jnp.concatenate((real, imag), axis=0)


def given_kernel(off_ref, x_ref, w0_ref, w2_ref, w1_ref, a_ref, y_ref, g0_ref, g1_ref):
    x = x_ref[0]
    low = x[:, :512]
    high = x[:, 512:]
    y0 = low + high
    d1 = dot3_left(low - high, w1_ref[...])
    y_ref[0, 0, :, 256:512] = d1[:, :256]
    y_ref[0, 1, :, 256:512] = d1[:, 256:]
    d0 = dot3_left(y0[:, :256] + y0[:, 256:], w0_ref[...])
    y_ref[0, 0, :, 0:128] = d0[:, :128]
    y_ref[0, 1, :, 0:128] = d0[:, 128:]
    d2 = dot3_left(y0[:, :256] - y0[:, 256:], w2_ref[...])
    y_ref[0, 0, :, 128:256] = d2[:, :128]
    y_ref[0, 1, :, 128:256] = d2[:, 128:]
    for out_ref, k in ((g0_ref, 0), (g1_ref, 1)):
        spec = dot3_right(a_ref[k], choose(y_ref.at[0], off_ref[k]))
        out_ref[0, 0] = spec[:A]
        out_ref[0, 1] = spec[A:]


def own_kernel(off_ref, y_ref, a_ref, g0_ref, g1_ref):
    for out_ref, k in ((g0_ref, 0), (g1_ref, 1)):
        spec = dot3_right(a_ref[k], choose(y_ref.at[0], off_ref[k]))
        out_ref[0, 0] = spec[:A]
        out_ref[0, 1] = spec[A:]


def whole(shape):
    return pl.BlockSpec(shape, lambda *_: (0,) * len(shape))


def forward_given(planes, offs, fwd, mats, interpret=False):
    depth = planes.shape[0]
    spec_shape = jax.ShapeDtypeStruct((depth, 2, A, 512), F32)
    spec_block = pl.BlockSpec((1, 2, A, 512), lambda z, *_: (z, 0, 0, 0))
    return pl.pallas_call(
        given_kernel,
        out_shape=(jax.ShapeDtypeStruct((depth, 2, 256, 512), F32), spec_shape, spec_shape),
        grid_spec=pltpu.PrefetchScalarGridSpec(
            num_scalar_prefetch=1,
            grid=(depth,),
            in_specs=[
                pl.BlockSpec((1, 256, L), lambda z, *_: (z, 0, 0)),
                whole((768, 256)),
                whole((768, 256)),
                whole((1536, 512)),
                whole((2, 256, 768)),
            ],
            out_specs=[pl.BlockSpec((1, 2, 256, 512), lambda z, *_: (z, 0, 0, 0)), spec_block, spec_block],
        ),
        cost_estimate=pl.CostEstimate(flops=depth * 900_000_000, bytes_accessed=depth * 3_200_000, transcendentals=0),
        interpret=interpret,
        name="forward_given",
    )(offs, planes, *fwd, mats)


def forward_own(y, offs, mats, interpret=False):
    depth = y.shape[0]
    spec_shape = jax.ShapeDtypeStruct((depth, 2, A, 512), F32)
    spec_block = pl.BlockSpec((1, 2, A, 512), lambda z, *_: (z, 0, 0, 0))
    return pl.pallas_call(
        own_kernel,
        out_shape=(spec_shape, spec_shape),
        grid_spec=pltpu.PrefetchScalarGridSpec(
            num_scalar_prefetch=1,
            grid=(depth,),
            in_specs=[
                pl.BlockSpec((1, 2, 256, 512), lambda z, *_: (z, 0, 0, 0)),
                whole((2, 256, 768)),
            ],
            out_specs=[spec_block, spec_block],
        ),
        cost_estimate=pl.CostEstimate(flops=depth * 400_000_000, bytes_accessed=depth * 2_000_000, transcendentals=0),
        interpret=interpret,
        name="forward_own",
    )(offs, y, mats)


def times_i(x, sign):
    return (-sign * x[1], sign * x[0])


def cadd(x, y):
    return (x[0] + y[0], x[1] + y[1])


def csub(x, y):
    return (x[0] - y[0], x[1] - y[1])


def eighth(x, sign):
    return ((x[0] - sign * x[1]) * HALF, (x[1] + sign * x[0]) * HALF)


def dft4(x, sign):
    a = cadd(x[0], x[2])
    b = csub(x[0], x[2])
    c = cadd(x[1], x[3])
    d = times_i(csub(x[1], x[3]), sign)
    return [cadd(a, c), cadd(b, d), csub(a, c), csub(b, d)]


def dft8(x, sign):
    even = dft4([x[0], x[2], x[4], x[6]], sign)
    odd = dft4([x[1], x[3], x[5], x[7]], sign)
    odd = [odd[0], eighth(odd[1], sign), times_i(odd[2], sign), times_i(eighth(odd[3], sign), sign)]
    return [cadd(even[k], odd[k]) for k in range(4)] + [csub(even[k], odd[k]) for k in range(4)]


def normalized(p, q):
    real = p[0] * q[0] + p[1] * q[1]
    imag = p[1] * q[0] - p[0] * q[1]
    scale = lax.rsqrt(jnp.maximum(real * real + imag * imag, FLOOR * FLOOR))
    return (real * scale, imag * scale)


def to_lanes(ref, part):
    lane = lax.broadcasted_iota(jnp.int32, (A, 128), 1)
    out = jnp.zeros((A, 128), F32)
    for z in range(Z):
        block = ref(z, part)
        if z:
            block = pltpu.roll(block, z, 1)
        out = jnp.where(lane == z, block, out)
    return out


def pair_kernel(pieces, *refs):
    own_refs = refs[:pieces]
    far_refs = refs[pieces : 2 * pieces]
    ab_ref, v0_ref, v2_ref, v1_ref, ef_ref, er_ref, flip_ref = refs[2 * pieces : 2 * pieces + 7]
    surf_ref, peak_ref, r_ref, qh_ref, ql_ref = refs[-5:]
    step = pl.program_id(0)

    def get(group, z, part, rows):
        return group[z % pieces][z // pieces, part, rows, :]

    def chunk(i, _):
        rows = pl.ds(pl.multiple_of(i * 8, 8), 8)
        own = dft8([(get(own_refs, z, 0, rows), get(own_refs, z, 1, rows)) for z in range(Z)], -1.0)
        far = dft8([(get(far_refs, z, 0, rows), get(far_refs, z, 1, rows)) for z in range(Z)], -1.0)
        back = dft8([normalized(own[u], far[u]) for u in range(Z)], 1.0)
        for z in range(Z):
            r_ref[rows, z * 128 : (z + 1) * 128] = back[z][0]
            r_ref[pl.ds(pl.multiple_of(i * 8 + A, 8), 8), z * 128 : (z + 1) * 128] = back[z][1]
        return 0

    lax.fori_loop(0, A // 8, chunk, 0)

    @pl.when(step == 0)
    def _():
        high = lax.Precision.HIGHEST
        every = slice(None)

        def edge(group):
            packed = jnp.concatenate(
                [to_lanes(lambda z, part: get(group, z, part, every), part) for part in range(2)], axis=1
            )
            here = jnp.dot(packed, ef_ref[...], precision=high, preferred_element_type=F32)
            turned = jnp.dot(packed, er_ref[...], precision=high, preferred_element_type=F32)
            there = jnp.dot(flip_ref[...], turned, precision=high, preferred_element_type=F32)
            hr, hi = here[:, :128], here[:, 128:]
            tr, ti = there[:, :128], there[:, 128:]
            return ((hr + tr) * 0.5, (hi - ti) * 0.5), ((hi + ti) * 0.5, (tr - hr) * 0.5)

        own_zero, own_last = edge(own_refs)
        far_zero, far_last = edge(far_refs)
        zero = normalized(own_zero, far_zero)
        last = normalized(own_last, far_last)
        both = jnp.concatenate((zero[0] - last[1], zero[1] + last[0]), axis=1)
        field = jnp.dot(both, er_ref[...], precision=high, preferred_element_type=F32)
        lane = lax.broadcasted_iota(jnp.int32, (A, 128), 1)
        for part in range(2):
            source = field[:, part * 128 : (part + 1) * 128]
            for z in range(Z):
                moved = pltpu.roll(source, 128 - z, 1) if z else source
                place = (slice(part * A, (part + 1) * A), slice(z * 128, (z + 1) * 128))
                r_ref[place] = jnp.where(lane == 0, moved, r_ref[place])

    for half in range(2):
        q = dot3_right(ab_ref[...], r_ref[:, half * 512 : (half + 1) * 512])
        hi, lo = split(q)
        for k in range(4):
            z = half * 4 + k
            for part in range(2):
                rows = slice(part * A, (part + 1) * A)
                qh_ref[step, z, :, part * 128 : (part + 1) * 128] = hi[rows, k * 128 : (k + 1) * 128]
                ql_ref[step, z, :, part * 128 : (part + 1) * 128] = lo[rows, k * 128 : (k + 1) * 128]

    @pl.when(step == 3)
    def _():
        def planes(i, _):
            two = pl.ds(i * 2, 2)

            def take(b):
                return qh_ref[b, two].reshape(2 * A, 256), ql_ref[b, two].reshape(2 * A, 256)

            h0, l0 = take(0)
            y00 = jnp.dot(jnp.concatenate((h0, l0, h0), axis=1), v0_ref[...], preferred_element_type=F32)
            h2, l2 = take(1)
            y01 = jnp.dot(jnp.concatenate((h2, l2, h2), axis=1), v2_ref[...], preferred_element_type=F32)
            h1, l1 = take(2)
            h3, l3 = take(3)
            y1 = jnp.dot(
                jnp.concatenate((h1, h3, l1, l3, h1, h3), axis=1), v1_ref[...], preferred_element_type=F32
            )
            y0 = jnp.concatenate((y00 + y01, y00 - y01), axis=1)
            top = jnp.concatenate((y0 + y1, y0 - y1), axis=1)
            top = jnp.maximum(top[:A], top[A:])

            @pl.when(i == 0)
            def _():
                surf_ref[0] = top

            @pl.when(i > 0)
            def _():
                surf_ref[0] = jnp.maximum(surf_ref[0], top)

            return 0

        lax.fori_loop(0, Z // 2, planes, 0)
        peak_ref[0] = jnp.broadcast_to(jnp.max(surf_ref[0]), (8, 128))


def pair(rnd, own, far, ab, back, edges, before, interpret=False):
    pieces = len(own)
    depth = Z // pieces
    block = pl.BlockSpec((depth, 2, A, 128), lambda w: (0, 0, 0, w))
    args = list(own) + list(far) + [ab, *back, *edges]
    in_specs = [block] * (2 * pieces) + [
        whole((256, 768)),
        whole((768, 256)),
        whole((768, 256)),
        whole((1536, 512)),
        whole((256, 256)),
        whole((256, 256)),
        whole((128, 128)),
    ]
    aliases = {}
    if before is not None:
        aliases = {len(args): 0, len(args) + 1: 1}
        args += list(before)
        in_specs += [pl.BlockSpec(memory_space=pl.ANY)] * 2
    return pl.pallas_call(
        functools.partial(pair_kernel, pieces),
        out_shape=(
            jax.ShapeDtypeStruct((ROUNDS, A, L), F32),
            jax.ShapeDtypeStruct((ROUNDS, 8, 128), F32),
        ),
        grid=(4,),
        in_specs=in_specs,
        out_specs=(
            pl.BlockSpec((1, A, L), lambda w: (rnd, 0, 0)),
            pl.BlockSpec((1, 8, 128), lambda w: (rnd, 0, 0)),
        ),
        scratch_shapes=[
            pltpu.VMEM((2 * A, Z * 128), F32),
            pltpu.VMEM((4, Z, A, 256), BF),
            pltpu.VMEM((4, Z, A, 256), BF),
        ],
        input_output_aliases=aliases,
        cost_estimate=pl.CostEstimate(flops=5_000_000_000, bytes_accessed=12_000_000, transcendentals=500_000),
        interpret=interpret,
        name=f"pair_{rnd}",
    )(*args)


def shift(x, by, size, ok):
    pairs = [(i + by, i) for i in range(size) if ok(i)]
    return lax.ppermute(x, ("tile", "slab"), pairs)


def on_device(stored, offsets):
    size = lax.axis_size(("tile", "slab"))
    owned = lax.all_to_all(stored, "slab", split_axis=0, concat_axis=1, tiled=True)[0]
    offs = offsets[:, :, 0]
    fwd = along_tables()
    back = back_tables()
    ab = across_back()
    edges = edge_tables()
    own_mats = jnp.stack([across_forward(offs[r, 0]) for r in range(ROUNDS)])
    given_mats = jnp.stack([across_forward(offs[r, 1]) for r in range(ROUNDS)])
    y, g0, g1 = forward_given(owned, offs[:, 1], fwd, given_mats)
    far0 = shift(g0, 1, size, lambda t: t % GC != GC - 1 and t + 1 < size)
    far1 = shift(g1, GC, size, lambda t: t + GC < size)
    own0, own1 = forward_own(y, offs[:, 0], own_mats)
    out = pair(0, [own0], [far0], ab, back, edges, None)
    surface, peak = pair(1, [own1], [far1], ab, back, edges, out)
    return surface[:, None], peak[:, 0, :1]


def solution(mesh):
    return jax.shard_map(
        on_device,
        mesh=mesh,
        in_specs=(P("tile", "slab", None, None), P(None, None, ("tile", "slab"))),
        out_specs=(P(None, ("tile", "slab"), None, None), P(None, ("tile", "slab"))),
        check_vma=False,
    )
```

```python
import functools
import math

import jax
import jax.numpy as jnp
from jax import lax
from jax.experimental import pallas as pl
from jax.experimental.pallas import tpu as pltpu
from jax.sharding import PartitionSpec as P

GC = 7
ROUNDS = 2
A = 128
L = 1024
Z = 8
FLOOR = 0.25
BF = jnp.bfloat16
F32 = jnp.float32
HALF = math.sqrt(0.5)


def split(x):
    hi = x.astype(BF)
    lo = (x - hi.astype(F32)).astype(BF)
    return hi, lo


def split_table(x):
    hi = lax.reduce_precision(x, exponent_bits=8, mantissa_bits=7)
    return hi.astype(BF), (x - hi).astype(BF)


def three_rows(x):
    hi, lo = split_table(x)
    return jnp.concatenate((hi, hi, lo), axis=0)


def three_cols(x):
    hi, lo = split_table(x)
    return jnp.concatenate((hi, hi, lo), axis=1)


def trig(index, total):
    angle = (index % total).astype(F32) * (2.0 * math.pi / total)
    return jnp.cos(angle), jnp.sin(angle)


def iota(length):
    return lax.optimization_barrier(jnp.arange(length, dtype=jnp.int32))


def odd_tables():
    rows = iota(512)[:, None]
    m = iota(256)[None, :]
    c, s = trig(rows * (2 * m + 1), L)
    scale = 1.0 / L
    return three_rows(
        scale * jnp.concatenate((c[:, :128], -s[:, :128], c[:, 128:], -s[:, 128:]), axis=1)
    )


def even_tables():
    n = iota(256)[:, None]
    m = iota(A)[None, :]
    c0, s0 = trig(n * (4 * m), L)
    c2, s2 = trig(n * (4 * m + 2), L)
    last = (1 - 2 * (n % 2)).astype(F32)
    im0 = jnp.where(m == 0, last, -s0)
    scale = 1.0 / L
    return (
        three_rows(scale * jnp.concatenate((c0, im0), axis=1)),
        three_rows(scale * jnp.concatenate((c2, -s2), axis=1)),
    )


def odd_back():
    cols = iota(512)[None, :]
    m = iota(256)[:, None]
    c, s = trig(cols * (2 * m + 1), L)
    scale = 2.0 / L
    return jnp.stack(
        [three_rows(scale * jnp.concatenate((c[b : b + A], -s[b : b + A]), axis=0)) for b in (0, A)]
    )


def even_back():
    cols = iota(256)[None, :]
    m = iota(A)[:, None]
    c0, s0 = trig(cols * (4 * m), L)
    c2, s2 = trig(cols * (4 * m + 2), L)
    last = (1 - 2 * (cols % 2)).astype(F32)
    scale = 2.0 / L
    re0 = jnp.where(m == 0, 0.5 * scale, scale * c0)
    im0 = jnp.where(m == 0, 0.5 * scale * last, -scale * s0)
    return jnp.stack(
        (
            three_rows(jnp.concatenate((re0, im0), axis=0)),
            three_rows(scale * jnp.concatenate((c2, -s2), axis=0)),
        )
    )


def across_forward(offset):
    v = iota(A)[:, None]
    r = iota(A)[None, :]
    c, s = trig((r - offset + A) * v, A)
    top = jnp.concatenate((c, s), axis=1)
    low = jnp.concatenate((-s, c), axis=1)
    return three_cols(jnp.concatenate((top, low), axis=0))


def across_back():
    v = iota(A)[None, :]
    a = iota(A)[:, None]
    c, s = trig(a * v, A)
    top = jnp.concatenate((c, -s), axis=1)
    low = jnp.concatenate((s, c), axis=1)
    return three_cols(jnp.concatenate((top, low), axis=0))


def edge_tables():
    lane = iota(A)
    i = lane[:, None]
    j = lane[None, :]
    inside = jnp.logical_and(i < Z, j < Z)
    c, s = trig(i * j, Z)
    c = jnp.where(inside, c, 0.0)
    s = jnp.where(inside, s, 0.0)
    fwd = jnp.concatenate(
        (jnp.concatenate((c, -s), axis=1), jnp.concatenate((s, c), axis=1)), axis=0
    )
    rev = jnp.concatenate(
        (jnp.concatenate((c, s), axis=1), jnp.concatenate((-s, c), axis=1)), axis=0
    )
    flip = ((i + j) % A == 0).astype(F32)
    return fwd, rev, flip


def dot3_left(x, table):
    hi, lo = split(x)
    return jnp.dot(jnp.concatenate((hi, lo, hi), axis=1), table, preferred_element_type=F32)


def dot3_right(table, x):
    hi, lo = split(x)
    return jnp.dot(table, jnp.concatenate((hi, lo, hi), axis=0), preferred_element_type=F32)


def whole(shape):
    return pl.BlockSpec(shape, lambda *_: (0,) * len(shape))


def times_i(x, sign):
    return (-sign * x[1], sign * x[0])


def cadd(x, y):
    return (x[0] + y[0], x[1] + y[1])


def csub(x, y):
    return (x[0] - y[0], x[1] - y[1])


def eighth(x, sign):
    return ((x[0] - sign * x[1]) * HALF, (x[1] + sign * x[0]) * HALF)


def dft4(x, sign):
    a = cadd(x[0], x[2])
    b = csub(x[0], x[2])
    c = cadd(x[1], x[3])
    d = times_i(csub(x[1], x[3]), sign)
    return [cadd(a, c), cadd(b, d), csub(a, c), csub(b, d)]


def dft8(x, sign):
    even = dft4([x[0], x[2], x[4], x[6]], sign)
    odd = dft4([x[1], x[3], x[5], x[7]], sign)
    odd = [odd[0], eighth(odd[1], sign), times_i(odd[2], sign), times_i(eighth(odd[3], sign), sign)]
    return [cadd(even[k], odd[k]) for k in range(4)] + [csub(even[k], odd[k]) for k in range(4)]


def odd_kernel(order_ref, x_ref, w_ref, out_ref):
    x = x_ref[0].reshape(512, L)
    out_ref[0] = dot3_left(x[:, :512] - x[:, 512:], w_ref[...]).reshape(2, 256, 512)


def even_kernel(order_ref, x_ref, w0_ref, w2_ref, out_ref):
    x = x_ref[0].reshape(512, L)
    y = x[:, :512] + x[:, 512:]
    out_ref[0, :, :, :256] = dot3_left(y[:, :256] + y[:, 256:], w0_ref[...]).reshape(2, 256, 256)
    out_ref[0, :, :, 256:] = dot3_left(y[:, :256] - y[:, 256:], w2_ref[...]).reshape(2, 256, 256)


def along(kernel, name, stored, order, tables, interpret=False):
    tiles, planes = stored.shape[:2]
    return pl.pallas_call(
        kernel,
        out_shape=jax.ShapeDtypeStruct((tiles, planes, 256, 512), F32),
        grid_spec=pltpu.PrefetchScalarGridSpec(
            num_scalar_prefetch=1,
            grid=(tiles,),
            in_specs=[pl.BlockSpec((1, planes, 256, L), lambda i, order: (order[i], 0, 0, 0))]
            + [whole(t.shape) for t in tables],
            out_specs=pl.BlockSpec((1, planes, 256, 512), lambda i, order: (i, 0, 0, 0)),
        ),
        cost_estimate=pl.CostEstimate(flops=3_200_000_000, bytes_accessed=14_000_000, transcendentals=0),
        interpret=interpret,
        name=name,
    )(order, stored, *tables)


def across(y_ref, first, count, offset, table):
    later = lax.broadcasted_iota(jnp.int32, (A, 256), 0) >= offset
    picked = [jnp.where(later, y_ref[first + k, :A, :], y_ref[first + k, A:, :]) for k in range(count)]
    real = jnp.concatenate([p[:, :128] for p in picked], axis=1)
    imag = jnp.concatenate([p[:, 128:] for p in picked], axis=1)
    return dot3_right(table, jnp.concatenate((real, imag), axis=0))


def send_kernel(off_ref, y_ref, a_ref, g0_ref, g1_ref):
    for out_ref, k in ((g0_ref, 0), (g1_ref, 1)):
        out_ref[0] = across(y_ref, 0, 4, off_ref[k], a_ref[k])


def spectra(y, offs, mats, interpret=False):
    shape = jax.ShapeDtypeStruct((2, 256, Z * 128), F32)
    block = pl.BlockSpec((1, 256, 512), lambda w, h, *_: (w, 0, h))
    return pl.pallas_call(
        send_kernel,
        out_shape=(shape, shape),
        grid_spec=pltpu.PrefetchScalarGridSpec(
            num_scalar_prefetch=1,
            grid=(2, 2),
            in_specs=[pl.BlockSpec((4, 256, 256), lambda w, h, *_: (h, 0, w)), whole((2, 256, 768))],
            out_specs=(block, block),
        ),
        cost_estimate=pl.CostEstimate(flops=1_600_000_000, bytes_accessed=8_000_000, transcendentals=0),
        interpret=interpret,
        name="spectra",
    )(offs, y, mats)


def normalized(p, q, sign):
    real = p[0] * q[0] + p[1] * q[1]
    imag = p[1] * q[0] - p[0] * q[1]
    scale = lax.rsqrt(jnp.maximum(real * real + imag * imag, FLOOR * FLOOR))
    return (real * scale, imag * (scale * sign))


def to_lanes(ref, part):
    lane = lax.broadcasted_iota(jnp.int32, (A, 128), 1)
    out = jnp.zeros((A, 128), F32)
    for z in range(Z):
        block = ref[part * A : (part + 1) * A, z * 128 : (z + 1) * 128]
        if z:
            block = pltpu.roll(block, z, 1)
        out = jnp.where(lane == z, block, out)
    return out


def edge_fix(own_ref, far_ref, r_ref, ef_ref, er_ref, flip_ref, sign):
    high = lax.Precision.HIGHEST

    def edge(ref):
        packed = jnp.concatenate([to_lanes(ref, part) for part in range(2)], axis=1)
        here = jnp.dot(packed, ef_ref[...], precision=high, preferred_element_type=F32)
        turned = jnp.dot(packed, er_ref[...], precision=high, preferred_element_type=F32)
        there = jnp.dot(flip_ref[...], turned, precision=high, preferred_element_type=F32)
        hr, hi = here[:, :128], here[:, 128:]
        tr, ti = there[:, :128], there[:, 128:]
        return ((hr + tr) * 0.5, (hi - ti) * 0.5), ((hi + ti) * 0.5, (tr - hr) * 0.5)

    own_zero, own_last = edge(own_ref)
    far_zero, far_last = edge(far_ref)
    zero = normalized(own_zero, far_zero, sign)
    last = normalized(own_last, far_last, sign)
    both = jnp.concatenate((zero[0] - last[1], zero[1] + last[0]), axis=1)
    field = jnp.dot(both, er_ref[...], precision=high, preferred_element_type=F32)
    lane = lax.broadcasted_iota(jnp.int32, (A, 128), 1)
    for part in range(2):
        source = field[:, part * 128 : (part + 1) * 128]
        for z in range(Z):
            moved = pltpu.roll(source, 128 - z, 1) if z else source
            place = (slice(part * A, (part + 1) * A), slice(z * 128, (z + 1) * 128))
            r_ref[place] = jnp.where(lane == 0, moved, r_ref[place])


def pair_kernel(even, ints_ref, y_ref, far_ref, a_ref, ab_ref, v_ref, *refs):
    if even:
        ef_ref, er_ref, flip_ref, odd_ref, out_ref, own_ref, r_ref, acc_ref = refs
    else:
        out_ref, own_ref, r_ref = refs
    step = pl.program_id(0)
    sign = ints_ref[1].astype(F32)
    for half in range(2):
        own_ref[:, half * 512 : (half + 1) * 512] = across(y_ref, half * 4, 4, ints_ref[0], a_ref[...])

    def chunk(i, _):
        up = pl.ds(pl.multiple_of(i * 8, 8), 8)
        down = pl.ds(pl.multiple_of(i * 8 + A, 8), 8)

        def load(ref):
            return [(ref[up, z * 128 : (z + 1) * 128], ref[down, z * 128 : (z + 1) * 128]) for z in range(Z)]

        own = dft8(load(own_ref), -1.0)
        far = dft8(load(far_ref.at[0]), -1.0)
        back = dft8([normalized(own[u], far[u], sign) for u in range(Z)], 1.0)
        for z in range(Z):
            r_ref[up, z * 128 : (z + 1) * 128] = back[z][0]
            r_ref[down, z * 128 : (z + 1) * 128] = back[z][1]
        return 0

    lax.fori_loop(0, A // 8, chunk, 0)

    if even:
        @pl.when(step == 0)
        def _():
            edge_fix(own_ref, far_ref.at[0], r_ref, ef_ref, er_ref, flip_ref, sign)

    def parts():
        for half in range(2):
            q = dot3_right(ab_ref[...], r_ref[:, half * 512 : (half + 1) * 512])
            for k in range(0, 4, 2):
                rows = [
                    jnp.concatenate((q[:A, j * 128 : (j + 1) * 128], q[A:, j * 128 : (j + 1) * 128]), axis=1)
                    for j in (k, k + 1)
                ]
                yield half * 4 + k, dot3_left(jnp.concatenate(rows, axis=0), v_ref[0])

    @pl.when(step == 0)
    def _():
        target = acc_ref if even else out_ref
        for z, part in parts():
            target[z : z + 2] = part.reshape(2, A, -1)

    @pl.when(step == 1)
    def _():
        top = None
        for z, part in parts():
            if not even:
                out_ref[z : z + 2] += part.reshape(2, A, -1)
                continue
            first = acc_ref[z : z + 2].reshape(2 * A, 256)
            odd = odd_ref[z : z + 2].reshape(2 * A, 512)
            y = jnp.concatenate((first + part, first - part), axis=1)
            x = jnp.concatenate((y + odd, y - odd), axis=1)
            x = jnp.maximum(x[:A], x[A:])
            if z == 0:
                out_ref[...] = x
            else:
                out_ref[...] = jnp.maximum(out_ref[...], x)


def pair(rnd, even, ints, y, far, mat, ab, back, edges, odd, interpret=False):
    args = [y, far, mat, ab, back]
    in_specs = [
        pl.BlockSpec((Z, 256, 256), lambda w, *_: (0, 0, w)),
        pl.BlockSpec((1, 256, Z * 128), lambda w, *_: (w, 0, 0)),
        whole((256, 768)),
        whole((256, 768)),
        pl.BlockSpec((1, 768, back.shape[2]), lambda w, *_: (w, 0, 0)),
    ]
    scratch = [pltpu.VMEM((256, Z * 128), F32)] * 2
    out_shape = (Z, A, 512)
    if even:
        args += [*edges, odd]
        in_specs += [whole((256, 256)), whole((256, 256)), whole((128, 128)), whole((Z, A, 512))]
        scratch += [pltpu.VMEM((Z, A, 256), F32)]
        out_shape = (A, L)
    return pl.pallas_call(
        functools.partial(pair_kernel, even),
        out_shape=jax.ShapeDtypeStruct(out_shape, F32),
        grid_spec=pltpu.PrefetchScalarGridSpec(
            num_scalar_prefetch=1,
            grid=(2,),
            in_specs=in_specs,
            out_specs=whole(out_shape),
            scratch_shapes=scratch,
        ),
        cost_estimate=pl.CostEstimate(flops=3_000_000_000, bytes_accessed=10_000_000, transcendentals=500_000),
        interpret=interpret,
        name=("even" if even else "odd") + f"_{rnd}",
    )(ints, *args)


SLAB_OF = [t % 4 for t in range(128)]
TURN_ROW = [False] * 19
TURN_COLUMN = [False] * 7
MOVED = False


def moved(x, pairs):
    return lax.ppermute(x, ("tile", "slab"), pairs)


def lookup(table, place):
    return jnp.asarray(table, dtype=jnp.int32)[place]


def plan(size, slabs):
    home = list(range(size))
    at = [slabs * (t // slabs) + SLAB_OF[t] for t in home]
    holds = [0] * size
    for t in home:
        holds[at[t]] = t
    order = [holds[p] % slabs for p in home]
    turned = [[TURN_ROW[t // GC] for t in home], [TURN_COLUMN[t % GC] for t in home]]
    travel, result = [], []
    for rnd, step in enumerate((1, GC)):
        go, out = [], []
        for t in home:
            if t + step >= size or (rnd == 0 and t % GC == GC - 1):
                continue
            near, far = at[t], at[t + step]
            go.append((near, far) if turned[rnd][t] else (far, near))
            out.append((far if turned[rnd][t] else near, t))
        travel.append(go)
        result.append(out)
    return at, holds, order, turned, travel, result


def on_device(stored, offsets):
    size = lax.axis_size(("tile", "slab"))
    slabs = lax.axis_size("slab")
    place = lax.axis_index(("tile", "slab"))
    at, holds, order, turned, travel, result = plan(size, slabs)
    group = place // slabs
    sequence = jnp.asarray(order, dtype=jnp.int32).reshape(-1, slabs)[group]
    tile = lookup(holds, place)

    def gather(x):
        y = lax.all_to_all(x, "slab", split_axis=0, concat_axis=1, tiled=True)
        return y.reshape(Z, 256, 512)

    odd_src = along(odd_kernel, "along_odd", stored, sequence, (odd_tables(),))
    odd_all = gather(odd_src)
    offs = moved(offsets[:, :, 0], [(t, at[t]) for t in range(size)]) if MOVED else offsets[:, :, 0]
    turn = [lookup([int(f) for f in turned[r]], tile) for r in range(ROUNDS)]
    keep = [jnp.where(turn[r] == 1, offs[r, 1], offs[r, 0]) for r in range(ROUNDS)]
    send = [jnp.where(turn[r] == 1, offs[r, 0], offs[r, 1]) for r in range(ROUNDS)]
    ints = [jnp.stack((keep[r], 1 - 2 * turn[r])) for r in range(ROUNDS)]
    sends = jnp.stack(send)
    send_mats = jnp.stack([across_forward(o) for o in send])
    even_src = along(even_kernel, "along_even", stored, sequence, even_tables())
    odd_all, even_src, sends, send_mats = lax.optimization_barrier((odd_all, even_src, sends, send_mats))
    even_all = gather(even_src)
    odd_sent = spectra(odd_all, sends, send_mats)
    odd_far = [moved(odd_sent[r], travel[r]) for r in range(ROUNDS)]
    keep_mats = [across_forward(o) for o in keep]
    ab = across_back()
    edges = edge_tables()
    back_odd = odd_back()
    back_even = even_back()
    even_sent = spectra(even_all, sends, send_mats)
    even_sent, ints = lax.optimization_barrier((even_sent, ints))
    even_far = [moved(even_sent[r], travel[r]) for r in range(ROUNDS)]
    odd = [
        pair(r, False, ints[r], odd_all, odd_far[r], keep_mats[r], ab, back_odd, None, None)
        for r in range(ROUNDS)
    ]
    surfaces = []
    for r in range(ROUNDS):
        top = pair(r, True, ints[r], even_all, even_far[r], keep_mats[r], ab, back_even, edges, odd[r])
        surfaces.append(moved(top, result[r]) if MOVED else top)
    surface = jnp.stack(surfaces)[:, None]
    peak = jnp.max(surface, axis=(2, 3))
    return surface, peak


def solution(mesh):
    return jax.shard_map(
        on_device,
        mesh=mesh,
        in_specs=(P("tile", "slab", None, None), P(None, None, ("tile", "slab"))),
        out_specs=(P(None, ("tile", "slab"), None, None), P(None, ("tile", "slab"))),
        check_vma=False,
    )
```

```python
import functools
import math

import jax
import jax.numpy as jnp
from jax import lax
from jax.experimental import pallas as pl
from jax.experimental.pallas import tpu as pltpu
from jax.sharding import PartitionSpec as P

GC = 7
ROUNDS = 2
A = 128
L = 1024
Z = 8
FLOOR = 0.25
BF = jnp.bfloat16
F32 = jnp.float32
HALF = math.sqrt(0.5)


def split(x):
    hi = x.astype(BF)
    lo = (x - hi.astype(F32)).astype(BF)
    return hi, lo


def split_table(x):
    hi = lax.reduce_precision(x, exponent_bits=8, mantissa_bits=7)
    return hi.astype(BF), (x - hi).astype(BF)


def three_rows(x):
    hi, lo = split_table(x)
    return jnp.concatenate((hi, hi, lo), axis=0)


def three_cols(x):
    hi, lo = split_table(x)
    return jnp.concatenate((hi, hi, lo), axis=1)


def trig(index, total):
    angle = (index % total).astype(F32) * (2.0 * math.pi / total)
    return jnp.cos(angle), jnp.sin(angle)


def iota(length):
    return lax.optimization_barrier(jnp.arange(length, dtype=jnp.int32))


def odd_tables():
    rows = iota(512)[:, None]
    m = iota(256)[None, :]
    c, s = trig(rows * (2 * m + 1), L)
    scale = 1.0 / L
    return three_rows(
        scale * jnp.concatenate((c[:, :128], -s[:, :128], c[:, 128:], -s[:, 128:]), axis=1)
    )


def even_tables():
    n = iota(256)[:, None]
    m = iota(A)[None, :]
    c0, s0 = trig(n * (4 * m), L)
    c2, s2 = trig(n * (4 * m + 2), L)
    last = (1 - 2 * (n % 2)).astype(F32)
    im0 = jnp.where(m == 0, last, -s0)
    scale = 1.0 / L
    return (
        three_rows(scale * jnp.concatenate((c0, im0), axis=1)),
        three_rows(scale * jnp.concatenate((c2, -s2), axis=1)),
    )


def odd_back():
    cols = iota(512)[None, :]
    m = iota(256)[:, None]
    c, s = trig(cols * (2 * m + 1), L)
    scale = 2.0 / L
    return jnp.stack(
        [three_rows(scale * jnp.concatenate((c[b : b + A], -s[b : b + A]), axis=0)) for b in (0, A)]
    )


def even_back():
    cols = iota(256)[None, :]
    m = iota(A)[:, None]
    c0, s0 = trig(cols * (4 * m), L)
    c2, s2 = trig(cols * (4 * m + 2), L)
    last = (1 - 2 * (cols % 2)).astype(F32)
    scale = 2.0 / L
    re0 = jnp.where(m == 0, 0.5 * scale, scale * c0)
    im0 = jnp.where(m == 0, 0.5 * scale * last, -scale * s0)
    return jnp.stack(
        (
            three_rows(jnp.concatenate((re0, im0), axis=0)),
            three_rows(scale * jnp.concatenate((c2, -s2), axis=0)),
        )
    )


def across_forward(offset):
    v = iota(A)[:, None]
    r = iota(A)[None, :]
    c, s = trig((r - offset + A) * v, A)
    top = jnp.concatenate((c, s), axis=1)
    low = jnp.concatenate((-s, c), axis=1)
    return three_cols(jnp.concatenate((top, low), axis=0))


def across_back():
    v = iota(A)[None, :]
    a = iota(A)[:, None]
    c, s = trig(a * v, A)
    top = jnp.concatenate((c, -s), axis=1)
    low = jnp.concatenate((s, c), axis=1)
    return three_cols(jnp.concatenate((top, low), axis=0))


def edge_tables():
    lane = iota(A)
    i = lane[:, None]
    j = lane[None, :]
    inside = jnp.logical_and(i < Z, j < Z)
    c, s = trig(i * j, Z)
    c = jnp.where(inside, c, 0.0)
    s = jnp.where(inside, s, 0.0)
    fwd = jnp.concatenate(
        (jnp.concatenate((c, -s), axis=1), jnp.concatenate((s, c), axis=1)), axis=0
    )
    rev = jnp.concatenate(
        (jnp.concatenate((c, s), axis=1), jnp.concatenate((-s, c), axis=1)), axis=0
    )
    flip = ((i + j) % A == 0).astype(F32)
    return fwd, rev, flip


def dot3_left(x, table):
    hi, lo = split(x)
    return jnp.dot(jnp.concatenate((hi, lo, hi), axis=1), table, preferred_element_type=F32)


def dot3_right(table, x):
    hi, lo = split(x)
    return jnp.dot(table, jnp.concatenate((hi, lo, hi), axis=0), preferred_element_type=F32)


def whole(shape):
    return pl.BlockSpec(shape, lambda *_: (0,) * len(shape))


def times_i(x, sign):
    return (-sign * x[1], sign * x[0])


def cadd(x, y):
    return (x[0] + y[0], x[1] + y[1])


def csub(x, y):
    return (x[0] - y[0], x[1] - y[1])


def eighth(x, sign):
    return ((x[0] - sign * x[1]) * HALF, (x[1] + sign * x[0]) * HALF)


def dft4(x, sign):
    a = cadd(x[0], x[2])
    b = csub(x[0], x[2])
    c = cadd(x[1], x[3])
    d = times_i(csub(x[1], x[3]), sign)
    return [cadd(a, c), cadd(b, d), csub(a, c), csub(b, d)]


def dft8(x, sign):
    even = dft4([x[0], x[2], x[4], x[6]], sign)
    odd = dft4([x[1], x[3], x[5], x[7]], sign)
    odd = [odd[0], eighth(odd[1], sign), times_i(odd[2], sign), times_i(eighth(odd[3], sign), sign)]
    return [cadd(even[k], odd[k]) for k in range(4)] + [csub(even[k], odd[k]) for k in range(4)]


def odd_kernel(x_ref, w_ref, out_ref):
    x = x_ref[0].reshape(512, L)
    out_ref[0] = dot3_left(x[:, :512] - x[:, 512:], w_ref[...]).reshape(2, 256, 512)


def even_kernel(x_ref, w0_ref, w2_ref, out_ref):
    x = x_ref[0].reshape(512, L)
    y = x[:, :512] + x[:, 512:]
    out_ref[0, :, :, :256] = dot3_left(y[:, :256] + y[:, 256:], w0_ref[...]).reshape(2, 256, 256)
    out_ref[0, :, :, 256:] = dot3_left(y[:, :256] - y[:, 256:], w2_ref[...]).reshape(2, 256, 256)


def along(kernel, name, stored, tables, interpret=False):
    tiles, planes = stored.shape[:2]
    return pl.pallas_call(
        kernel,
        out_shape=jax.ShapeDtypeStruct((tiles, planes, 256, 512), F32),
        grid_spec=pl.GridSpec(
            grid=(tiles,),
            in_specs=[pl.BlockSpec((1, planes, 256, L), lambda i: (i, 0, 0, 0))]
            + [whole(t.shape) for t in tables],
            out_specs=pl.BlockSpec((1, planes, 256, 512), lambda i: (i, 0, 0, 0)),
        ),
        cost_estimate=pl.CostEstimate(flops=3_200_000_000, bytes_accessed=14_000_000, transcendentals=0),
        interpret=interpret,
        name=name,
    )(stored, *tables)


def across(y_ref, first, count, offset, table):
    later = lax.broadcasted_iota(jnp.int32, (A, 256), 0) >= offset
    picked = [jnp.where(later, y_ref[first + k, :A, :], y_ref[first + k, A:, :]) for k in range(count)]
    real = jnp.concatenate([p[:, :128] for p in picked], axis=1)
    imag = jnp.concatenate([p[:, 128:] for p in picked], axis=1)
    return dot3_right(table, jnp.concatenate((real, imag), axis=0))


def send_kernel(off_ref, x_ref, a_ref, out_ref):
    tile = pl.program_id(0)
    rnd = pl.program_id(1)
    later = lax.broadcasted_iota(jnp.int32, (A, 256), 0) >= off_ref[rnd, tile]
    picked = [
        jnp.where(later, x_ref[0, p, :A, cols], x_ref[0, p, A:, cols])
        for p in range(2)
        for cols in (slice(0, 256), slice(256, 512))
    ]
    real = jnp.concatenate([p[:, :128] for p in picked], axis=1)
    imag = jnp.concatenate([p[:, 128:] for p in picked], axis=1)
    spec = dot3_right(a_ref[0, 0], jnp.concatenate((real, imag), axis=0))
    for k in range(4):
        out_ref[0, 0, k // 2, k % 2] = spec[:, k * 128 : (k + 1) * 128]


def spectra(x, offs, mats, interpret=False):
    tiles = x.shape[0]
    return pl.pallas_call(
        send_kernel,
        out_shape=jax.ShapeDtypeStruct((tiles, ROUNDS, 2, 2, 256, 128), F32),
        grid_spec=pltpu.PrefetchScalarGridSpec(
            num_scalar_prefetch=1,
            grid=(tiles, ROUNDS),
            in_specs=[
                pl.BlockSpec((1, 2, 256, 512), lambda t, r, *_: (t, 0, 0, 0)),
                pl.BlockSpec((1, 1, 256, 768), lambda t, r, *_: (r, t, 0, 0)),
            ],
            out_specs=pl.BlockSpec(
                (1, 1, 2, 2, 256, 128),
                lambda t, r, *_: (lax.rem(t + 3 - 2 * r, tiles), r, 0, 0, 0, 0),
            ),
        ),
        cost_estimate=pl.CostEstimate(flops=1_600_000_000, bytes_accessed=12_000_000, transcendentals=0),
        interpret=interpret,
        name="spectra",
    )(offs, x, mats)


def normalized(p, q, sign):
    real = p[0] * q[0] + p[1] * q[1]
    imag = p[1] * q[0] - p[0] * q[1]
    scale = lax.rsqrt(jnp.maximum(real * real + imag * imag, FLOOR * FLOOR)) * sign
    return (real * scale, imag * scale)


def to_lanes(block_of, part):
    lane = lax.broadcasted_iota(jnp.int32, (A, 128), 1)
    out = jnp.zeros((A, 128), F32)
    for z in range(Z):
        block = block_of(z, slice(part * A, (part + 1) * A))
        if z:
            block = pltpu.roll(block, z, 1)
        out = jnp.where(lane == z, block, out)
    return out


def edge_fix(own_of, far_of, r_ref, ef_ref, er_ref, flip_ref, sign):
    high = lax.Precision.HIGHEST

    def edge(block_of):
        packed = jnp.concatenate([to_lanes(block_of, part) for part in range(2)], axis=1)
        here = jnp.dot(packed, ef_ref[...], precision=high, preferred_element_type=F32)
        turned = jnp.dot(packed, er_ref[...], precision=high, preferred_element_type=F32)
        there = jnp.dot(flip_ref[...], turned, precision=high, preferred_element_type=F32)
        hr, hi = here[:, :128], here[:, 128:]
        tr, ti = there[:, :128], there[:, 128:]
        return ((hr + tr) * 0.5, (hi - ti) * 0.5), ((hi + ti) * 0.5, (tr - hr) * 0.5)

    own_zero, own_last = edge(own_of)
    far_zero, far_last = edge(far_of)
    zero = normalized(own_zero, far_zero, sign)
    last = normalized(own_last, far_last, sign)
    both = jnp.concatenate((zero[0] - last[1], zero[1] + last[0]), axis=1)
    field = jnp.dot(both, er_ref[...], precision=high, preferred_element_type=F32)
    lane = lax.broadcasted_iota(jnp.int32, (A, 128), 1)
    for part in range(2):
        source = field[:, part * 128 : (part + 1) * 128]
        for z in range(Z):
            moved = pltpu.roll(source, 128 - z, 1) if z else source
            place = (slice(part * A, (part + 1) * A), slice(z * 128, (z + 1) * 128))
            r_ref[place] = jnp.where(lane == 0, moved, r_ref[place])


def pair_kernel(even, ints_ref, y_ref, far_ref, a_ref, ab_ref, v_ref, *refs):
    if even:
        ef_ref, er_ref, flip_ref, odd_ref, out_ref, own_ref, r_ref, acc_ref = refs
    else:
        out_ref, own_ref, r_ref = refs
    step = pl.program_id(0)
    sign = ints_ref[1].astype(F32)
    for half in range(2):
        own_ref[:, half * 512 : (half + 1) * 512] = across(y_ref, half * 4, 4, ints_ref[0], a_ref[...])

    def own_of(z, rows):
        return own_ref[rows, z * 128 : (z + 1) * 128]

    def far_of(z, rows):
        return far_ref[z // 2, 0, z % 2, 0, rows, :]

    def chunk(i, _):
        up = pl.ds(pl.multiple_of(i * 8, 8), 8)
        down = pl.ds(pl.multiple_of(i * 8 + A, 8), 8)

        own = dft8([(own_of(z, up), own_of(z, down)) for z in range(Z)], -1.0)
        far = dft8([(far_of(z, up), far_of(z, down)) for z in range(Z)], -1.0)
        back = dft8([normalized(own[u], far[u], sign) for u in range(Z)], 1.0)
        for z in range(Z):
            r_ref[up, z * 128 : (z + 1) * 128] = back[z][0]
            r_ref[down, z * 128 : (z + 1) * 128] = back[z][1]
        return 0

    lax.fori_loop(0, A // 8, chunk, 0)

    if even:
        @pl.when(step == 0)
        def _():
            edge_fix(own_of, far_of, r_ref, ef_ref, er_ref, flip_ref, sign)

    def parts():
        for half in range(2):
            q = dot3_right(ab_ref[...], r_ref[:, half * 512 : (half + 1) * 512])
            for k in range(0, 4, 2):
                rows = [
                    jnp.concatenate((q[:A, j * 128 : (j + 1) * 128], q[A:, j * 128 : (j + 1) * 128]), axis=1)
                    for j in (k, k + 1)
                ]
                yield half * 4 + k, dot3_left(jnp.concatenate(rows, axis=0), v_ref[0])

    @pl.when(step == 0)
    def _():
        target = acc_ref if even else out_ref
        for z, part in parts():
            target[z : z + 2] = part.reshape(2, A, -1)

    @pl.when(step == 1)
    def _():
        top = None
        for z, part in parts():
            if not even:
                out_ref[z : z + 2] += part.reshape(2, A, -1)
                continue
            first = acc_ref[z : z + 2].reshape(2 * A, 256)
            odd = odd_ref[z : z + 2].reshape(2 * A, 512)
            y = jnp.concatenate((first + part, first - part), axis=1)
            x = jnp.concatenate((y + odd, y - odd), axis=1)
            x = jnp.maximum(x[:A], x[A:])
            if z == 0:
                out_ref[...] = x
            else:
                out_ref[...] = jnp.maximum(out_ref[...], x)


def pair(rnd, even, ints, y, far, mat, ab, back, edges, odd, interpret=False):
    args = [y, far, mat, ab, back]
    in_specs = [
        pl.BlockSpec((Z, 256, 256), lambda w, *_: (0, 0, w)),
        pl.BlockSpec((4, 1, 2, 1, 256, 128), lambda w, *_: (0, rnd if far.shape[1] > 1 else 0, 0, w, 0, 0)),
        whole((256, 768)),
        whole((256, 768)),
        pl.BlockSpec((1, 768, back.shape[2]), lambda w, *_: (w, 0, 0)),
    ]
    scratch = [pltpu.VMEM((256, Z * 128), F32)] * 2
    out_shape = (Z, A, 512)
    if even:
        args += [*edges, odd]
        in_specs += [whole((256, 256)), whole((256, 256)), whole((128, 128)), whole((Z, A, 512))]
        scratch += [pltpu.VMEM((Z, A, 256), F32)]
        out_shape = (A, L)
    return pl.pallas_call(
        functools.partial(pair_kernel, even),
        out_shape=jax.ShapeDtypeStruct(out_shape, F32),
        grid_spec=pltpu.PrefetchScalarGridSpec(
            num_scalar_prefetch=1,
            grid=(2,),
            in_specs=in_specs,
            out_specs=whole(out_shape),
            scratch_shapes=scratch,
        ),
        cost_estimate=pl.CostEstimate(flops=3_000_000_000, bytes_accessed=10_000_000, transcendentals=500_000),
        interpret=interpret,
        name=("even" if even else "odd") + f"_{rnd}",
    )(ints, *args)


def from_next(x, step, groups):
    return lax.ppermute(x, "tile", [(g + step, g) for g in range(groups - step)])


def after(first, second):
    return lax.optimization_barrier((first, second))


def on_device(stored, offsets):
    size = lax.axis_size(("tile", "slab"))
    groups = lax.axis_size("tile")
    slabs = lax.axis_size("slab")
    place = lax.axis_index(("tile", "slab"))

    def gather(x):
        return lax.all_to_all(x, "slab", split_axis=0, concat_axis=1, tiled=True)[0]

    def collect(x):
        return lax.all_to_all(x, "slab", split_axis=0, concat_axis=0, tiled=True)

    odd_src = along(odd_kernel, "along_odd", stored, (odd_tables(),))
    odd_all = gather(odd_src)
    mine = offsets[:, 1, 0]
    turns = [mine] + [
        lax.ppermute(mine, "slab", [((i + k) % slabs, i) for i in range(slabs)]) for k in range(1, slabs)
    ]
    given = jnp.roll(jnp.stack(turns, axis=1), lax.axis_index("slab"), axis=1)
    mats = jnp.stack([jnp.stack([across_forward(given[r, j]) for j in range(slabs)]) for r in range(ROUNDS)])

    def shifted(src):
        made = spectra(src, given, mats)
        near = from_next(jnp.stack((made[3, 0], made[0, 1])), 1, groups)
        far = from_next(made[1:, 1], 2, groups)
        zero = [made[0, 0], made[1, 0], made[2, 0], near[0]]
        one = [near[1], far[0], far[1], far[2]]
        return zero, one

    odd_sent = jnp.stack([x for pair_of in zip(*shifted(odd_src)) for x in pair_of]).reshape(slabs, ROUNDS, 2, 2, 256, 128)
    even_src = along(even_kernel, "along_even", stored, even_tables())
    even_sent = [jnp.stack(x)[:, None] for x in shifted(even_src)]
    odd_all, even_src = after(odd_all, even_src)
    even_all = gather(even_src)
    valid = (
        jnp.logical_and(place % GC != GC - 1, place + 1 < size),
        place + GC < size,
    )
    own = [offsets[r, 0, 0] for r in range(ROUNDS)]
    ints = [jnp.stack((own[r], valid[r].astype(jnp.int32))) for r in range(ROUNDS)]
    own_mats = [across_forward(o) for o in own]
    ab = across_back()
    edges = edge_tables()
    back_odd = odd_back()
    back_even = even_back()
    even_all, odd_sent = after(even_all, odd_sent)
    odd_far = collect(odd_sent)
    odd_far, even_zero = after(odd_far, even_sent[0])
    zero_far = collect(even_zero)
    odd = [
        pair(r, False, ints[r], odd_all, odd_far, own_mats[r], ab, back_odd, None, None)
        for r in range(ROUNDS)
    ]
    zero_far, odd, even_one = lax.optimization_barrier((zero_far, odd, even_sent[1]))
    even_far = [zero_far, collect(even_one)]
    surfaces = [
        pair(r, True, ints[r], even_all, even_far[r], own_mats[r], ab, back_even, edges, odd[r])
        for r in range(ROUNDS)
    ]
    surface = jnp.stack(surfaces)[:, None]
    peak = jnp.max(surface, axis=(2, 3))
    return surface, peak


def solution(mesh):
    return jax.shard_map(
        on_device,
        mesh=mesh,
        in_specs=(P("tile", "slab", None, None), P(None, None, ("tile", "slab"))),
        out_specs=(P(None, ("tile", "slab"), None, None), P(None, ("tile", "slab"))),
        check_vma=False,
    )
```

```python
import functools
import math

import jax
import jax.numpy as jnp
from jax import lax
from jax.experimental import pallas as pl
from jax.experimental.pallas import tpu as pltpu
from jax.sharding import PartitionSpec as P


GC = 7
ROUNDS = 2
A = 128
L = 1024
Z = 8
FLOOR = 0.25
BF = jnp.bfloat16
F32 = jnp.float32
HALF = math.sqrt(0.5)


def split(x):
    hi = x.astype(BF)
    lo = (x - hi.astype(F32)).astype(BF)
    return hi, lo


def split_table(x):
    hi = lax.reduce_precision(x, exponent_bits=8, mantissa_bits=7)
    return hi.astype(BF), (x - hi).astype(BF)


def three_rows(x):
    hi, lo = split_table(x)
    return jnp.concatenate((hi, hi, lo), axis=0)


def three_cols(x):
    hi, lo = split_table(x)
    return jnp.concatenate((hi, hi, lo), axis=1)


def trig(index, total):
    angle = (index % total).astype(F32) * (2.0 * math.pi / total)
    return jnp.cos(angle), jnp.sin(angle)


def iota(length):
    return lax.optimization_barrier(jnp.arange(length, dtype=jnp.int32))


def odd_table():
    rows = iota(512)[:, None]
    m = iota(256)[None, :]
    c, s = trig(rows * (2 * m + 1), L)
    scale = 1.0 / L
    return three_rows(
        scale * jnp.concatenate((c[:, :128], -s[:, :128], c[:, 128:], -s[:, 128:]), axis=1)
    )


def fours_table():
    n = iota(256)[:, None]
    m = iota(A)[None, :]
    c, s = trig(n * (4 * m), L)
    last = (1 - 2 * (n % 2)).astype(F32)
    return three_rows((1.0 / L) * jnp.concatenate((c, jnp.where(m == 0, last, -s)), axis=1))


def twos_table():
    n = iota(256)[:, None]
    m = iota(A)[None, :]
    c, s = trig(n * (4 * m + 2), L)
    return three_rows((1.0 / L) * jnp.concatenate((c, -s), axis=1))


def odd_back():
    cols = iota(512)[None, :]
    m = iota(256)[:, None]
    c, s = trig(cols * (2 * m + 1), L)
    scale = 2.0 / L
    return jnp.stack(
        [three_rows(scale * jnp.concatenate((c[b : b + A], -s[b : b + A]), axis=0)) for b in (0, A)]
    )


def fours_back():
    cols = iota(256)[None, :]
    m = iota(A)[:, None]
    c, s = trig(cols * (4 * m), L)
    last = (1 - 2 * (cols % 2)).astype(F32)
    scale = 2.0 / L
    real = jnp.where(m == 0, 0.5 * scale, scale * c)
    imag = jnp.where(m == 0, 0.5 * scale * last, -scale * s)
    return three_rows(jnp.concatenate((real, imag), axis=0))


def twos_back():
    cols = iota(256)[None, :]
    m = iota(A)[:, None]
    c, s = trig(cols * (4 * m + 2), L)
    return three_rows((2.0 / L) * jnp.concatenate((c, -s), axis=0))


def across_base():
    v = iota(A)
    return trig(v[:, None] * v[None, :], A)


def across_forward(offset, base):
    c0, s0 = base
    cv, sv = trig(offset * iota(A)[:, None], A)
    c = c0 * cv + s0 * sv
    s = s0 * cv - c0 * sv
    top = jnp.concatenate((c, s), axis=1)
    low = jnp.concatenate((-s, c), axis=1)
    return three_cols(jnp.concatenate((top, low), axis=0))


def across_back():
    v = iota(A)[None, :]
    a = iota(A)[:, None]
    c, s = trig(a * v, A)
    top = jnp.concatenate((c, -s), axis=1)
    low = jnp.concatenate((s, c), axis=1)
    return three_cols(jnp.concatenate((top, low), axis=0))


def edge_tables():
    lane = iota(A)
    i = lane[:, None]
    j = lane[None, :]
    inside = jnp.logical_and(i < Z, j < Z)
    c, s = trig(i * j, Z)
    c = jnp.where(inside, c, 0.0)
    s = jnp.where(inside, s, 0.0)
    fwd = jnp.concatenate(
        (jnp.concatenate((c, -s), axis=1), jnp.concatenate((s, c), axis=1)), axis=0
    )
    rev = jnp.concatenate(
        (jnp.concatenate((c, s), axis=1), jnp.concatenate((-s, c), axis=1)), axis=0
    )
    flip = ((i + j) % A == 0).astype(F32)
    return fwd, rev, flip


def dot3_left(x, table):
    hi, lo = split(x)
    return jnp.dot(jnp.concatenate((hi, lo, hi), axis=1), table, preferred_element_type=F32)


def dot3_right(table, x):
    hi, lo = split(x)
    return jnp.dot(table, jnp.concatenate((hi, lo, hi), axis=0), preferred_element_type=F32)


def whole(shape):
    return pl.BlockSpec(shape, lambda *_: (0,) * len(shape))


def times_i(x, sign):
    return (-sign * x[1], sign * x[0])


def cadd(x, y):
    return (x[0] + y[0], x[1] + y[1])


def csub(x, y):
    return (x[0] - y[0], x[1] - y[1])


def eighth(x, sign):
    return ((x[0] - sign * x[1]) * HALF, (x[1] + sign * x[0]) * HALF)


def dft4(x, sign):
    a = cadd(x[0], x[2])
    b = csub(x[0], x[2])
    c = cadd(x[1], x[3])
    d = times_i(csub(x[1], x[3]), sign)
    return [cadd(a, c), cadd(b, d), csub(a, c), csub(b, d)]


def dft8(x, sign):
    even = dft4([x[0], x[2], x[4], x[6]], sign)
    odd = dft4([x[1], x[3], x[5], x[7]], sign)
    odd = [odd[0], eighth(odd[1], sign), times_i(odd[2], sign), times_i(eighth(odd[3], sign), sign)]
    return [cadd(even[k], odd[k]) for k in range(4)] + [csub(even[k], odd[k]) for k in range(4)]


def large_kernel(x_ref, w1_ref, w0_ref, out_ref):
    x = x_ref[0].reshape(512, L)
    out_ref[0, :, :, :512] = dot3_left(x[:, :512] - x[:, 512:], w1_ref[...]).reshape(2, 256, 512)
    y = x[:, :512] + x[:, 512:]
    out_ref[0, :, :, 512:] = dot3_left(y[:, :256] + y[:, 256:], w0_ref[...]).reshape(2, 256, 256)


def small_kernel(x_ref, w2_ref, out_ref):
    x = x_ref[0].reshape(512, L)
    y = x[:, :512] + x[:, 512:]
    out_ref[0] = dot3_left(y[:, :256] - y[:, 256:], w2_ref[...]).reshape(2, 256, 256)


def along(kernel, stored, tables, columns, interpret=False):
    tiles, planes = stored.shape[:2]
    return pl.pallas_call(
        kernel,
        out_shape=jax.ShapeDtypeStruct((tiles, planes, 256, columns), F32),
        grid_spec=pl.GridSpec(
            grid=(tiles,),
            in_specs=[pl.BlockSpec((1, planes, 256, L), lambda i: (i, 0, 0, 0))]
            + [whole(t.shape) for t in tables],
            out_specs=pl.BlockSpec((1, planes, 256, columns), lambda i: (i, 0, 0, 0)),
        ),
        cost_estimate=pl.CostEstimate(flops=6_000_000 * columns, bytes_accessed=14_000_000, transcendentals=0),
        interpret=interpret,
    )(stored, *tables)


def across(y_ref, first, count, offset, table):
    later = lax.broadcasted_iota(jnp.int32, (A, 256), 0) >= offset
    picked = [jnp.where(later, y_ref[first + k, :A, :], y_ref[first + k, A:, :]) for k in range(count)]
    real = jnp.concatenate([p[:, :128] for p in picked], axis=1)
    imag = jnp.concatenate([p[:, 128:] for p in picked], axis=1)
    return dot3_right(table, jnp.concatenate((real, imag), axis=0))


def send_kernel(blocks, off_ref, x_ref, a_ref, out_ref):
    tile = pl.program_id(0)
    rnd = pl.program_id(1)
    later = lax.broadcasted_iota(jnp.int32, (A, 256), 0) >= off_ref[rnd, tile]
    picked = [
        jnp.where(later, x_ref[0, p, :A, w * 256 : (w + 1) * 256], x_ref[0, p, A:, w * 256 : (w + 1) * 256])
        for p in range(2)
        for w in range(blocks)
    ]
    real = jnp.concatenate([p[:, :128] for p in picked], axis=1)
    imag = jnp.concatenate([p[:, 128:] for p in picked], axis=1)
    spec = dot3_right(a_ref[0, 0], jnp.concatenate((real, imag), axis=0))
    for k in range(2 * blocks):
        out_ref[0, 0, k // blocks, k % blocks] = spec[:, k * 128 : (k + 1) * 128]


def spectra(x, offs, mats, interpret=False):
    tiles = x.shape[0]
    blocks = x.shape[3] // 256
    return pl.pallas_call(
        functools.partial(send_kernel, blocks),
        out_shape=jax.ShapeDtypeStruct((tiles, ROUNDS, 2, blocks, 256, 128), F32),
        grid_spec=pltpu.PrefetchScalarGridSpec(
            num_scalar_prefetch=1,
            grid=(tiles, ROUNDS),
            in_specs=[
                pl.BlockSpec((1, 2, 256, 256 * blocks), lambda t, r, *_: (t, 0, 0, 0)),
                pl.BlockSpec((1, 1, 256, 768), lambda t, r, *_: (r, t, 0, 0)),
            ],
            out_specs=pl.BlockSpec(
                (1, 1, 2, blocks, 256, 128),
                lambda t, r, *_: (lax.rem(t + 3 - 2 * r, tiles), r, 0, 0, 0, 0),
            ),
        ),
        cost_estimate=pl.CostEstimate(flops=800_000_000 * blocks, bytes_accessed=6_000_000 * blocks, transcendentals=0),
        interpret=interpret,
        name="spectra",
    )(offs, x, mats)


def normalized(p, q, sign):
    real = p[0] * q[0] + p[1] * q[1]
    imag = p[1] * q[0] - p[0] * q[1]
    scale = lax.rsqrt(jnp.maximum(real * real + imag * imag, FLOOR * FLOOR)) * sign
    return (real * scale, imag * scale)


def to_lanes(block_of, part):
    lane = lax.broadcasted_iota(jnp.int32, (A, 128), 1)
    out = jnp.zeros((A, 128), F32)
    for z in range(Z):
        block = block_of(z, slice(part * A, (part + 1) * A))
        if z:
            block = pltpu.roll(block, z, 1)
        out = jnp.where(lane == z, block, out)
    return out


def edge_fix(own_of, far_of, r_ref, ef_ref, er_ref, flip_ref, sign):
    high = lax.Precision.HIGHEST

    def edge(block_of):
        packed = jnp.concatenate([to_lanes(block_of, part) for part in range(2)], axis=1)
        here = jnp.dot(packed, ef_ref[...], precision=high, preferred_element_type=F32)
        turned = jnp.dot(packed, er_ref[...], precision=high, preferred_element_type=F32)
        there = jnp.dot(flip_ref[...], turned, precision=high, preferred_element_type=F32)
        hr, hi = here[:, :128], here[:, 128:]
        tr, ti = there[:, :128], there[:, 128:]
        return ((hr + tr) * 0.5, (hi - ti) * 0.5), ((hi + ti) * 0.5, (tr - hr) * 0.5)

    own_zero, own_last = edge(own_of)
    far_zero, far_last = edge(far_of)
    zero = normalized(own_zero, far_zero, sign)
    last = normalized(own_last, far_last, sign)
    both = jnp.concatenate((zero[0] - last[1], zero[1] + last[0]), axis=1)
    field = jnp.dot(both, er_ref[...], precision=high, preferred_element_type=F32)
    lane = lax.broadcasted_iota(jnp.int32, (A, 128), 1)
    for part in range(2):
        source = field[:, part * 128 : (part + 1) * 128]
        for z in range(Z):
            moved = pltpu.roll(source, 128 - z, 1) if z else source
            place = (slice(part * A, (part + 1) * A), slice(z * 128, (z + 1) * 128))
            r_ref[place] = jnp.where(lane == 0, moved, r_ref[place])


def pair_core(ints_ref, y_ref, far_ref, a_ref, own_ref, r_ref, valid):
    for half in range(2):
        own_ref[:, half * 512 : (half + 1) * 512] = across(y_ref, half * 4, 4, ints_ref[0], a_ref[...])

    def own_of(z, rows):
        return own_ref[rows, z * 128 : (z + 1) * 128]

    def far_of(z, rows):
        return far_ref[z // 2, 0, z % 2, 0, rows, :]

    def chunk(i, _):
        up = pl.ds(pl.multiple_of(i * 8, 8), 8)
        down = pl.ds(pl.multiple_of(i * 8 + A, 8), 8)
        own = dft8([(own_of(z, up), own_of(z, down)) for z in range(Z)], -1.0)
        far = dft8([(far_of(z, up), far_of(z, down)) for z in range(Z)], -1.0)
        back = dft8([normalized(own[u], far[u], valid) for u in range(Z)], 1.0)
        for z in range(Z):
            r_ref[up, z * 128 : (z + 1) * 128] = back[z][0]
            r_ref[down, z * 128 : (z + 1) * 128] = back[z][1]
        return 0

    lax.fori_loop(0, A // 8, chunk, 0)
    return own_of, far_of


def parts(ab_ref, r_ref, v_ref):
    for half in range(2):
        q = dot3_right(ab_ref[...], r_ref[:, half * 512 : (half + 1) * 512])
        for k in range(0, 4, 2):
            rows = [
                jnp.concatenate((q[:A, j * 128 : (j + 1) * 128], q[A:, j * 128 : (j + 1) * 128]), axis=1)
                for j in (k, k + 1)
            ]
            yield half * 4 + k, dot3_left(jnp.concatenate(rows, axis=0), v_ref[...])


def large_pair_kernel(
    ints_ref, y_ref, far_ref, a_ref, ab_ref, v1_ref, v0_ref, ef_ref, er_ref, flip_ref,
    odd_ref, fours_ref, own_ref, r_ref,
):
    step = pl.program_id(0)
    valid = ints_ref[1].astype(F32)
    own_of, far_of = pair_core(ints_ref, y_ref, far_ref, a_ref, own_ref, r_ref, valid)

    @pl.when(step == 0)
    def _():
        for z, part in parts(ab_ref, r_ref, v1_ref.at[0]):
            odd_ref[z : z + 2] = part.reshape(2, A, 512)

    @pl.when(step == 1)
    def _():
        for z, part in parts(ab_ref, r_ref, v1_ref.at[0]):
            odd_ref[z : z + 2] += part.reshape(2, A, 512)

    @pl.when(step == 2)
    def _():
        edge_fix(own_of, far_of, r_ref, ef_ref, er_ref, flip_ref, valid)
        for z, part in parts(ab_ref, r_ref, v0_ref):
            fours_ref[z : z + 2] = part.reshape(2, A, 256)


def small_pair_kernel(ints_ref, y_ref, far_ref, a_ref, ab_ref, v2_ref, odd_ref, fours_ref, *refs):
    surf_ref, peak_ref, own_ref, r_ref = refs[-4:]
    valid = ints_ref[1].astype(F32)
    pair_core(ints_ref, y_ref, far_ref, a_ref, own_ref, r_ref, valid)
    for z, part in parts(ab_ref, r_ref, v2_ref):
        first = fours_ref[z : z + 2].reshape(2 * A, 256)
        odd = odd_ref[z : z + 2].reshape(2 * A, 512)
        y = jnp.concatenate((first + part, first - part), axis=1)
        x = jnp.concatenate((y + odd, y - odd), axis=1)
        x = jnp.maximum(x[:A], x[A:])
        if z == 0:
            surf_ref[0, 0] = x
        else:
            surf_ref[0, 0] = jnp.maximum(surf_ref[0, 0], x)
    peak_ref[0] = jnp.broadcast_to(jnp.max(surf_ref[0, 0]), (8, 128))


SCRATCH = [pltpu.VMEM((256, Z * 128), F32), pltpu.VMEM((256, Z * 128), F32)]


def large_pair(ints, y, far, mat, ab, back1, back0, edges, interpret=False):
    return pl.pallas_call(
        large_pair_kernel,
        out_shape=(jax.ShapeDtypeStruct((Z, A, 512), F32), jax.ShapeDtypeStruct((Z, A, 256), F32)),
        grid_spec=pltpu.PrefetchScalarGridSpec(
            num_scalar_prefetch=1,
            grid=(3,),
            in_specs=[
                pl.BlockSpec((Z, 256, 256), lambda w, *_: (0, 0, w)),
                pl.BlockSpec((4, 1, 2, 1, 256, 128), lambda w, *_: (0, 0, 0, w, 0, 0)),
                whole((256, 768)),
                whole((256, 768)),
                pl.BlockSpec((1, 768, 512), lambda w, *_: (jnp.minimum(w, 1), 0, 0)),
                whole((768, 256)),
                whole((256, 256)),
                whole((256, 256)),
                whole((128, 128)),
            ],
            out_specs=(whole((Z, A, 512)), whole((Z, A, 256))),
            scratch_shapes=SCRATCH,
        ),
        cost_estimate=pl.CostEstimate(flops=6_000_000_000, bytes_accessed=16_000_000, transcendentals=500_000),
        interpret=interpret,
    )(ints, y, far, mat, ab, back1, back0, *edges)


def small_pair(rnd, ints, y, far, mat, ab, back2, odd, fours, before, interpret=False):
    args = [y, far, mat, ab, back2, odd, fours]
    pick = rnd if far.shape[1] > 1 else 0
    in_specs = [
        whole((Z, 256, 256)),
        pl.BlockSpec((4, 1, 2, 1, 256, 128), lambda w, *_: (0, pick, 0, 0, 0, 0)),
        whole((256, 768)),
        whole((256, 768)),
        whole((768, 256)),
        whole((Z, A, 512)),
        whole((Z, A, 256)),
    ]
    aliases = {}
    if before is not None:
        aliases = {len(args) + 1: 0, len(args) + 2: 1}
        args += list(before)
        in_specs += [pl.BlockSpec(memory_space=pl.ANY)] * 2
    return pl.pallas_call(
        small_pair_kernel,
        out_shape=(
            jax.ShapeDtypeStruct((ROUNDS, 1, A, L), F32),
            jax.ShapeDtypeStruct((ROUNDS, 8, 128), F32),
        ),
        grid_spec=pltpu.PrefetchScalarGridSpec(
            num_scalar_prefetch=1,
            grid=(1,),
            in_specs=in_specs,
            out_specs=(
                pl.BlockSpec((1, 1, A, L), lambda w, *_: (rnd, 0, 0, 0)),
                pl.BlockSpec((1, 8, 128), lambda w, *_: (rnd, 0, 0)),
            ),
            scratch_shapes=SCRATCH,
        ),
        input_output_aliases=aliases,
        cost_estimate=pl.CostEstimate(flops=2_000_000_000, bytes_accessed=10_000_000, transcendentals=300_000),
        interpret=interpret,
    )(ints, *args)


def from_next(x, step, groups):
    return lax.ppermute(x, "tile", [(g + step, g) for g in range(groups - step)])


def after(*values):
    return lax.optimization_barrier(values)


def register(stored, offsets):
    size = lax.axis_size(("tile", "slab"))
    groups = lax.axis_size("tile")
    slabs = lax.axis_size("slab")
    place = lax.axis_index(("tile", "slab"))

    def gather(x):
        return lax.all_to_all(x, "slab", split_axis=0, concat_axis=1, tiled=True)[0]

    def collect(x):
        return lax.all_to_all(x, "slab", split_axis=0, concat_axis=0, tiled=True)

    small_src = along(small_kernel, stored, (twos_table(),), 256)
    small_all = gather(small_src)
    small_src, table = after(small_src, odd_table())
    large_src = along(large_kernel, stored, (table, fours_table()), 768)
    large_src, mine = after(large_src, offsets[:, 1, 0])
    turns = [mine] + [
        lax.ppermute(mine, "slab", [((i + k) % slabs, i) for i in range(slabs)]) for k in range(1, slabs)
    ]
    base = lax.optimization_barrier(across_base())
    given = jnp.roll(jnp.stack(turns, axis=1), lax.axis_index("slab"), axis=1)
    mats = jnp.stack([jnp.stack([across_forward(given[r, j], base) for j in range(slabs)]) for r in range(ROUNDS)])
    small_all, large_src = after(small_all, large_src)
    large_all = gather(large_src)

    def shifted(src):
        made = spectra(src, given, mats)
        near = from_next(jnp.stack((made[3, 0], made[0, 1])), 1, groups)
        far = from_next(made[1:, 1], 2, groups)
        zero = [made[0, 0], made[1, 0], made[2, 0], near[0]]
        one = [near[1], far[0], far[1], far[2]]
        return zero, one

    large_zero, large_one = [jnp.stack(x)[:, None] for x in shifted(large_src)]
    both = zip(*shifted(small_src), strict=True)
    small_sent = jnp.stack([x for two in both for x in two]).reshape(slabs, ROUNDS, 2, 1, 256, 128)
    valid = (
        jnp.logical_and(place % GC != GC - 1, place + 1 < size),
        place + GC < size,
    )
    own = [offsets[r, 0, 0] for r in range(ROUNDS)]
    ints = [jnp.stack((own[r], valid[r].astype(jnp.int32))) for r in range(ROUNDS)]
    own_mats = [across_forward(o, base) for o in own]
    ab = across_back()
    edges = edge_tables()
    back1, back0, back2 = odd_back(), fours_back(), twos_back()
    large_all, large_zero, small_sent, large_one, own_mats, ab, edges, back1, back0, back2 = after(
        large_all, large_zero, small_sent, large_one, own_mats, ab, edges, back1, back0, back2
    )
    far_zero = collect(large_zero)
    far_zero, large_one = after(far_zero, large_one)
    far_one = collect(large_one)
    first = large_pair(ints[0], large_all, far_zero, own_mats[0], ab, back1, back0, edges)
    far_one, first, small_sent = after(far_one, first, small_sent)
    small_far = collect(small_sent)
    second = large_pair(ints[1], large_all, far_one, own_mats[1], ab, back1, back0, edges)
    out = small_pair(0, ints[0], small_all, small_far, own_mats[0], ab, back2, *first, None)
    surface, peak = small_pair(1, ints[1], small_all, small_far, own_mats[1], ab, back2, *second, out)
    return surface, peak[:, 0, :1]


def solution(mesh):
    return jax.shard_map(
        register,
        mesh=mesh,
        in_specs=(P("tile", "slab", None, None), P(None, None, ("tile", "slab"))),
        out_specs=(P(None, ("tile", "slab"), None, None), P(None, ("tile", "slab"))),
        check_vma=False,
    )
```

```python
import functools
import math

import jax
import jax.numpy as jnp
from jax import lax
from jax.experimental import pallas as pl
from jax.experimental.pallas import tpu as pltpu
from jax.sharding import PartitionSpec as P


GC = 7
ROUNDS = 2
A = 128
L = 1024
Z = 8
FLOOR = 0.25
BF = jnp.bfloat16
F32 = jnp.float32
HALF = math.sqrt(0.5)


def split(x):
    hi = x.astype(BF)
    lo = (x - hi.astype(F32)).astype(BF)
    return hi, lo


def split_table(x):
    hi = lax.reduce_precision(x, exponent_bits=8, mantissa_bits=7)
    return hi.astype(BF), (x - hi).astype(BF)


def three_rows(x):
    hi, lo = split_table(x)
    return jnp.concatenate((hi, hi, lo), axis=0)


def three_cols(x):
    hi, lo = split_table(x)
    return jnp.concatenate((hi, hi, lo), axis=1)


def trig(index, total):
    angle = (index % total).astype(F32) * (2.0 * math.pi / total)
    return jnp.cos(angle), jnp.sin(angle)


SEEDS = []


def iota(length):
    return lax.optimization_barrier((jnp.arange(length, dtype=jnp.int32), *SEEDS))[0]


def odd_table():
    rows = iota(512)[:, None]
    m = iota(256)[None, :]
    c, s = trig(rows * (2 * m + 1), L)
    scale = 1.0 / L
    return three_rows(
        scale * jnp.concatenate((c[:, :128], -s[:, :128], c[:, 128:], -s[:, 128:]), axis=1)
    )


def fours_table():
    n = iota(256)[:, None]
    m = iota(A)[None, :]
    c, s = trig(n * (4 * m), L)
    last = (1 - 2 * (n % 2)).astype(F32)
    return three_rows((1.0 / L) * jnp.concatenate((c, jnp.where(m == 0, last, -s)), axis=1))


def twos_table():
    n = iota(256)[:, None]
    m = iota(A)[None, :]
    c, s = trig(n * (4 * m + 2), L)
    return three_rows((1.0 / L) * jnp.concatenate((c, -s), axis=1))


def odd_back():
    cols = iota(512)[None, :]
    m = iota(256)[:, None]
    c, s = trig(cols * (2 * m + 1), L)
    scale = 2.0 / L
    return jnp.stack(
        [three_rows(scale * jnp.concatenate((c[b : b + A], -s[b : b + A]), axis=0)) for b in (0, A)]
    )


def fours_back():
    cols = iota(256)[None, :]
    m = iota(A)[:, None]
    c, s = trig(cols * (4 * m), L)
    last = (1 - 2 * (cols % 2)).astype(F32)
    scale = 2.0 / L
    real = jnp.where(m == 0, 0.5 * scale, scale * c)
    imag = jnp.where(m == 0, 0.5 * scale * last, -scale * s)
    return three_rows(jnp.concatenate((real, imag), axis=0))


def twos_back():
    cols = iota(256)[None, :]
    m = iota(A)[:, None]
    c, s = trig(cols * (4 * m + 2), L)
    return three_rows((2.0 / L) * jnp.concatenate((c, -s), axis=0))


def across_base():
    v = iota(A)
    return trig(v[:, None] * v[None, :], A)


def across_forward(offset, base):
    c0, s0 = base
    cv, sv = trig(offset * iota(A)[:, None], A)
    c = c0 * cv + s0 * sv
    s = s0 * cv - c0 * sv
    top = jnp.concatenate((c, s), axis=1)
    low = jnp.concatenate((-s, c), axis=1)
    return three_cols(jnp.concatenate((top, low), axis=0))


def across_back():
    v = iota(A)[None, :]
    a = iota(A)[:, None]
    c, s = trig(a * v, A)
    top = jnp.concatenate((c, -s), axis=1)
    low = jnp.concatenate((s, c), axis=1)
    return three_cols(jnp.concatenate((top, low), axis=0))


def edge_tables():
    lane = iota(A)
    i = lane[:, None]
    j = lane[None, :]
    inside = jnp.logical_and(i < Z, j < Z)
    c, s = trig(i * j, Z)
    c = jnp.where(inside, c, 0.0)
    s = jnp.where(inside, s, 0.0)
    fwd = jnp.concatenate(
        (jnp.concatenate((c, -s), axis=1), jnp.concatenate((s, c), axis=1)), axis=0
    )
    rev = jnp.concatenate(
        (jnp.concatenate((c, s), axis=1), jnp.concatenate((-s, c), axis=1)), axis=0
    )
    flip = ((i + j) % A == 0).astype(F32)
    return fwd, rev, flip


def dot3_left(x, table):
    hi, lo = split(x)
    return jnp.dot(jnp.concatenate((hi, lo, hi), axis=1), table, preferred_element_type=F32)


def dot3_right(table, x):
    hi, lo = split(x)
    return jnp.dot(table, jnp.concatenate((hi, lo, hi), axis=0), preferred_element_type=F32)


def whole(shape):
    return pl.BlockSpec(shape, lambda *_: (0,) * len(shape))


def times_i(x, sign):
    return (-sign * x[1], sign * x[0])


def cadd(x, y):
    return (x[0] + y[0], x[1] + y[1])


def csub(x, y):
    return (x[0] - y[0], x[1] - y[1])


def eighth(x, sign):
    return ((x[0] - sign * x[1]) * HALF, (x[1] + sign * x[0]) * HALF)


def dft4(x, sign):
    a = cadd(x[0], x[2])
    b = csub(x[0], x[2])
    c = cadd(x[1], x[3])
    d = times_i(csub(x[1], x[3]), sign)
    return [cadd(a, c), cadd(b, d), csub(a, c), csub(b, d)]


def dft8(x, sign):
    even = dft4([x[0], x[2], x[4], x[6]], sign)
    odd = dft4([x[1], x[3], x[5], x[7]], sign)
    odd = [odd[0], eighth(odd[1], sign), times_i(odd[2], sign), times_i(eighth(odd[3], sign), sign)]
    return [cadd(even[k], odd[k]) for k in range(4)] + [csub(even[k], odd[k]) for k in range(4)]


def large_kernel(x_ref, w1_ref, w0_ref, out_ref):
    x = x_ref[0].reshape(512, L)
    out_ref[0, :, :, :512] = dot3_left(x[:, :512] - x[:, 512:], w1_ref[...]).reshape(2, 256, 512)
    y = x[:, :512] + x[:, 512:]
    out_ref[0, :, :, 512:] = dot3_left(y[:, :256] + y[:, 256:], w0_ref[...]).reshape(2, 256, 256)


def small_kernel(x_ref, w2_ref, out_ref):
    x = x_ref[0].reshape(512, L)
    y = x[:, :512] + x[:, 512:]
    out_ref[0] = dot3_left(y[:, :256] - y[:, 256:], w2_ref[...]).reshape(2, 256, 256)


def along(kernel, stored, tables, columns, interpret=False):
    tiles, planes = stored.shape[:2]
    return pl.pallas_call(
        kernel,
        out_shape=jax.ShapeDtypeStruct((tiles, planes, 256, columns), F32),
        grid_spec=pl.GridSpec(
            grid=(tiles,),
            in_specs=[pl.BlockSpec((1, planes, 256, L), lambda i: (i, 0, 0, 0))]
            + [whole(t.shape) for t in tables],
            out_specs=pl.BlockSpec((1, planes, 256, columns), lambda i: (i, 0, 0, 0)),
        ),
        cost_estimate=pl.CostEstimate(flops=6_000_000 * columns, bytes_accessed=14_000_000, transcendentals=0),
        interpret=interpret,
    )(stored, *tables)


def across(y_ref, first, count, offset, table):
    later = lax.broadcasted_iota(jnp.int32, (A, 256), 0) >= offset
    picked = [jnp.where(later, y_ref[first + k, :A, :], y_ref[first + k, A:, :]) for k in range(count)]
    real = jnp.concatenate([p[:, :128] for p in picked], axis=1)
    imag = jnp.concatenate([p[:, 128:] for p in picked], axis=1)
    return dot3_right(table, jnp.concatenate((real, imag), axis=0))


def send_kernel(blocks, off_ref, x_ref, a_ref, out_ref):
    tile = pl.program_id(0)
    rnd = pl.program_id(1)
    later = lax.broadcasted_iota(jnp.int32, (A, 256), 0) >= off_ref[rnd, tile]
    picked = [
        jnp.where(later, x_ref[0, p, :A, w * 256 : (w + 1) * 256], x_ref[0, p, A:, w * 256 : (w + 1) * 256])
        for p in range(2)
        for w in range(blocks)
    ]
    real = jnp.concatenate([p[:, :128] for p in picked], axis=1)
    imag = jnp.concatenate([p[:, 128:] for p in picked], axis=1)
    spec = dot3_right(a_ref[0, 0], jnp.concatenate((real, imag), axis=0))
    for k in range(2 * blocks):
        out_ref[0, 0, k // blocks, k % blocks] = spec[:, k * 128 : (k + 1) * 128]


def spectra(x, offs, mats, interpret=False):
    tiles = x.shape[0]
    blocks = x.shape[3] // 256
    return pl.pallas_call(
        functools.partial(send_kernel, blocks),
        out_shape=jax.ShapeDtypeStruct((tiles, ROUNDS, 2, blocks, 256, 128), F32),
        grid_spec=pltpu.PrefetchScalarGridSpec(
            num_scalar_prefetch=1,
            grid=(tiles, ROUNDS),
            in_specs=[
                pl.BlockSpec((1, 2, 256, 256 * blocks), lambda t, r, *_: (t, 0, 0, 0)),
                pl.BlockSpec((1, 1, 256, 768), lambda t, r, *_: (r, t, 0, 0)),
            ],
            out_specs=pl.BlockSpec(
                (1, 1, 2, blocks, 256, 128),
                lambda t, r, *_: (lax.rem(t + 3 - 2 * r, tiles), r, 0, 0, 0, 0),
            ),
        ),
        cost_estimate=pl.CostEstimate(flops=800_000_000 * blocks, bytes_accessed=6_000_000 * blocks, transcendentals=0),
        interpret=interpret,
        name="spectra",
    )(offs, x, mats)


def normalized(p, q, sign):
    real = p[0] * q[0] + p[1] * q[1]
    imag = p[1] * q[0] - p[0] * q[1]
    scale = lax.rsqrt(jnp.maximum(real * real + imag * imag, FLOOR * FLOOR)) * sign
    return (real * scale, imag * scale)


def to_lanes(block_of, part):
    lane = lax.broadcasted_iota(jnp.int32, (A, 128), 1)
    out = jnp.zeros((A, 128), F32)
    for z in range(Z):
        block = block_of(z, slice(part * A, (part + 1) * A))
        if z:
            block = pltpu.roll(block, z, 1)
        out = jnp.where(lane == z, block, out)
    return out


def edge_fix(own_of, far_of, r_ref, ef_ref, er_ref, flip_ref, sign):
    high = lax.Precision.HIGHEST

    def edge(block_of):
        packed = jnp.concatenate([to_lanes(block_of, part) for part in range(2)], axis=1)
        here = jnp.dot(packed, ef_ref[...], precision=high, preferred_element_type=F32)
        turned = jnp.dot(packed, er_ref[...], precision=high, preferred_element_type=F32)
        there = jnp.dot(flip_ref[...], turned, precision=high, preferred_element_type=F32)
        hr, hi = here[:, :128], here[:, 128:]
        tr, ti = there[:, :128], there[:, 128:]
        return ((hr + tr) * 0.5, (hi - ti) * 0.5), ((hi + ti) * 0.5, (tr - hr) * 0.5)

    own_zero, own_last = edge(own_of)
    far_zero, far_last = edge(far_of)
    zero = normalized(own_zero, far_zero, sign)
    last = normalized(own_last, far_last, sign)
    both = jnp.concatenate((zero[0] - last[1], zero[1] + last[0]), axis=1)
    field = jnp.dot(both, er_ref[...], precision=high, preferred_element_type=F32)
    lane = lax.broadcasted_iota(jnp.int32, (A, 128), 1)
    for part in range(2):
        source = field[:, part * 128 : (part + 1) * 128]
        for z in range(Z):
            moved = pltpu.roll(source, 128 - z, 1) if z else source
            place = (slice(part * A, (part + 1) * A), slice(z * 128, (z + 1) * 128))
            r_ref[place] = jnp.where(lane == 0, moved, r_ref[place])


def pair_core(ints_ref, y_ref, far_ref, a_ref, own_ref, r_ref, valid):
    for half in range(2):
        own_ref[:, half * 512 : (half + 1) * 512] = across(y_ref, half * 4, 4, ints_ref[0], a_ref[...])

    def own_of(z, rows):
        return own_ref[rows, z * 128 : (z + 1) * 128]

    def far_of(z, rows):
        return far_ref[z // 2, 0, z % 2, 0, rows, :]

    def chunk(i, _):
        up = pl.ds(pl.multiple_of(i * 8, 8), 8)
        down = pl.ds(pl.multiple_of(i * 8 + A, 8), 8)
        own = dft8([(own_of(z, up), own_of(z, down)) for z in range(Z)], -1.0)
        far = dft8([(far_of(z, up), far_of(z, down)) for z in range(Z)], -1.0)
        back = dft8([normalized(own[u], far[u], valid) for u in range(Z)], 1.0)
        for z in range(Z):
            r_ref[up, z * 128 : (z + 1) * 128] = back[z][0]
            r_ref[down, z * 128 : (z + 1) * 128] = back[z][1]
        return 0

    lax.fori_loop(0, A // 8, chunk, 0)
    return own_of, far_of


def parts(ab_ref, r_ref, v_ref):
    for half in range(2):
        q = dot3_right(ab_ref[...], r_ref[:, half * 512 : (half + 1) * 512])
        for k in range(0, 4, 2):
            rows = [
                jnp.concatenate((q[:A, j * 128 : (j + 1) * 128], q[A:, j * 128 : (j + 1) * 128]), axis=1)
                for j in (k, k + 1)
            ]
            yield half * 4 + k, dot3_left(jnp.concatenate(rows, axis=0), v_ref[...])


def large_pair_kernel(
    ints_ref, y_ref, far_ref, a_ref, ab_ref, v1_ref, v0_ref, ef_ref, er_ref, flip_ref,
    odd_ref, fours_ref, own_ref, r_ref,
):
    step = pl.program_id(0)
    valid = ints_ref[1].astype(F32)
    own_of, far_of = pair_core(ints_ref, y_ref, far_ref, a_ref, own_ref, r_ref, valid)

    @pl.when(step == 0)
    def _():
        for z, part in parts(ab_ref, r_ref, v1_ref.at[0]):
            odd_ref[z : z + 2] = part.reshape(2, A, 512)

    @pl.when(step == 1)
    def _():
        for z, part in parts(ab_ref, r_ref, v1_ref.at[0]):
            odd_ref[z : z + 2] += part.reshape(2, A, 512)

    @pl.when(step == 2)
    def _():
        edge_fix(own_of, far_of, r_ref, ef_ref, er_ref, flip_ref, valid)
        for z, part in parts(ab_ref, r_ref, v0_ref):
            fours_ref[z : z + 2] = part.reshape(2, A, 256)


def small_pair_kernel(ints_ref, y_ref, far_ref, a_ref, ab_ref, v2_ref, odd_ref, fours_ref, *refs):
    surf_ref, peak_ref, own_ref, r_ref = refs[-4:]
    valid = ints_ref[1].astype(F32)
    pair_core(ints_ref, y_ref, far_ref, a_ref, own_ref, r_ref, valid)
    for z, part in parts(ab_ref, r_ref, v2_ref):
        first = fours_ref[z : z + 2].reshape(2 * A, 256)
        odd = odd_ref[z : z + 2].reshape(2 * A, 512)
        y = jnp.concatenate((first + part, first - part), axis=1)
        x = jnp.concatenate((y + odd, y - odd), axis=1)
        x = jnp.maximum(x[:A], x[A:])
        if z == 0:
            surf_ref[0, 0] = x
        else:
            surf_ref[0, 0] = jnp.maximum(surf_ref[0, 0], x)
    peak_ref[0] = jnp.broadcast_to(jnp.max(surf_ref[0, 0]), (8, 128))


SCRATCH = [pltpu.VMEM((256, Z * 128), F32), pltpu.VMEM((256, Z * 128), F32)]


def large_pair(ints, y, far, mat, ab, back1, back0, edges, interpret=False):
    return pl.pallas_call(
        large_pair_kernel,
        out_shape=(jax.ShapeDtypeStruct((Z, A, 512), F32), jax.ShapeDtypeStruct((Z, A, 256), F32)),
        grid_spec=pltpu.PrefetchScalarGridSpec(
            num_scalar_prefetch=1,
            grid=(3,),
            in_specs=[
                pl.BlockSpec((Z, 256, 256), lambda w, *_: (0, 0, w)),
                pl.BlockSpec((4, 1, 2, 1, 256, 128), lambda w, *_: (0, 0, 0, w, 0, 0)),
                whole((256, 768)),
                whole((256, 768)),
                pl.BlockSpec((1, 768, 512), lambda w, *_: (jnp.minimum(w, 1), 0, 0)),
                whole((768, 256)),
                whole((256, 256)),
                whole((256, 256)),
                whole((128, 128)),
            ],
            out_specs=(whole((Z, A, 512)), whole((Z, A, 256))),
            scratch_shapes=SCRATCH,
        ),
        cost_estimate=pl.CostEstimate(flops=6_000_000_000, bytes_accessed=16_000_000, transcendentals=500_000),
        interpret=interpret,
    )(ints, y, far, mat, ab, back1, back0, *edges)


def small_pair(rnd, ints, y, far, mat, ab, back2, odd, fours, before, interpret=False):
    args = [y, far, mat, ab, back2, odd, fours]
    pick = rnd if far.shape[1] > 1 else 0
    in_specs = [
        whole((Z, 256, 256)),
        pl.BlockSpec((4, 1, 2, 1, 256, 128), lambda w, *_: (0, pick, 0, 0, 0, 0)),
        whole((256, 768)),
        whole((256, 768)),
        whole((768, 256)),
        whole((Z, A, 512)),
        whole((Z, A, 256)),
    ]
    aliases = {}
    if before is not None:
        aliases = {len(args) + 1: 0, len(args) + 2: 1}
        args += list(before)
        in_specs += [pl.BlockSpec(memory_space=pl.ANY)] * 2
    return pl.pallas_call(
        small_pair_kernel,
        out_shape=(
            jax.ShapeDtypeStruct((ROUNDS, 1, A, L), F32),
            jax.ShapeDtypeStruct((ROUNDS, 8, 128), F32),
        ),
        grid_spec=pltpu.PrefetchScalarGridSpec(
            num_scalar_prefetch=1,
            grid=(1,),
            in_specs=in_specs,
            out_specs=(
                pl.BlockSpec((1, 1, A, L), lambda w, *_: (rnd, 0, 0, 0)),
                pl.BlockSpec((1, 8, 128), lambda w, *_: (rnd, 0, 0)),
            ),
            scratch_shapes=SCRATCH,
        ),
        input_output_aliases=aliases,
        cost_estimate=pl.CostEstimate(flops=2_000_000_000, bytes_accessed=10_000_000, transcendentals=300_000),
        interpret=interpret,
    )(ints, *args)


def from_next(x, step, groups):
    return lax.ppermute(x, "tile", [(g + step, g) for g in range(groups - step)])


def after(*values):
    return lax.optimization_barrier(values)


def register(stored, offsets):
    size = lax.axis_size(("tile", "slab"))
    groups = lax.axis_size("tile")
    slabs = lax.axis_size("slab")
    place = lax.axis_index(("tile", "slab"))

    def gather(x):
        return lax.all_to_all(x, "slab", split_axis=0, concat_axis=1, tiled=True)[0]

    def collect(x):
        return lax.all_to_all(x, "slab", split_axis=0, concat_axis=0, tiled=True)

    small_src = along(small_kernel, stored, (twos_table(),), 256)
    small_all = gather(small_src)
    mine = offsets[:, 1, 0]
    turns = [mine] + [lax.ppermute(mine, "slab", [((i + k) % slabs, i) for i in range(slabs)]) for k in range(1, slabs)]
    large_src = along(large_kernel, stored, (odd_table(), fours_table()), 768)
    base = lax.optimization_barrier(across_base())
    given = jnp.roll(jnp.stack(turns, axis=1), lax.axis_index("slab"), axis=1)
    mats = jnp.stack([jnp.stack([across_forward(given[r, j], base) for j in range(slabs)]) for r in range(ROUNDS)])
    small_all, band_src = after(small_all, large_src)
    large_all = gather(band_src)

    def shifted(made):
        near = from_next(jnp.stack((made[3, 0], made[0, 1])), 1, groups)
        far = from_next(made[1:, 1], 2, groups)
        zero = [made[0, 0], made[1, 0], made[2, 0], near[0]]
        one = [near[1], far[0], far[1], far[2]]
        return zero, one

    large_made = spectra(large_src, given, mats)
    large_zero, large_one = [jnp.stack(x)[:, None] for x in shifted(large_made)]
    small_made = spectra(small_src, given, mats)
    both = zip(*shifted(small_made), strict=True)
    small_sent = jnp.stack([x for two in both for x in two]).reshape(slabs, ROUNDS, 2, 1, 256, 128)
    valid = (
        jnp.logical_and(place % GC != GC - 1, place + 1 < size),
        place + GC < size,
    )
    SEEDS.append(small_made)
    own = [offsets[r, 0, 0] for r in range(ROUNDS)]
    ints = [jnp.stack((own[r], valid[r].astype(jnp.int32))) for r in range(ROUNDS)]
    own_mats = [across_forward(o, base) for o in own]
    ab = across_back()
    edges = edge_tables()
    back1, back0, back2 = odd_back(), fours_back(), twos_back()
    SEEDS.clear()
    large_all, large_zero = after(large_all, large_zero)
    far_zero = collect(large_zero)
    far_zero, large_one = after(far_zero, large_one)
    far_one = collect(large_one)
    first = large_pair(ints[0], large_all, far_zero, own_mats[0], ab, back1, back0, edges)
    far_one, first, small_sent = after(far_one, first, small_sent)
    small_far = collect(small_sent)
    second = large_pair(ints[1], large_all, far_one, own_mats[1], ab, back1, back0, edges)
    out = small_pair(0, ints[0], small_all, small_far, own_mats[0], ab, back2, *first, None)
    surface, peak = small_pair(1, ints[1], small_all, small_far, own_mats[1], ab, back2, *second, out)
    return surface, peak[:, 0, :1]


def solution(mesh):
    return jax.shard_map(
        register,
        mesh=mesh,
        in_specs=(P("tile", "slab", None, None), P(None, None, ("tile", "slab"))),
        out_specs=(P(None, ("tile", "slab"), None, None), P(None, ("tile", "slab"))),
        check_vma=False,
    )
```

```python
import functools
import math

import jax
import jax.numpy as jnp
from jax import lax
from jax.experimental import pallas as pl
from jax.experimental.pallas import tpu as pltpu
from jax.sharding import PartitionSpec as P


GC = 7
ROUNDS = 2
A = 128
L = 1024
Z = 8
FLOOR = 0.25
BF = jnp.bfloat16
F32 = jnp.float32
HALF = math.sqrt(0.5)


def split(x):
    hi = x.astype(BF)
    lo = (x - hi.astype(F32)).astype(BF)
    return hi, lo


def split_table(x):
    hi = lax.reduce_precision(x, exponent_bits=8, mantissa_bits=7)
    return hi.astype(BF), (x - hi).astype(BF)


def three_rows(x):
    hi, lo = split_table(x)
    return jnp.concatenate((hi, hi, lo), axis=0)


def three_cols(x):
    hi, lo = split_table(x)
    return jnp.concatenate((hi, hi, lo), axis=1)


def trig(index, total):
    angle = (index % total).astype(F32) * (2.0 * math.pi / total)
    return jnp.cos(angle), jnp.sin(angle)


SEEDS = []


def iota(length):
    return lax.optimization_barrier((jnp.arange(length, dtype=jnp.int32), *SEEDS))[0]


def odd_table():
    rows = iota(512)[:, None]
    m = iota(256)[None, :]
    c, s = trig(rows * (2 * m + 1), L)
    scale = 1.0 / L
    return three_rows(
        scale * jnp.concatenate((c[:, :128], -s[:, :128], c[:, 128:], -s[:, 128:]), axis=1)
    )


def fours_table():
    n = iota(256)[:, None]
    m = iota(A)[None, :]
    c, s = trig(n * (4 * m), L)
    last = (1 - 2 * (n % 2)).astype(F32)
    return three_rows((1.0 / L) * jnp.concatenate((c, jnp.where(m == 0, last, -s)), axis=1))


def twos_table():
    n = iota(256)[:, None]
    m = iota(A)[None, :]
    c, s = trig(n * (4 * m + 2), L)
    return three_rows((1.0 / L) * jnp.concatenate((c, -s), axis=1))


def odd_back():
    cols = iota(512)[None, :]
    m = iota(256)[:, None]
    c, s = trig(cols * (2 * m + 1), L)
    scale = 2.0 / L
    return jnp.stack(
        [three_rows(scale * jnp.concatenate((c[b : b + A], -s[b : b + A]), axis=0)) for b in (0, A)]
    )


def fours_back():
    cols = iota(256)[None, :]
    m = iota(A)[:, None]
    c, s = trig(cols * (4 * m), L)
    last = (1 - 2 * (cols % 2)).astype(F32)
    scale = 2.0 / L
    real = jnp.where(m == 0, 0.5 * scale, scale * c)
    imag = jnp.where(m == 0, 0.5 * scale * last, -scale * s)
    return three_rows(jnp.concatenate((real, imag), axis=0))


def twos_back():
    cols = iota(256)[None, :]
    m = iota(A)[:, None]
    c, s = trig(cols * (4 * m + 2), L)
    return three_rows((2.0 / L) * jnp.concatenate((c, -s), axis=0))


def across_base():
    v = iota(A)
    return trig(v[:, None] * v[None, :], A)


def across_forward(offset, base):
    c0, s0 = base
    cv, sv = trig(offset * iota(A)[:, None], A)
    c = c0 * cv + s0 * sv
    s = s0 * cv - c0 * sv
    top = jnp.concatenate((c, s), axis=1)
    low = jnp.concatenate((-s, c), axis=1)
    return three_cols(jnp.concatenate((top, low), axis=0))


def across_back():
    v = iota(A)[None, :]
    a = iota(A)[:, None]
    c, s = trig(a * v, A)
    top = jnp.concatenate((c, -s), axis=1)
    low = jnp.concatenate((s, c), axis=1)
    return three_cols(jnp.concatenate((top, low), axis=0))


def edge_tables():
    lane = iota(A)
    i = lane[:, None]
    j = lane[None, :]
    inside = jnp.logical_and(i < Z, j < Z)
    c, s = trig(i * j, Z)
    c = jnp.where(inside, c, 0.0)
    s = jnp.where(inside, s, 0.0)
    fwd = jnp.concatenate(
        (jnp.concatenate((c, -s), axis=1), jnp.concatenate((s, c), axis=1)), axis=0
    )
    rev = jnp.concatenate(
        (jnp.concatenate((c, s), axis=1), jnp.concatenate((-s, c), axis=1)), axis=0
    )
    flip = ((i + j) % A == 0).astype(F32)
    return fwd, rev, flip


def dot3_left(x, table):
    hi, lo = split(x)
    return jnp.dot(jnp.concatenate((hi, lo, hi), axis=1), table, preferred_element_type=F32)


def dot3_right(table, x):
    hi, lo = split(x)
    return jnp.dot(table, jnp.concatenate((hi, lo, hi), axis=0), preferred_element_type=F32)


def whole(shape):
    return pl.BlockSpec(shape, lambda *_: (0,) * len(shape))


def times_i(x, sign):
    return (-sign * x[1], sign * x[0])


def cadd(x, y):
    return (x[0] + y[0], x[1] + y[1])


def csub(x, y):
    return (x[0] - y[0], x[1] - y[1])


def eighth(x, sign):
    return ((x[0] - sign * x[1]) * HALF, (x[1] + sign * x[0]) * HALF)


def dft4(x, sign):
    a = cadd(x[0], x[2])
    b = csub(x[0], x[2])
    c = cadd(x[1], x[3])
    d = times_i(csub(x[1], x[3]), sign)
    return [cadd(a, c), cadd(b, d), csub(a, c), csub(b, d)]


def dft8(x, sign):
    even = dft4([x[0], x[2], x[4], x[6]], sign)
    odd = dft4([x[1], x[3], x[5], x[7]], sign)
    odd = [odd[0], eighth(odd[1], sign), times_i(odd[2], sign), times_i(eighth(odd[3], sign), sign)]
    return [cadd(even[k], odd[k]) for k in range(4)] + [csub(even[k], odd[k]) for k in range(4)]


def large_kernel(x_ref, w1_ref, w0_ref, out_ref):
    x = x_ref[0].reshape(512, L)
    out_ref[0, :, :, :512] = dot3_left(x[:, :512] - x[:, 512:], w1_ref[...]).reshape(2, 256, 512)
    y = x[:, :512] + x[:, 512:]
    out_ref[0, :, :, 512:] = dot3_left(y[:, :256] + y[:, 256:], w0_ref[...]).reshape(2, 256, 256)


def small_kernel(x_ref, w2_ref, out_ref):
    x = x_ref[0].reshape(512, L)
    y = x[:, :512] + x[:, 512:]
    out_ref[0] = dot3_left(y[:, :256] - y[:, 256:], w2_ref[...]).reshape(2, 256, 256)


def along(kernel, stored, tables, columns, interpret=False):
    tiles, planes = stored.shape[:2]
    return pl.pallas_call(
        kernel,
        out_shape=jax.ShapeDtypeStruct((tiles, planes, 256, columns), F32),
        grid_spec=pl.GridSpec(
            grid=(tiles,),
            in_specs=[pl.BlockSpec((1, planes, 256, L), lambda i: (i, 0, 0, 0))]
            + [whole(t.shape) for t in tables],
            out_specs=pl.BlockSpec((1, planes, 256, columns), lambda i: (i, 0, 0, 0)),
        ),
        cost_estimate=pl.CostEstimate(flops=6_000_000 * columns, bytes_accessed=14_000_000, transcendentals=0),
        interpret=interpret,
    )(stored, *tables)


def across(y_ref, first, count, offset, table):
    later = lax.broadcasted_iota(jnp.int32, (A, 256), 0) >= offset
    picked = [jnp.where(later, y_ref[first + k, :A, :], y_ref[first + k, A:, :]) for k in range(count)]
    real = jnp.concatenate([p[:, :128] for p in picked], axis=1)
    imag = jnp.concatenate([p[:, 128:] for p in picked], axis=1)
    return dot3_right(table, jnp.concatenate((real, imag), axis=0))


def send_kernel(blocks, tile_ref, round_ref, off_ref, x_ref, a_ref, near_ref, far_ref, keep_ref):
    i = pl.program_id(0)
    later = lax.broadcasted_iota(jnp.int32, (A, 256), 0) >= off_ref[round_ref[i], tile_ref[i]]
    picked = [
        jnp.where(later, x_ref[0, p, :A, w * 256 : (w + 1) * 256], x_ref[0, p, A:, w * 256 : (w + 1) * 256])
        for p in range(2)
        for w in range(blocks)
    ]
    real = jnp.concatenate([p[:, :128] for p in picked], axis=1)
    imag = jnp.concatenate([p[:, 128:] for p in picked], axis=1)
    spec = dot3_right(a_ref[0, 0], jnp.concatenate((real, imag), axis=0))

    def put(ref):
        for k in range(2 * blocks):
            ref[0, k // blocks, k % blocks] = spec[:, k * 128 : (k + 1) * 128]

    @pl.when(i < 2)
    def _():
        put(near_ref)

    @pl.when(jnp.logical_and(i >= 2, i < 5))
    def _():
        put(far_ref)

    @pl.when(i >= 5)
    def _():
        put(keep_ref)


SEND_TILE = (0, 3, 0, 1, 2, 1, 2, 3)
SEND_ROUND = (0, 1, 1, 1, 1, 0, 0, 0)


def spectra(x, offs, mats, interpret=False):
    blocks = x.shape[3] // 256

    def out(count, first):
        shape = (2, blocks, 256, 128)
        return (
            jax.ShapeDtypeStruct((count, *shape), F32),
            pl.BlockSpec((1, *shape), lambda i, *_: (jnp.clip(i - first, 0, count - 1), 0, 0, 0, 0)),
        )

    outs = (out(2, 0), out(3, 2), out(3, 5))
    return pl.pallas_call(
        functools.partial(send_kernel, blocks),
        out_shape=tuple(o[0] for o in outs),
        grid_spec=pltpu.PrefetchScalarGridSpec(
            num_scalar_prefetch=3,
            grid=(8,),
            in_specs=[
                pl.BlockSpec((1, 2, 256, 256 * blocks), lambda i, t, r, o: (t[i], 0, 0, 0)),
                pl.BlockSpec((1, 1, 256, 768), lambda i, t, r, o: (r[i], t[i], 0, 0)),
            ],
            out_specs=tuple(o[1] for o in outs),
        ),
        cost_estimate=pl.CostEstimate(flops=800_000_000 * blocks, bytes_accessed=6_000_000 * blocks, transcendentals=0),
        interpret=interpret,
        name="spectra",
    )(jnp.asarray(SEND_TILE, jnp.int32), jnp.asarray(SEND_ROUND, jnp.int32), offs, x, mats)


def normalized(p, q, sign):
    real = p[0] * q[0] + p[1] * q[1]
    imag = p[1] * q[0] - p[0] * q[1]
    scale = lax.rsqrt(jnp.maximum(real * real + imag * imag, FLOOR * FLOOR)) * sign
    return (real * scale, imag * scale)


def to_lanes(block_of, part):
    lane = lax.broadcasted_iota(jnp.int32, (A, 128), 1)
    out = jnp.zeros((A, 128), F32)
    for z in range(Z):
        block = block_of(z, slice(part * A, (part + 1) * A))
        if z:
            block = pltpu.roll(block, z, 1)
        out = jnp.where(lane == z, block, out)
    return out


def edge_fix(own_of, far_of, r_ref, ef_ref, er_ref, flip_ref, sign):
    high = lax.Precision.HIGHEST

    def edge(block_of):
        packed = jnp.concatenate([to_lanes(block_of, part) for part in range(2)], axis=1)
        here = jnp.dot(packed, ef_ref[...], precision=high, preferred_element_type=F32)
        turned = jnp.dot(packed, er_ref[...], precision=high, preferred_element_type=F32)
        there = jnp.dot(flip_ref[...], turned, precision=high, preferred_element_type=F32)
        hr, hi = here[:, :128], here[:, 128:]
        tr, ti = there[:, :128], there[:, 128:]
        return ((hr + tr) * 0.5, (hi - ti) * 0.5), ((hi + ti) * 0.5, (tr - hr) * 0.5)

    own_zero, own_last = edge(own_of)
    far_zero, far_last = edge(far_of)
    zero = normalized(own_zero, far_zero, sign)
    last = normalized(own_last, far_last, sign)
    both = jnp.concatenate((zero[0] - last[1], zero[1] + last[0]), axis=1)
    field = jnp.dot(both, er_ref[...], precision=high, preferred_element_type=F32)
    lane = lax.broadcasted_iota(jnp.int32, (A, 128), 1)
    for part in range(2):
        source = field[:, part * 128 : (part + 1) * 128]
        for z in range(Z):
            moved = pltpu.roll(source, 128 - z, 1) if z else source
            place = (slice(part * A, (part + 1) * A), slice(z * 128, (z + 1) * 128))
            r_ref[place] = jnp.where(lane == 0, moved, r_ref[place])


def pair_core(offset, y_ref, far_ref, a_ref, own_ref, r_ref, valid):
    for half in range(2):
        own_ref[:, half * 512 : (half + 1) * 512] = across(y_ref, half * 4, 4, offset, a_ref[...])

    def own_of(z, rows):
        return own_ref[rows, z * 128 : (z + 1) * 128]

    def far_of(z, rows):
        return far_ref[z // 2, 0, z % 2, 0, rows, :]

    def chunk(i, _):
        up = pl.ds(pl.multiple_of(i * 8, 8), 8)
        down = pl.ds(pl.multiple_of(i * 8 + A, 8), 8)
        own = dft8([(own_of(z, up), own_of(z, down)) for z in range(Z)], -1.0)
        far = dft8([(far_of(z, up), far_of(z, down)) for z in range(Z)], -1.0)
        back = dft8([normalized(own[u], far[u], valid) for u in range(Z)], 1.0)
        for z in range(Z):
            r_ref[up, z * 128 : (z + 1) * 128] = back[z][0]
            r_ref[down, z * 128 : (z + 1) * 128] = back[z][1]
        return 0

    lax.fori_loop(0, A // 8, chunk, 0)
    return own_of, far_of


def parts(ab_ref, r_ref, v_ref):
    for half in range(2):
        q = dot3_right(ab_ref[...], r_ref[:, half * 512 : (half + 1) * 512])
        for k in range(0, 4, 2):
            rows = [
                jnp.concatenate((q[:A, j * 128 : (j + 1) * 128], q[A:, j * 128 : (j + 1) * 128]), axis=1)
                for j in (k, k + 1)
            ]
            yield half * 4 + k, dot3_left(jnp.concatenate(rows, axis=0), v_ref[...])


def large_pair_kernel(
    ints_ref, y_ref, far_ref, a_ref, ab_ref, v1_ref, v0_ref, ef_ref, er_ref, flip_ref, *refs
):
    odd_ref, fours_ref, own_ref, r_ref = refs[-4:]
    step = pl.program_id(0)
    valid = ints_ref[1].astype(F32)
    own_of, far_of = pair_core(ints_ref[0], y_ref, far_ref, a_ref, own_ref, r_ref, valid)

    @pl.when(step == 0)
    def _():
        for z, part in parts(ab_ref, r_ref, v1_ref.at[0]):
            odd_ref[0, z : z + 2] = part.reshape(2, A, 512)

    @pl.when(step == 1)
    def _():
        for z, part in parts(ab_ref, r_ref, v1_ref.at[0]):
            odd_ref[0, z : z + 2] += part.reshape(2, A, 512)

    @pl.when(step == 2)
    def _():
        edge_fix(own_of, far_of, r_ref, ef_ref, er_ref, flip_ref, valid)
        for z, part in parts(ab_ref, r_ref, v0_ref):
            fours_ref[0, z : z + 2] = part.reshape(2, A, 256)


def small_pair_kernel(
    own_off_ref, valid_ref, y_ref, far_ref, a_ref, ab_ref, v2_ref, odd_ref, fours_ref,
    surf_ref, peak_ref, own_ref, r_ref,
):
    rnd = pl.program_id(0)
    valid = valid_ref[rnd].astype(F32)
    pair_core(own_off_ref[rnd], y_ref, far_ref, a_ref.at[0], own_ref, r_ref, valid)
    for z, part in parts(ab_ref, r_ref, v2_ref):
        first = fours_ref[0, z : z + 2].reshape(2 * A, 256)
        odd = odd_ref[0, z : z + 2].reshape(2 * A, 512)
        y = jnp.concatenate((first + part, first - part), axis=1)
        x = jnp.concatenate((y + odd, y - odd), axis=1)
        x = jnp.maximum(x[:A], x[A:])
        if z == 0:
            surf_ref[0, 0] = x
        else:
            surf_ref[0, 0] = jnp.maximum(surf_ref[0, 0], x)
    peak_ref[0] = jnp.broadcast_to(jnp.max(surf_ref[0, 0]), (8, 128))


SCRATCH = [pltpu.VMEM((256, Z * 128), F32), pltpu.VMEM((256, Z * 128), F32)]


def large_pair(rnd, ints, y, far, mat, ab, back1, back0, edges, before, interpret=False):
    args = [y, far, mat, ab, back1, back0, *edges]
    in_specs = [
        pl.BlockSpec((Z, 256, 256), lambda w, *_: (0, 0, w)),
        pl.BlockSpec((4, 1, 2, 1, 256, 128), lambda w, *_: (0, 0, 0, w, 0, 0)),
        whole((256, 768)),
        whole((256, 768)),
        pl.BlockSpec((1, 768, 512), lambda w, *_: (jnp.minimum(w, 1), 0, 0)),
        whole((768, 256)),
        whole((256, 256)),
        whole((256, 256)),
        whole((128, 128)),
    ]
    aliases = {}
    if before is not None:
        aliases = {len(args) + 1: 0, len(args) + 2: 1}
        args += list(before)
        in_specs += [pl.BlockSpec(memory_space=pl.ANY)] * 2
    return pl.pallas_call(
        large_pair_kernel,
        out_shape=(
            jax.ShapeDtypeStruct((ROUNDS, Z, A, 512), F32),
            jax.ShapeDtypeStruct((ROUNDS, Z, A, 256), F32),
        ),
        grid_spec=pltpu.PrefetchScalarGridSpec(
            num_scalar_prefetch=1,
            grid=(3,),
            in_specs=in_specs,
            out_specs=(
                pl.BlockSpec((1, Z, A, 512), lambda w, *_: (rnd, 0, 0, 0)),
                pl.BlockSpec((1, Z, A, 256), lambda w, *_: (rnd, 0, 0, 0)),
            ),
            scratch_shapes=SCRATCH,
        ),
        input_output_aliases=aliases,
        cost_estimate=pl.CostEstimate(flops=6_000_000_000, bytes_accessed=16_000_000, transcendentals=500_000),
        interpret=interpret,
    )(ints, *args)


def small_pair(own, valid, y, far, mats, ab, back2, odd, fours, interpret=False):
    return pl.pallas_call(
        small_pair_kernel,
        out_shape=(
            jax.ShapeDtypeStruct((ROUNDS, 1, A, L), F32),
            jax.ShapeDtypeStruct((ROUNDS, 8, 128), F32),
        ),
        grid_spec=pltpu.PrefetchScalarGridSpec(
            num_scalar_prefetch=2,
            grid=(ROUNDS,),
            in_specs=[
                whole((Z, 256, 256)),
                pl.BlockSpec((4, 1, 2, 1, 256, 128), lambda r, *_: (0, r, 0, 0, 0, 0)),
                pl.BlockSpec((1, 256, 768), lambda r, *_: (r, 0, 0)),
                whole((256, 768)),
                whole((768, 256)),
                pl.BlockSpec((1, Z, A, 512), lambda r, *_: (r, 0, 0, 0)),
                pl.BlockSpec((1, Z, A, 256), lambda r, *_: (r, 0, 0, 0)),
            ],
            out_specs=(
                pl.BlockSpec((1, 1, A, L), lambda r, *_: (r, 0, 0, 0)),
                pl.BlockSpec((1, 8, 128), lambda r, *_: (r, 0, 0)),
            ),
            scratch_shapes=SCRATCH,
        ),
        cost_estimate=pl.CostEstimate(flops=4_000_000_000, bytes_accessed=16_000_000, transcendentals=500_000),
        interpret=interpret,
        name="small_pairs",
    )(own, valid, y, far, mats, ab, back2, odd, fours)


def from_next(x, step, groups):
    return lax.ppermute(x, "tile", [(g + step, g) for g in range(groups - step)])


def after(*values):
    return lax.optimization_barrier(values)


def register(stored, offsets):
    size = lax.axis_size(("tile", "slab"))
    groups = lax.axis_size("tile")
    slabs = lax.axis_size("slab")
    place = lax.axis_index(("tile", "slab"))

    def gather(x):
        return lax.all_to_all(x, "slab", split_axis=0, concat_axis=1, tiled=True)[0]

    def collect(x):
        return lax.all_to_all(x, "slab", split_axis=0, concat_axis=0, tiled=True)

    small_src = along(small_kernel, stored, (twos_table(),), 256)
    small_all = gather(small_src)
    mine = offsets[:, 1, 0]
    turns = [mine] + [lax.ppermute(mine, "slab", [((i + k) % slabs, i) for i in range(slabs)]) for k in range(1, slabs)]
    large_src = along(large_kernel, stored, (odd_table(), fours_table()), 768)
    base = lax.optimization_barrier(across_base())
    given = jnp.roll(jnp.stack(turns, axis=1), lax.axis_index("slab"), axis=1)
    mats = jnp.stack(
        [jnp.stack([across_forward(given[r, j], base) for j in range(slabs)]) for r in range(ROUNDS)]
    )
    small_all, band_src = after(small_all, large_src)
    large_all = gather(band_src)

    def shifted(made):
        near, far, keep = made
        near = from_next(near, 1, groups)
        far = from_next(far, 2, groups)
        return jnp.concatenate((keep, near[:1])), jnp.concatenate((near[1:], far))

    large_made = spectra(large_src, given, mats)
    large_zero, large_one = [x[:, None] for x in shifted(large_made)]
    small_made = spectra(small_src, given, mats)
    small_sent = jnp.stack(shifted(small_made), axis=1)
    valid = (
        jnp.logical_and(place % GC != GC - 1, place + 1 < size),
        place + GC < size,
    )
    SEEDS.append(small_made[0])
    own = [offsets[r, 0, 0] for r in range(ROUNDS)]
    ints = [jnp.stack((own[r], valid[r].astype(jnp.int32))) for r in range(ROUNDS)]
    own_mats = [across_forward(o, base) for o in own]
    ab = across_back()
    edges = edge_tables()
    back1, back0, back2 = odd_back(), fours_back(), twos_back()
    SEEDS.clear()
    large_all, large_zero = after(large_all, large_zero)
    far_zero = collect(large_zero)
    far_zero, large_one = after(far_zero, large_one)
    far_one = collect(large_one)
    first = large_pair(0, ints[0], large_all, far_zero, own_mats[0], ab, back1, back0, edges, None)
    far_one, first, small_sent = after(far_one, first, small_sent)
    small_far = collect(small_sent)
    odd, fours = large_pair(1, ints[1], large_all, far_one, own_mats[1], ab, back1, back0, edges, first)
    surface, peak = small_pair(
        jnp.stack(own),
        jnp.stack([v.astype(jnp.int32) for v in valid]),
        small_all,
        small_far,
        jnp.stack(own_mats),
        ab,
        back2,
        odd,
        fours,
    )
    return surface, peak[:, 0, :1]


def solution(mesh):
    return jax.shard_map(
        register,
        mesh=mesh,
        in_specs=(P("tile", "slab", None, None), P(None, None, ("tile", "slab"))),
        out_specs=(P(None, ("tile", "slab"), None, None), P(None, ("tile", "slab"))),
        check_vma=False,
    )
```

```python
import functools
import math

import jax
import jax.numpy as jnp
from jax import lax
from jax.experimental import pallas as pl
from jax.experimental.pallas import tpu as pltpu
from jax.sharding import PartitionSpec as P


GC = 7
ROUNDS = 2
A = 128
L = 1024
Z = 8
FLOOR = 0.25
BF = jnp.bfloat16
F32 = jnp.float32
HALF = math.sqrt(0.5)


def split(x):
    hi = x.astype(BF)
    lo = (x - hi.astype(F32)).astype(BF)
    return hi, lo


def split_table(x):
    hi = lax.reduce_precision(x, exponent_bits=8, mantissa_bits=7)
    return hi.astype(BF), (x - hi).astype(BF)


def three_rows(x):
    hi, lo = split_table(x)
    return jnp.concatenate((hi, hi, lo), axis=0)


def three_cols(x):
    hi, lo = split_table(x)
    return jnp.concatenate((hi, hi, lo), axis=1)


def trig(index, total):
    angle = (index % total).astype(F32) * (2.0 * math.pi / total)
    return jnp.cos(angle), jnp.sin(angle)


SEEDS = []


def iota(length):
    return lax.optimization_barrier((jnp.arange(length, dtype=jnp.int32), *SEEDS))[0]


def odd_table():
    rows = iota(512)[:, None]
    m = iota(256)[None, :]
    c, s = trig(rows * (2 * m + 1), L)
    scale = 1.0 / L
    return three_rows(
        scale * jnp.concatenate((c[:, :128], -s[:, :128], c[:, 128:], -s[:, 128:]), axis=1)
    )


def fours_table():
    n = iota(256)[:, None]
    m = iota(A)[None, :]
    c, s = trig(n * (4 * m), L)
    last = (1 - 2 * (n % 2)).astype(F32)
    return three_rows((1.0 / L) * jnp.concatenate((c, jnp.where(m == 0, last, -s)), axis=1))


def twos_table():
    n = iota(256)[:, None]
    m = iota(A)[None, :]
    c, s = trig(n * (4 * m + 2), L)
    return three_rows((1.0 / L) * jnp.concatenate((c, -s), axis=1))


def odd_back():
    cols = iota(512)[None, :]
    m = iota(256)[:, None]
    c, s = trig(cols * (2 * m + 1), L)
    scale = 2.0 / L
    return jnp.stack(
        [three_rows(scale * jnp.concatenate((c[b : b + A], -s[b : b + A]), axis=0)) for b in (0, A)]
    )


def fours_back():
    cols = iota(256)[None, :]
    m = iota(A)[:, None]
    c, s = trig(cols * (4 * m), L)
    last = (1 - 2 * (cols % 2)).astype(F32)
    scale = 2.0 / L
    real = jnp.where(m == 0, 0.5 * scale, scale * c)
    imag = jnp.where(m == 0, 0.5 * scale * last, -scale * s)
    return three_rows(jnp.concatenate((real, imag), axis=0))


def twos_back():
    cols = iota(256)[None, :]
    m = iota(A)[:, None]
    c, s = trig(cols * (4 * m + 2), L)
    return three_rows((2.0 / L) * jnp.concatenate((c, -s), axis=0))


def across_base():
    v = iota(A)
    return trig(v[:, None] * v[None, :], A)


def across_forward(offset, base):
    c0, s0 = base
    cv, sv = trig(offset * iota(A)[:, None], A)
    c = c0 * cv + s0 * sv
    s = s0 * cv - c0 * sv
    top = jnp.concatenate((c, s), axis=1)
    low = jnp.concatenate((-s, c), axis=1)
    return three_cols(jnp.concatenate((top, low), axis=0))


def across_back():
    v = iota(A)[None, :]
    a = iota(A)[:, None]
    c, s = trig(a * v, A)
    top = jnp.concatenate((c, -s), axis=1)
    low = jnp.concatenate((s, c), axis=1)
    return three_cols(jnp.concatenate((top, low), axis=0))


def edge_tables():
    lane = iota(A)
    i = lane[:, None]
    j = lane[None, :]
    inside = jnp.logical_and(i < Z, j < Z)
    c, s = trig(i * j, Z)
    c = jnp.where(inside, c, 0.0)
    s = jnp.where(inside, s, 0.0)
    fwd = jnp.concatenate(
        (jnp.concatenate((c, -s), axis=1), jnp.concatenate((s, c), axis=1)), axis=0
    )
    rev = jnp.concatenate(
        (jnp.concatenate((c, s), axis=1), jnp.concatenate((-s, c), axis=1)), axis=0
    )
    flip = ((i + j) % A == 0).astype(F32)
    return fwd, rev, flip


def dot3_left(x, table):
    hi, lo = split(x)
    return jnp.dot(jnp.concatenate((hi, lo, hi), axis=1), table, preferred_element_type=F32)


def dot3_right(table, x):
    hi, lo = split(x)
    return jnp.dot(table, jnp.concatenate((hi, lo, hi), axis=0), preferred_element_type=F32)


def whole(shape):
    return pl.BlockSpec(shape, lambda *_: (0,) * len(shape))


def times_i(x, sign):
    return (-sign * x[1], sign * x[0])


def cadd(x, y):
    return (x[0] + y[0], x[1] + y[1])


def csub(x, y):
    return (x[0] - y[0], x[1] - y[1])


def eighth(x, sign):
    return ((x[0] - sign * x[1]) * HALF, (x[1] + sign * x[0]) * HALF)


def dft4(x, sign):
    a = cadd(x[0], x[2])
    b = csub(x[0], x[2])
    c = cadd(x[1], x[3])
    d = times_i(csub(x[1], x[3]), sign)
    return [cadd(a, c), cadd(b, d), csub(a, c), csub(b, d)]


def dft8(x, sign):
    even = dft4([x[0], x[2], x[4], x[6]], sign)
    odd = dft4([x[1], x[3], x[5], x[7]], sign)
    odd = [odd[0], eighth(odd[1], sign), times_i(odd[2], sign), times_i(eighth(odd[3], sign), sign)]
    return [cadd(even[k], odd[k]) for k in range(4)] + [csub(even[k], odd[k]) for k in range(4)]


def large_kernel(x_ref, w1_ref, w0_ref, out_ref):
    x = x_ref[0].reshape(512, L)
    out_ref[0, :, :, :512] = dot3_left(x[:, :512] - x[:, 512:], w1_ref[...]).reshape(2, 256, 512)
    y = x[:, :512] + x[:, 512:]
    out_ref[0, :, :, 512:] = dot3_left(y[:, :256] + y[:, 256:], w0_ref[...]).reshape(2, 256, 256)


def small_kernel(x_ref, w2_ref, out_ref):
    x = x_ref[0].reshape(512, L)
    y = x[:, :512] + x[:, 512:]
    out_ref[0] = dot3_left(y[:, :256] - y[:, 256:], w2_ref[...]).reshape(2, 256, 256)


def along(kernel, stored, tables, columns, interpret=False):
    tiles, planes = stored.shape[:2]
    return pl.pallas_call(
        kernel,
        out_shape=jax.ShapeDtypeStruct((tiles, planes, 256, columns), F32),
        grid_spec=pl.GridSpec(
            grid=(tiles,),
            in_specs=[pl.BlockSpec((1, planes, 256, L), lambda i: (i, 0, 0, 0))]
            + [whole(t.shape) for t in tables],
            out_specs=pl.BlockSpec((1, planes, 256, columns), lambda i: (i, 0, 0, 0)),
        ),
        cost_estimate=pl.CostEstimate(flops=6_000_000 * columns, bytes_accessed=14_000_000, transcendentals=0),
        interpret=interpret,
    )(stored, *tables)


def across(y_ref, first, count, offset, table):
    later = lax.broadcasted_iota(jnp.int32, (A, 256), 0) >= offset
    picked = [jnp.where(later, y_ref[first + k, :A, :], y_ref[first + k, A:, :]) for k in range(count)]
    real = jnp.concatenate([p[:, :128] for p in picked], axis=1)
    imag = jnp.concatenate([p[:, 128:] for p in picked], axis=1)
    return dot3_right(table, jnp.concatenate((real, imag), axis=0))


def send_kernel(count, steps, src_ref, round_ref, tile_ref, off_ref, *refs):
    x_refs, a_ref, outs = refs[:count], refs[count], refs[count + 1 :]
    i = pl.program_id(0)
    later = lax.broadcasted_iota(jnp.int32, (A, 256), 0) >= off_ref[round_ref[i], tile_ref[i]]
    first = 0
    for x_ref in x_refs:
        blocks = x_ref.shape[3] // 256
        picked = [
            jnp.where(later, x_ref[0, p, :A, w * 256 : (w + 1) * 256], x_ref[0, p, A:, w * 256 : (w + 1) * 256])
            for p in range(2)
            for w in range(blocks)
        ]
        real = jnp.concatenate([p[:, :128] for p in picked], axis=1)
        imag = jnp.concatenate([p[:, 128:] for p in picked], axis=1)
        spec = dot3_right(a_ref[0, 0], jnp.concatenate((real, imag), axis=0))
        for step in range(steps):
            @pl.when(i == step)
            def _(step=step, first=first, spec=spec, blocks=blocks):
                for k in range(2 * blocks):
                    outs[step][k // blocks, first + k % blocks] = spec[:, k * 128 : (k + 1) * 128]

        first += blocks


def spectra(xs, sources, rounds, tiles, offs, mats, interpret=False):
    steps = len(sources)
    blocks = sum(x.shape[3] for x in xs) // 256
    shape = (2, blocks, 256, 128)

    def array(values):
        return jnp.stack([jnp.asarray(v, jnp.int32) for v in values])

    return pl.pallas_call(
        functools.partial(send_kernel, len(xs), steps),
        out_shape=(jax.ShapeDtypeStruct(shape, F32),) * steps,
        grid_spec=pltpu.PrefetchScalarGridSpec(
            num_scalar_prefetch=4,
            grid=(steps,),
            in_specs=[
                pl.BlockSpec((1, 2, 256, x.shape[3]), lambda i, s, r, t, o: (s[i], 0, 0, 0)) for x in xs
            ]
            + [pl.BlockSpec((1, 1, 256, 768), lambda i, s, r, t, o: (r[i], t[i], 0, 0))],
            out_specs=(whole(shape),) * steps,
        ),
        cost_estimate=pl.CostEstimate(
            flops=100_000_000 * blocks * steps, bytes_accessed=800_000 * blocks * steps, transcendentals=0
        ),
        interpret=interpret,
    )(array(sources), array(rounds), array(tiles), offs, *xs, mats)


def normalized(p, q, sign):
    real = p[0] * q[0] + p[1] * q[1]
    imag = p[1] * q[0] - p[0] * q[1]
    scale = lax.rsqrt(jnp.maximum(real * real + imag * imag, FLOOR * FLOOR)) * sign
    return (real * scale, imag * scale)


def to_lanes(block_of, part):
    lane = lax.broadcasted_iota(jnp.int32, (A, 128), 1)
    out = jnp.zeros((A, 128), F32)
    for z in range(Z):
        block = block_of(z, slice(part * A, (part + 1) * A))
        if z:
            block = pltpu.roll(block, z, 1)
        out = jnp.where(lane == z, block, out)
    return out


def edge_fix(own_of, far_of, r_ref, ef_ref, er_ref, flip_ref, sign):
    high = lax.Precision.HIGHEST

    def edge(block_of):
        packed = jnp.concatenate([to_lanes(block_of, part) for part in range(2)], axis=1)
        here = jnp.dot(packed, ef_ref[...], precision=high, preferred_element_type=F32)
        turned = jnp.dot(packed, er_ref[...], precision=high, preferred_element_type=F32)
        there = jnp.dot(flip_ref[...], turned, precision=high, preferred_element_type=F32)
        hr, hi = here[:, :128], here[:, 128:]
        tr, ti = there[:, :128], there[:, 128:]
        return ((hr + tr) * 0.5, (hi - ti) * 0.5), ((hi + ti) * 0.5, (tr - hr) * 0.5)

    own_zero, own_last = edge(own_of)
    far_zero, far_last = edge(far_of)
    zero = normalized(own_zero, far_zero, sign)
    last = normalized(own_last, far_last, sign)
    both = jnp.concatenate((zero[0] - last[1], zero[1] + last[0]), axis=1)
    field = jnp.dot(both, er_ref[...], precision=high, preferred_element_type=F32)
    lane = lax.broadcasted_iota(jnp.int32, (A, 128), 1)
    for part in range(2):
        source = field[:, part * 128 : (part + 1) * 128]
        for z in range(Z):
            moved = pltpu.roll(source, 128 - z, 1) if z else source
            place = (slice(part * A, (part + 1) * A), slice(z * 128, (z + 1) * 128))
            r_ref[place] = jnp.where(lane == 0, moved, r_ref[place])


def pair_core(offset, slab, y_ref, far_refs, a_ref, own_ref, r_ref, far_scr, valid):
    for turn in range(4):
        target = lax.rem(slab + turn, 4)
        far_scr[pl.ds(target, 1)] = far_refs[turn][:, 0][None]
    for half in range(2):
        own_ref[:, half * 512 : (half + 1) * 512] = across(y_ref, half * 4, 4, offset, a_ref[...])

    def own_of(z, rows):
        return own_ref[rows, z * 128 : (z + 1) * 128]

    def far_of(z, rows):
        return far_scr[z // 2, z % 2, rows, :]

    def chunk(i, _):
        up = pl.ds(pl.multiple_of(i * 8, 8), 8)
        down = pl.ds(pl.multiple_of(i * 8 + A, 8), 8)
        own = dft8([(own_of(z, up), own_of(z, down)) for z in range(Z)], -1.0)
        far = dft8([(far_of(z, up), far_of(z, down)) for z in range(Z)], -1.0)
        back = dft8([normalized(own[u], far[u], valid) for u in range(Z)], 1.0)
        for z in range(Z):
            r_ref[up, z * 128 : (z + 1) * 128] = back[z][0]
            r_ref[down, z * 128 : (z + 1) * 128] = back[z][1]
        return 0

    lax.fori_loop(0, A // 8, chunk, 0)
    return own_of, far_of


def parts(ab_ref, r_ref, v_ref):
    for half in range(2):
        q = dot3_right(ab_ref[...], r_ref[:, half * 512 : (half + 1) * 512])
        for k in range(0, 4, 2):
            rows = [
                jnp.concatenate((q[:A, j * 128 : (j + 1) * 128], q[A:, j * 128 : (j + 1) * 128]), axis=1)
                for j in (k, k + 1)
            ]
            yield half * 4 + k, dot3_left(jnp.concatenate(rows, axis=0), v_ref[...])


def large_pair_kernel(
    ints_ref, y_ref, f0_ref, f1_ref, f2_ref, f3_ref, a_ref, ab_ref, v1_ref, v0_ref, ef_ref, er_ref, flip_ref, *refs
):
    odd_ref, fours_ref, own_ref, r_ref, far_scr = refs[-5:]
    step = pl.program_id(0)
    valid = ints_ref[1].astype(F32)
    own_of, far_of = pair_core(
        ints_ref[0], ints_ref[2], y_ref, (f0_ref, f1_ref, f2_ref, f3_ref), a_ref, own_ref, r_ref, far_scr, valid
    )

    @pl.when(step == 0)
    def _():
        for z, part in parts(ab_ref, r_ref, v1_ref.at[0]):
            odd_ref[0, z : z + 2] = part.reshape(2, A, 512)

    @pl.when(step == 1)
    def _():
        for z, part in parts(ab_ref, r_ref, v1_ref.at[0]):
            odd_ref[0, z : z + 2] += part.reshape(2, A, 512)

    @pl.when(step == 2)
    def _():
        edge_fix(own_of, far_of, r_ref, ef_ref, er_ref, flip_ref, valid)
        for z, part in parts(ab_ref, r_ref, v0_ref):
            fours_ref[0, z : z + 2] = part.reshape(2, A, 256)


def small_pair_kernel(
    ints_ref, y_ref, f0_ref, f1_ref, f2_ref, f3_ref, a_ref, ab_ref, v2_ref, odd_ref, fours_ref, *refs
):
    surf_ref, peak_ref, own_ref, r_ref, far_scr = refs[-5:]
    valid = ints_ref[1].astype(F32)
    pair_core(
        ints_ref[0], ints_ref[2], y_ref, (f0_ref, f1_ref, f2_ref, f3_ref), a_ref, own_ref, r_ref, far_scr, valid
    )
    for z, part in parts(ab_ref, r_ref, v2_ref):
        first = fours_ref[0, z : z + 2].reshape(2 * A, 256)
        odd = odd_ref[0, z : z + 2].reshape(2 * A, 512)
        y = jnp.concatenate((first + part, first - part), axis=1)
        x = jnp.concatenate((y + odd, y - odd), axis=1)
        x = jnp.maximum(x[:A], x[A:])
        if z == 0:
            surf_ref[0, 0] = x
        else:
            surf_ref[0, 0] = jnp.maximum(surf_ref[0, 0], x)
    peak_ref[0] = jnp.broadcast_to(jnp.max(surf_ref[0, 0]), (8, 128))


SCRATCH = [pltpu.VMEM((256, Z * 128), F32)] * 2 + [pltpu.VMEM((4, 2, 256, 128), F32)]


def large_pair(rnd, ints, y, far, mat, ab, back1, back0, edges, before, interpret=False):
    args = [y, *far, mat, ab, back1, back0, *edges]
    in_specs = [
        pl.BlockSpec((Z, 256, 256), lambda w, *_: (0, 0, w)),
        *[pl.BlockSpec((2, 1, 256, 128), lambda w, *_: (0, w, 0, 0))] * 4,
        whole((256, 768)),
        whole((256, 768)),
        pl.BlockSpec((1, 768, 512), lambda w, *_: (jnp.minimum(w, 1), 0, 0)),
        whole((768, 256)),
        whole((256, 256)),
        whole((256, 256)),
        whole((128, 128)),
    ]
    aliases = {}
    if before is not None:
        aliases = {len(args) + 1: 0, len(args) + 2: 1}
        args += list(before)
        in_specs += [pl.BlockSpec(memory_space=pl.ANY)] * 2
    return pl.pallas_call(
        large_pair_kernel,
        out_shape=(
            jax.ShapeDtypeStruct((ROUNDS, Z, A, 512), F32),
            jax.ShapeDtypeStruct((ROUNDS, Z, A, 256), F32),
        ),
        grid_spec=pltpu.PrefetchScalarGridSpec(
            num_scalar_prefetch=1,
            grid=(3,),
            in_specs=in_specs,
            out_specs=(
                pl.BlockSpec((1, Z, A, 512), lambda w, *_: (rnd, 0, 0, 0)),
                pl.BlockSpec((1, Z, A, 256), lambda w, *_: (rnd, 0, 0, 0)),
            ),
            scratch_shapes=SCRATCH,
        ),
        input_output_aliases=aliases,
        cost_estimate=pl.CostEstimate(flops=6_000_000_000, bytes_accessed=16_000_000, transcendentals=500_000),
        interpret=interpret,
    )(ints, *args)


def small_pair(rnd, ints, y, far, mat, ab, back2, odd, fours, before, interpret=False):
    args = [y, *far, mat, ab, back2, odd, fours]
    in_specs = [
        whole((Z, 256, 256)),
        *[pl.BlockSpec((2, 1, 256, 128), lambda r, *_, last=x.shape[1] - 1: (0, last, 0, 0)) for x in far],
        whole((256, 768)),
        whole((256, 768)),
        whole((768, 256)),
        pl.BlockSpec((1, Z, A, 512), lambda r, *_: (rnd, 0, 0, 0)),
        pl.BlockSpec((1, Z, A, 256), lambda r, *_: (rnd, 0, 0, 0)),
    ]
    aliases = {}
    if before is not None:
        aliases = {len(args) + 1: 0, len(args) + 2: 1}
        args += list(before)
        in_specs += [pl.BlockSpec(memory_space=pl.ANY)] * 2
    return pl.pallas_call(
        small_pair_kernel,
        out_shape=(
            jax.ShapeDtypeStruct((ROUNDS, 1, A, L), F32),
            jax.ShapeDtypeStruct((ROUNDS, 8, 128), F32),
        ),
        grid_spec=pltpu.PrefetchScalarGridSpec(
            num_scalar_prefetch=1,
            grid=(1,),
            in_specs=in_specs,
            out_specs=(
                pl.BlockSpec((1, 1, A, L), lambda r, *_: (rnd, 0, 0, 0)),
                pl.BlockSpec((1, 8, 128), lambda r, *_: (rnd, 0, 0)),
            ),
            scratch_shapes=SCRATCH,
        ),
        input_output_aliases=aliases,
        cost_estimate=pl.CostEstimate(flops=2_000_000_000, bytes_accessed=10_000_000, transcendentals=300_000),
        interpret=interpret,
    )(ints, *args)


def after(*values):
    return lax.optimization_barrier(values)


DIRECT = (0, 1, 3)


def routes(groups, slabs, rnd, tile_of):
    pairs = []
    for g in range(groups):
        for s in range(slabs):
            i = tile_of(s)
            if rnd == 0:
                to, j = g - (i == 0), (i - 1) % slabs
            else:
                to, j = g - (1 if i == slabs - 1 else 2), (i + 1) % slabs
            if to >= 0:
                pairs.append((slabs * g + s, slabs * to + j))
    return pairs


def register(stored, offsets):
    size = lax.axis_size(("tile", "slab"))
    groups = lax.axis_size("tile")
    slabs = lax.axis_size("slab")
    slab = lax.axis_index("slab")
    place = lax.axis_index(("tile", "slab"))

    def gather(x):
        return lax.all_to_all(x, "slab", split_axis=0, concat_axis=1, tiled=True)[0]

    def send(x, rnd, tile_of):
        return lax.ppermute(x, ("tile", "slab"), routes(groups, slabs, rnd, tile_of))

    large_src = along(large_kernel, stored, (odd_table(), fours_table()), 768)
    large_all = gather(large_src)
    mine = offsets[:, 1, 0]
    turns = [mine] + [lax.ppermute(mine, "slab", [((i + k) % slabs, i) for i in range(slabs)]) for k in range(1, slabs)]
    small_src = along(small_kernel, stored, (twos_table(),), 256)
    base = lax.optimization_barrier(across_base())
    given = jnp.roll(jnp.stack(turns, axis=1), slab, axis=1)
    mats = jnp.stack(
        [jnp.stack([across_forward(given[r, j], base) for j in range(slabs)]) for r in range(ROUNDS)]
    )

    def shift_of(rnd, k):
        return 1 - k if rnd == 0 else -1 - k

    plan = [(r, k) for r in range(ROUNDS) for k in DIRECT]
    tiles = [(slab + shift_of(r, k) + slabs) % slabs for r, k in plan]
    made = spectra([large_src, small_src], tiles, [r for r, _ in plan], tiles, given, mats)
    far = [[None] * slabs for _ in range(ROUNDS)]
    for (r, k), x in zip(plan, made, strict=True):
        far[r][k] = send(x, r, lambda s, r=r, k=k: (s + shift_of(r, k)) % slabs)
    SEEDS.append(made[0])
    valid = (
        jnp.logical_and(place % GC != GC - 1, place + 1 < size),
        place + GC < size,
    )
    own = [offsets[r, 0, 0] for r in range(ROUNDS)]
    ints = [jnp.stack((own[r], valid[r].astype(jnp.int32), slab)) for r in range(ROUNDS)]
    own_mats = [across_forward(o, base) for o in own]
    ab = across_back()
    edges = edge_tables()
    back1, back0, back2 = odd_back(), fours_back(), twos_back()
    SEEDS.clear()
    large_all, band_src = after(large_all, small_src)
    small_all = gather(band_src)

    def relayed(x):
        whole_band = x.reshape(slabs, 2, 256, x.shape[2])
        both = spectra(
            [whole_band], [(slab + 1) % slabs, (slab + slabs - 1) % slabs], [0, 1], [slab, slab], given, mats
        )
        return [send(both[r], r, lambda s: s) for r in range(ROUNDS)]

    large_two = relayed(large_all)
    small_two = relayed(small_all)

    def around(r, two):
        return [far[r][0], far[r][1], two[r], far[r][3]]

    sums = None
    for r in range(ROUNDS):
        sums = large_pair(r, ints[r], large_all, around(r, large_two), own_mats[r], ab, back1, back0, edges, sums)
    out = None
    for r in range(ROUNDS):
        out = small_pair(r, ints[r], small_all, around(r, small_two), own_mats[r], ab, back2, *sums, out)
    surface, peak = out
    return surface, peak[:, 0, :1]


def solution(mesh):
    return jax.shard_map(
        register,
        mesh=mesh,
        in_specs=(P("tile", "slab", None, None), P(None, None, ("tile", "slab"))),
        out_specs=(P(None, ("tile", "slab"), None, None), P(None, ("tile", "slab"))),
        check_vma=False,
    )
```

```python
import functools
import math

import jax
import jax.numpy as jnp
from jax import lax
from jax.experimental import pallas as pl
from jax.experimental.pallas import tpu as pltpu
from jax.sharding import PartitionSpec as P


GC = 7
ROUNDS = 2
A = 128
L = 1024
Z = 8
FLOOR = 0.25
BF = jnp.bfloat16
F32 = jnp.float32
HALF = math.sqrt(0.5)


def split(x):
    hi = x.astype(BF)
    lo = (x - hi.astype(F32)).astype(BF)
    return hi, lo


def split_table(x):
    hi = lax.reduce_precision(x, exponent_bits=8, mantissa_bits=7)
    return hi.astype(BF), (x - hi).astype(BF)


def three_rows(x):
    hi, lo = split_table(x)
    return jnp.concatenate((hi, hi, lo), axis=0)


def three_cols(x):
    hi, lo = split_table(x)
    return jnp.concatenate((hi, hi, lo), axis=1)


def trig(index, total):
    angle = (index % total).astype(F32) * (2.0 * math.pi / total)
    return jnp.cos(angle), jnp.sin(angle)


SEEDS = []


def iota(length):
    return lax.optimization_barrier((jnp.arange(length, dtype=jnp.int32), *SEEDS))[0]


def odd_table():
    rows = iota(512)[:, None]
    m = iota(256)[None, :]
    c, s = trig(rows * (2 * m + 1), L)
    scale = 1.0 / L
    return three_rows(
        scale * jnp.concatenate((c[:, :128], -s[:, :128], c[:, 128:], -s[:, 128:]), axis=1)
    )


def fours_table():
    n = iota(256)[:, None]
    m = iota(A)[None, :]
    c, s = trig(n * (4 * m), L)
    last = (1 - 2 * (n % 2)).astype(F32)
    return three_rows((1.0 / L) * jnp.concatenate((c, jnp.where(m == 0, last, -s)), axis=1))


def twos_table():
    n = iota(256)[:, None]
    m = iota(A)[None, :]
    c, s = trig(n * (4 * m + 2), L)
    return three_rows((1.0 / L) * jnp.concatenate((c, -s), axis=1))


def odd_back():
    cols = iota(512)[None, :]
    m = iota(256)[:, None]
    c, s = trig(cols * (2 * m + 1), L)
    scale = 2.0 / L
    return jnp.stack(
        [three_rows(scale * jnp.concatenate((c[b : b + A], -s[b : b + A]), axis=0)) for b in (0, A)]
    )


def fours_back():
    cols = iota(256)[None, :]
    m = iota(A)[:, None]
    c, s = trig(cols * (4 * m), L)
    last = (1 - 2 * (cols % 2)).astype(F32)
    scale = 2.0 / L
    real = jnp.where(m == 0, 0.5 * scale, scale * c)
    imag = jnp.where(m == 0, 0.5 * scale * last, -scale * s)
    return three_rows(jnp.concatenate((real, imag), axis=0))


def twos_back():
    cols = iota(256)[None, :]
    m = iota(A)[:, None]
    c, s = trig(cols * (4 * m + 2), L)
    return three_rows((2.0 / L) * jnp.concatenate((c, -s), axis=0))


def across_base():
    v = iota(A)
    return trig(v[:, None] * v[None, :], A)


def across_forward(offset, base):
    c0, s0 = base
    cv, sv = trig(offset * iota(A)[:, None], A)
    c = c0 * cv + s0 * sv
    s = s0 * cv - c0 * sv
    top = jnp.concatenate((c, s), axis=1)
    low = jnp.concatenate((-s, c), axis=1)
    return three_cols(jnp.concatenate((top, low), axis=0))


def across_back():
    v = iota(A)[None, :]
    a = iota(A)[:, None]
    c, s = trig(a * v, A)
    top = jnp.concatenate((c, -s), axis=1)
    low = jnp.concatenate((s, c), axis=1)
    return three_cols(jnp.concatenate((top, low), axis=0))


def edge_tables():
    lane = iota(A)
    i = lane[:, None]
    j = lane[None, :]
    inside = jnp.logical_and(i < Z, j < Z)
    c, s = trig(i * j, Z)
    c = jnp.where(inside, c, 0.0)
    s = jnp.where(inside, s, 0.0)
    fwd = jnp.concatenate(
        (jnp.concatenate((c, -s), axis=1), jnp.concatenate((s, c), axis=1)), axis=0
    )
    rev = jnp.concatenate(
        (jnp.concatenate((c, s), axis=1), jnp.concatenate((-s, c), axis=1)), axis=0
    )
    flip = ((i + j) % A == 0).astype(F32)
    return fwd, rev, flip


def dot3_left(x, table):
    hi, lo = split(x)
    return jnp.dot(jnp.concatenate((hi, lo, hi), axis=1), table, preferred_element_type=F32)


def dot3_right(table, x):
    hi, lo = split(x)
    return jnp.dot(table, jnp.concatenate((hi, lo, hi), axis=0), preferred_element_type=F32)


def whole(shape):
    return pl.BlockSpec(shape, lambda *_: (0,) * len(shape))


def times_i(x, sign):
    return (-sign * x[1], sign * x[0])


def cadd(x, y):
    return (x[0] + y[0], x[1] + y[1])


def csub(x, y):
    return (x[0] - y[0], x[1] - y[1])


def eighth(x, sign):
    return ((x[0] - sign * x[1]) * HALF, (x[1] + sign * x[0]) * HALF)


def dft4(x, sign):
    a = cadd(x[0], x[2])
    b = csub(x[0], x[2])
    c = cadd(x[1], x[3])
    d = times_i(csub(x[1], x[3]), sign)
    return [cadd(a, c), cadd(b, d), csub(a, c), csub(b, d)]


def dft8(x, sign):
    even = dft4([x[0], x[2], x[4], x[6]], sign)
    odd = dft4([x[1], x[3], x[5], x[7]], sign)
    odd = [odd[0], eighth(odd[1], sign), times_i(odd[2], sign), times_i(eighth(odd[3], sign), sign)]
    return [cadd(even[k], odd[k]) for k in range(4)] + [csub(even[k], odd[k]) for k in range(4)]


def large_kernel(x_ref, w1_ref, w0_ref, out_ref):
    x = x_ref[0].reshape(512, L)
    out_ref[0, :, :, :512] = dot3_left(x[:, :512] - x[:, 512:], w1_ref[...]).reshape(2, 256, 512)
    y = x[:, :512] + x[:, 512:]
    out_ref[0, :, :, 512:] = dot3_left(y[:, :256] + y[:, 256:], w0_ref[...]).reshape(2, 256, 256)


def small_kernel(x_ref, w2_ref, out_ref):
    x = x_ref[0].reshape(512, L)
    y = x[:, :512] + x[:, 512:]
    out_ref[0] = dot3_left(y[:, :256] - y[:, 256:], w2_ref[...]).reshape(2, 256, 256)


def along(kernel, stored, tables, columns, interpret=False):
    tiles, planes = stored.shape[:2]
    return pl.pallas_call(
        kernel,
        out_shape=jax.ShapeDtypeStruct((tiles, planes, 256, columns), F32),
        grid_spec=pl.GridSpec(
            grid=(tiles,),
            in_specs=[pl.BlockSpec((1, planes, 256, L), lambda i: (i, 0, 0, 0))]
            + [whole(t.shape) for t in tables],
            out_specs=pl.BlockSpec((1, planes, 256, columns), lambda i: (i, 0, 0, 0)),
        ),
        cost_estimate=pl.CostEstimate(flops=6_000_000 * columns, bytes_accessed=14_000_000, transcendentals=0),
        interpret=interpret,
    )(stored, *tables)


def across(y_ref, first, count, offset, table):
    later = lax.broadcasted_iota(jnp.int32, (A, 256), 0) >= offset
    picked = [jnp.where(later, y_ref[first + k, :A, :], y_ref[first + k, A:, :]) for k in range(count)]
    real = jnp.concatenate([p[:, :128] for p in picked], axis=1)
    imag = jnp.concatenate([p[:, 128:] for p in picked], axis=1)
    return dot3_right(table, jnp.concatenate((real, imag), axis=0))


def send_kernel(count, steps, src_ref, round_ref, tile_ref, off_ref, *refs):
    x_refs, a_ref, outs = refs[:count], refs[count], refs[count + 1 :]
    i = pl.program_id(0)
    later = lax.broadcasted_iota(jnp.int32, (A, 256), 0) >= off_ref[round_ref[i], tile_ref[i]]
    first = 0
    for x_ref in x_refs:
        blocks = x_ref.shape[3] // 256
        picked = [
            jnp.where(later, x_ref[0, p, :A, w * 256 : (w + 1) * 256], x_ref[0, p, A:, w * 256 : (w + 1) * 256])
            for p in range(2)
            for w in range(blocks)
        ]
        real = jnp.concatenate([p[:, :128] for p in picked], axis=1)
        imag = jnp.concatenate([p[:, 128:] for p in picked], axis=1)
        spec = dot3_right(a_ref[0, 0], jnp.concatenate((real, imag), axis=0))
        for step in range(steps):
            @pl.when(i == step)
            def _(step=step, first=first, spec=spec, blocks=blocks):
                for k in range(2 * blocks):
                    outs[step][k // blocks, first + k % blocks] = spec[:, k * 128 : (k + 1) * 128]

        first += blocks


def spectra(xs, sources, rounds, tiles, offs, mats, interpret=False):
    steps = len(sources)
    blocks = sum(x.shape[3] for x in xs) // 256
    shape = (2, blocks, 256, 128)

    def array(values):
        return jnp.stack([jnp.asarray(v, jnp.int32) for v in values])

    return pl.pallas_call(
        functools.partial(send_kernel, len(xs), steps),
        out_shape=(jax.ShapeDtypeStruct(shape, F32),) * steps,
        grid_spec=pltpu.PrefetchScalarGridSpec(
            num_scalar_prefetch=4,
            grid=(steps,),
            in_specs=[
                pl.BlockSpec((1, 2, 256, x.shape[3]), lambda i, s, r, t, o: (s[i], 0, 0, 0)) for x in xs
            ]
            + [pl.BlockSpec((1, 1, 256, 768), lambda i, s, r, t, o: (r[i], t[i], 0, 0))],
            out_specs=(whole(shape),) * steps,
        ),
        cost_estimate=pl.CostEstimate(
            flops=100_000_000 * blocks * steps, bytes_accessed=800_000 * blocks * steps, transcendentals=0
        ),
        interpret=interpret,
    )(array(sources), array(rounds), array(tiles), offs, *xs, mats)


def normalized(p, q, sign):
    real = p[0] * q[0] + p[1] * q[1]
    imag = p[1] * q[0] - p[0] * q[1]
    scale = lax.rsqrt(jnp.maximum(real * real + imag * imag, FLOOR * FLOOR)) * sign
    return (real * scale, imag * scale)


def to_lanes(block_of, part):
    lane = lax.broadcasted_iota(jnp.int32, (A, 128), 1)
    out = jnp.zeros((A, 128), F32)
    for z in range(Z):
        block = block_of(z, slice(part * A, (part + 1) * A))
        if z:
            block = pltpu.roll(block, z, 1)
        out = jnp.where(lane == z, block, out)
    return out


def edge_fix(own_of, far_of, r_ref, ef_ref, er_ref, flip_ref, sign):
    high = lax.Precision.HIGHEST

    def edge(block_of):
        packed = jnp.concatenate([to_lanes(block_of, part) for part in range(2)], axis=1)
        here = jnp.dot(packed, ef_ref[...], precision=high, preferred_element_type=F32)
        turned = jnp.dot(packed, er_ref[...], precision=high, preferred_element_type=F32)
        there = jnp.dot(flip_ref[...], turned, precision=high, preferred_element_type=F32)
        hr, hi = here[:, :128], here[:, 128:]
        tr, ti = there[:, :128], there[:, 128:]
        return ((hr + tr) * 0.5, (hi - ti) * 0.5), ((hi + ti) * 0.5, (tr - hr) * 0.5)

    own_zero, own_last = edge(own_of)
    far_zero, far_last = edge(far_of)
    zero = normalized(own_zero, far_zero, sign)
    last = normalized(own_last, far_last, sign)
    both = jnp.concatenate((zero[0] - last[1], zero[1] + last[0]), axis=1)
    field = jnp.dot(both, er_ref[...], precision=high, preferred_element_type=F32)
    lane = lax.broadcasted_iota(jnp.int32, (A, 128), 1)
    for part in range(2):
        source = field[:, part * 128 : (part + 1) * 128]
        for z in range(Z):
            moved = pltpu.roll(source, 128 - z, 1) if z else source
            place = (slice(part * A, (part + 1) * A), slice(z * 128, (z + 1) * 128))
            r_ref[place] = jnp.where(lane == 0, moved, r_ref[place])


def arrange(slab, far_refs, far_scr):
    for turn in range(4):
        target = lax.rem(slab + turn, 4)
        far_scr[pl.ds(target, 1)] = far_refs[turn][:, 0][None]


def pair_core(offset, slab, y_ref, far_refs, a_ref, own_ref, r_ref, far_scr, valid):
    if far_refs is not None:
        arrange(slab, far_refs, far_scr)
    for half in range(2):
        own_ref[:, half * 512 : (half + 1) * 512] = across(y_ref, half * 4, 4, offset, a_ref[...])

    def own_of(z, rows):
        return own_ref[rows, z * 128 : (z + 1) * 128]

    def far_of(z, rows):
        return far_scr[z // 2, z % 2, rows, :]

    def chunk(i, _):
        up = pl.ds(pl.multiple_of(i * 8, 8), 8)
        down = pl.ds(pl.multiple_of(i * 8 + A, 8), 8)
        own = dft8([(own_of(z, up), own_of(z, down)) for z in range(Z)], -1.0)
        far = dft8([(far_of(z, up), far_of(z, down)) for z in range(Z)], -1.0)
        back = dft8([normalized(own[u], far[u], valid) for u in range(Z)], 1.0)
        for z in range(Z):
            r_ref[up, z * 128 : (z + 1) * 128] = back[z][0]
            r_ref[down, z * 128 : (z + 1) * 128] = back[z][1]
        return 0

    lax.fori_loop(0, A // 8, chunk, 0)
    return own_of, far_of


def parts(ab_ref, r_ref, v_ref):
    for half in range(2):
        q = dot3_right(ab_ref[...], r_ref[:, half * 512 : (half + 1) * 512])
        for k in range(0, 4, 2):
            rows = [
                jnp.concatenate((q[:A, j * 128 : (j + 1) * 128], q[A:, j * 128 : (j + 1) * 128]), axis=1)
                for j in (k, k + 1)
            ]
            yield half * 4 + k, dot3_left(jnp.concatenate(rows, axis=0), v_ref[...])


def large_pair_kernel(
    ints_ref, y_ref, f0_ref, f1_ref, f2_ref, f3_ref, a_ref, ab_ref, v1_ref, v0_ref, ef_ref, er_ref, flip_ref, *refs
):
    odd_ref, fours_ref, own_ref, r_ref, far_scr = refs[-5:]
    step = pl.program_id(0)
    valid = ints_ref[1].astype(F32)
    own_of, far_of = pair_core(
        ints_ref[0], ints_ref[2], y_ref, (f0_ref, f1_ref, f2_ref, f3_ref), a_ref, own_ref, r_ref, far_scr, valid
    )

    @pl.when(step == 0)
    def _():
        for z, part in parts(ab_ref, r_ref, v1_ref.at[0]):
            odd_ref[0, z : z + 2] = part.reshape(2, A, 512)

    @pl.when(step == 1)
    def _():
        for z, part in parts(ab_ref, r_ref, v1_ref.at[0]):
            odd_ref[0, z : z + 2] += part.reshape(2, A, 512)

    @pl.when(step == 2)
    def _():
        edge_fix(own_of, far_of, r_ref, ef_ref, er_ref, flip_ref, valid)
        for z, part in parts(ab_ref, r_ref, v0_ref):
            fours_ref[0, z : z + 2] = part.reshape(2, A, 256)


def small_pair_kernel(own_ref_s, valid_ref, slab_ref, y_ref, *refs):
    zero_refs, one_refs = refs[:4], refs[4:8]
    a_ref, ab_ref, v2_ref, odd_ref, fours_ref, surf_ref, peak_ref, own_ref, r_ref, far_scr = refs[8:]
    rnd = pl.program_id(0)
    valid = valid_ref[rnd].astype(F32)

    @pl.when(rnd == 0)
    def _():
        arrange(slab_ref[0], zero_refs, far_scr)

    @pl.when(rnd == 1)
    def _():
        arrange(slab_ref[0], one_refs, far_scr)

    pair_core(own_ref_s[rnd], None, y_ref, None, a_ref.at[0], own_ref, r_ref, far_scr, valid)
    for z, part in parts(ab_ref, r_ref, v2_ref):
        first = fours_ref[0, z : z + 2].reshape(2 * A, 256)
        odd = odd_ref[0, z : z + 2].reshape(2 * A, 512)
        y = jnp.concatenate((first + part, first - part), axis=1)
        x = jnp.concatenate((y + odd, y - odd), axis=1)
        x = jnp.maximum(x[:A], x[A:])
        if z == 0:
            surf_ref[0, 0] = x
        else:
            surf_ref[0, 0] = jnp.maximum(surf_ref[0, 0], x)
    peak_ref[rnd, 0] = jnp.max(surf_ref[0, 0])


SCRATCH = [pltpu.VMEM((256, Z * 128), F32)] * 2 + [pltpu.VMEM((4, 2, 256, 128), F32)]


def large_pair(rnd, ints, y, far, mat, ab, back1, back0, edges, before, interpret=False):
    args = [y, *far, mat, ab, back1, back0, *edges]
    in_specs = [
        pl.BlockSpec((Z, 256, 256), lambda w, *_: (0, 0, w)),
        *[pl.BlockSpec((2, 1, 256, 128), lambda w, *_: (0, w, 0, 0))] * 4,
        whole((256, 768)),
        whole((256, 768)),
        pl.BlockSpec((1, 768, 512), lambda w, *_: (jnp.minimum(w, 1), 0, 0)),
        whole((768, 256)),
        whole((256, 256)),
        whole((256, 256)),
        whole((128, 128)),
    ]
    aliases = {}
    if before is not None:
        aliases = {len(args) + 1: 0, len(args) + 2: 1}
        args += list(before)
        in_specs += [pl.BlockSpec(memory_space=pl.ANY)] * 2
    return pl.pallas_call(
        large_pair_kernel,
        out_shape=(
            jax.ShapeDtypeStruct((ROUNDS, Z, A, 512), F32),
            jax.ShapeDtypeStruct((ROUNDS, Z, A, 256), F32),
        ),
        grid_spec=pltpu.PrefetchScalarGridSpec(
            num_scalar_prefetch=1,
            grid=(3,),
            in_specs=in_specs,
            out_specs=(
                pl.BlockSpec((1, Z, A, 512), lambda w, *_: (rnd, 0, 0, 0)),
                pl.BlockSpec((1, Z, A, 256), lambda w, *_: (rnd, 0, 0, 0)),
            ),
            scratch_shapes=SCRATCH,
        ),
        input_output_aliases=aliases,
        cost_estimate=pl.CostEstimate(flops=6_000_000_000, bytes_accessed=16_000_000, transcendentals=500_000),
        interpret=interpret,
    )(ints, *args)


def small_pair(own, valid, slab, y, far, mats, ab, back2, odd, fours, interpret=False):
    flat = [*far[0], *far[1]]
    return pl.pallas_call(
        small_pair_kernel,
        out_shape=(
            jax.ShapeDtypeStruct((ROUNDS, 1, A, L), F32),
            jax.ShapeDtypeStruct((ROUNDS, 1), F32),
        ),
        grid_spec=pltpu.PrefetchScalarGridSpec(
            num_scalar_prefetch=3,
            grid=(ROUNDS,),
            in_specs=[
                whole((Z, 256, 256)),
                *[pl.BlockSpec((2, 1, 256, 128), lambda r, *_, last=x.shape[1] - 1: (0, last, 0, 0)) for x in flat],
                pl.BlockSpec((1, 256, 768), lambda r, *_: (r, 0, 0)),
                whole((256, 768)),
                whole((768, 256)),
                pl.BlockSpec((1, Z, A, 512), lambda r, *_: (r, 0, 0, 0)),
                pl.BlockSpec((1, Z, A, 256), lambda r, *_: (r, 0, 0, 0)),
            ],
            out_specs=(
                pl.BlockSpec((1, 1, A, L), lambda r, *_: (r, 0, 0, 0)),
                pl.BlockSpec(memory_space=pltpu.SMEM),
            ),
            scratch_shapes=SCRATCH,
        ),
        cost_estimate=pl.CostEstimate(flops=4_000_000_000, bytes_accessed=16_000_000, transcendentals=500_000),
        interpret=interpret,
        name="small_pairs",
    )(own, valid, slab, y, *flat, mats, ab, back2, odd, fours)


def after(*values):
    return lax.optimization_barrier(values)


DIRECT = (0, 1, 3)


def routes(groups, slabs, rnd, tile_of):
    pairs = []
    for g in range(groups):
        for s in range(slabs):
            i = tile_of(s)
            if rnd == 0:
                to, j = g - (i == 0), (i - 1) % slabs
            else:
                to, j = g - (1 if i == slabs - 1 else 2), (i + 1) % slabs
            if to >= 0:
                pairs.append((slabs * g + s, slabs * to + j))
    return pairs


def register(stored, offsets):
    size = lax.axis_size(("tile", "slab"))
    groups = lax.axis_size("tile")
    slabs = lax.axis_size("slab")
    slab = lax.axis_index("slab")
    place = lax.axis_index(("tile", "slab"))

    def gather(x):
        return lax.all_to_all(x, "slab", split_axis=0, concat_axis=1, tiled=True)[0]

    def send(x, rnd, tile_of):
        return lax.ppermute(x, ("tile", "slab"), routes(groups, slabs, rnd, tile_of))

    large_src = along(large_kernel, stored, (odd_table(), fours_table()), 768)
    large_all = gather(large_src)
    mine = offsets[:, 1, 0]
    turns = [mine] + [lax.ppermute(mine, "slab", [((i + k) % slabs, i) for i in range(slabs)]) for k in range(1, slabs)]
    small_src = along(small_kernel, stored, (twos_table(),), 256)
    base = lax.optimization_barrier(across_base())
    given = jnp.roll(jnp.stack(turns, axis=1), slab, axis=1)
    mats = jnp.stack(
        [jnp.stack([across_forward(given[r, j], base) for j in range(slabs)]) for r in range(ROUNDS)]
    )

    def shift_of(rnd, k):
        return 1 - k if rnd == 0 else -1 - k

    far = [[None] * slabs for _ in range(ROUNDS)]
    for r in range(ROUNDS):
        tiles = [(slab + shift_of(r, k) + slabs) % slabs for k in DIRECT]
        made = spectra([large_src, small_src], tiles, [r] * 3, tiles, given, mats)
        for k, x in zip(DIRECT, made, strict=True):
            far[r][k] = send(x, r, lambda s, r=r, k=k: (s + shift_of(r, k)) % slabs)
    SEEDS.append(made[0])
    valid = (
        jnp.logical_and(place % GC != GC - 1, place + 1 < size),
        place + GC < size,
    )
    own = [offsets[r, 0, 0] for r in range(ROUNDS)]
    ints = [jnp.stack((own[r], valid[r].astype(jnp.int32), slab)) for r in range(ROUNDS)]
    own_mats = [across_forward(o, base) for o in own]
    ab = across_back()
    edges = edge_tables()
    back1, back0, back2 = odd_back(), fours_back(), twos_back()
    SEEDS.clear()
    large_all, band_src = after(large_all, small_src)
    small_all = gather(band_src)

    def relayed(x):
        whole_band = x.reshape(slabs, 2, 256, x.shape[2])
        both = spectra(
            [whole_band], [(slab + 1) % slabs, (slab + slabs - 1) % slabs], [0, 1], [slab, slab], given, mats
        )
        return [send(both[r], r, lambda s: s) for r in range(ROUNDS)]

    large_two = relayed(large_all)
    small_two = relayed(small_all)

    def around(r, two):
        return [far[r][0], far[r][1], two[r], far[r][3]]

    sums = None
    for r in range(ROUNDS):
        sums = large_pair(r, ints[r], large_all, around(r, large_two), own_mats[r], ab, back1, back0, edges, sums)
    return small_pair(
        jnp.stack(own),
        jnp.stack([v.astype(jnp.int32) for v in valid]),
        jnp.stack([slab]),
        small_all,
        [around(r, small_two) for r in range(ROUNDS)],
        jnp.stack(own_mats),
        ab,
        back2,
        *sums,
    )


def solution(mesh):
    return jax.shard_map(
        register,
        mesh=mesh,
        in_specs=(P("tile", "slab", None, None), P(None, None, ("tile", "slab"))),
        out_specs=(P(None, ("tile", "slab"), None, None), P(None, ("tile", "slab"))),
        check_vma=False,
    )
```

```python
import functools
import math

import jax
import jax.numpy as jnp
from jax import lax
from jax.experimental import pallas as pl
from jax.experimental.pallas import tpu as pltpu
from jax.sharding import PartitionSpec as P


GC = 7
ROUNDS = 2
A = 128
L = 1024
Z = 8
FLOOR = 0.25
BF = jnp.bfloat16
F32 = jnp.float32
HALF = math.sqrt(0.5)


def split(x):
    hi = x.astype(BF)
    lo = (x - hi.astype(F32)).astype(BF)
    return hi, lo


def split_table(x):
    hi = lax.reduce_precision(x, exponent_bits=8, mantissa_bits=7)
    return hi.astype(BF), (x - hi).astype(BF)


def three_rows(x):
    hi, lo = split_table(x)
    return jnp.concatenate((hi, hi, lo), axis=0)


def three_cols(x):
    hi, lo = split_table(x)
    return jnp.concatenate((hi, hi, lo), axis=1)


def trig(index, total):
    angle = (index % total).astype(F32) * (2.0 * math.pi / total)
    return jnp.cos(angle), jnp.sin(angle)


SEEDS = []


def iota(length):
    return lax.optimization_barrier((jnp.arange(length, dtype=jnp.int32), *SEEDS))[0]


def odd_table():
    rows = iota(512)[:, None]
    m = iota(256)[None, :]
    c, s = trig(rows * (2 * m + 1), L)
    scale = 1.0 / L
    return three_rows(
        scale * jnp.concatenate((c[:, :128], -s[:, :128], c[:, 128:], -s[:, 128:]), axis=1)
    )


def fours_table():
    n = iota(256)[:, None]
    m = iota(A)[None, :]
    c, s = trig(n * (4 * m), L)
    last = (1 - 2 * (n % 2)).astype(F32)
    return three_rows((1.0 / L) * jnp.concatenate((c, jnp.where(m == 0, last, -s)), axis=1))


def twos_table():
    n = iota(256)[:, None]
    m = iota(A)[None, :]
    c, s = trig(n * (4 * m + 2), L)
    return three_rows((1.0 / L) * jnp.concatenate((c, -s), axis=1))


def odd_back():
    cols = iota(512)[None, :]
    m = iota(256)[:, None]
    c, s = trig(cols * (2 * m + 1), L)
    scale = 2.0 / L
    return jnp.stack(
        [three_rows(scale * jnp.concatenate((c[b : b + A], -s[b : b + A]), axis=0)) for b in (0, A)]
    )


def fours_back():
    cols = iota(256)[None, :]
    m = iota(A)[:, None]
    c, s = trig(cols * (4 * m), L)
    last = (1 - 2 * (cols % 2)).astype(F32)
    scale = 2.0 / L
    real = jnp.where(m == 0, 0.5 * scale, scale * c)
    imag = jnp.where(m == 0, 0.5 * scale * last, -scale * s)
    return three_rows(jnp.concatenate((real, imag), axis=0))


def twos_back():
    cols = iota(256)[None, :]
    m = iota(A)[:, None]
    c, s = trig(cols * (4 * m + 2), L)
    return three_rows((2.0 / L) * jnp.concatenate((c, -s), axis=0))


def across_base():
    v = iota(A)
    return trig(v[:, None] * v[None, :], A)


def across_forward(offset, base):
    c0, s0 = base
    cv, sv = trig(offset * iota(A)[:, None], A)
    c = c0 * cv + s0 * sv
    s = s0 * cv - c0 * sv
    top = jnp.concatenate((c, s), axis=1)
    low = jnp.concatenate((-s, c), axis=1)
    return three_cols(jnp.concatenate((top, low), axis=0))


def across_back():
    v = iota(A)[None, :]
    a = iota(A)[:, None]
    c, s = trig(a * v, A)
    top = jnp.concatenate((c, -s), axis=1)
    low = jnp.concatenate((s, c), axis=1)
    return three_cols(jnp.concatenate((top, low), axis=0))


def edge_tables():
    lane = iota(A)
    i = lane[:, None]
    j = lane[None, :]
    inside = jnp.logical_and(i < Z, j < Z)
    c, s = trig(i * j, Z)
    c = jnp.where(inside, c, 0.0)
    s = jnp.where(inside, s, 0.0)
    fwd = jnp.concatenate(
        (jnp.concatenate((c, -s), axis=1), jnp.concatenate((s, c), axis=1)), axis=0
    )
    rev = jnp.concatenate(
        (jnp.concatenate((c, s), axis=1), jnp.concatenate((-s, c), axis=1)), axis=0
    )
    flip = ((i + j) % A == 0).astype(F32)
    return fwd, rev, flip


def dot3_left(x, table):
    hi, lo = split(x)
    return jnp.dot(jnp.concatenate((hi, lo, hi), axis=1), table, preferred_element_type=F32)


def dot3_right(table, x):
    hi, lo = split(x)
    return jnp.dot(table, jnp.concatenate((hi, lo, hi), axis=0), preferred_element_type=F32)


def whole(shape):
    return pl.BlockSpec(shape, lambda *_: (0,) * len(shape))


def times_i(x, sign):
    return (-sign * x[1], sign * x[0])


def cadd(x, y):
    return (x[0] + y[0], x[1] + y[1])


def csub(x, y):
    return (x[0] - y[0], x[1] - y[1])


def eighth(x, sign):
    return ((x[0] - sign * x[1]) * HALF, (x[1] + sign * x[0]) * HALF)


def dft4(x, sign):
    a = cadd(x[0], x[2])
    b = csub(x[0], x[2])
    c = cadd(x[1], x[3])
    d = times_i(csub(x[1], x[3]), sign)
    return [cadd(a, c), cadd(b, d), csub(a, c), csub(b, d)]


def dft8(x, sign):
    even = dft4([x[0], x[2], x[4], x[6]], sign)
    odd = dft4([x[1], x[3], x[5], x[7]], sign)
    odd = [odd[0], eighth(odd[1], sign), times_i(odd[2], sign), times_i(eighth(odd[3], sign), sign)]
    return [cadd(even[k], odd[k]) for k in range(4)] + [csub(even[k], odd[k]) for k in range(4)]


def large_kernel(x_ref, w1_ref, w0_ref, out_ref):
    x = x_ref[0].reshape(512, L)
    out_ref[0, :, :, :512] = dot3_left(x[:, :512] - x[:, 512:], w1_ref[...]).reshape(2, 256, 512)
    y = x[:, :512] + x[:, 512:]
    out_ref[0, :, :, 512:] = dot3_left(y[:, :256] + y[:, 256:], w0_ref[...]).reshape(2, 256, 256)


def small_kernel(x_ref, w2_ref, out_ref):
    x = x_ref[0].reshape(512, L)
    y = x[:, :512] + x[:, 512:]
    out_ref[0] = dot3_left(y[:, :256] - y[:, 256:], w2_ref[...]).reshape(2, 256, 256)


def along(kernel, stored, tables, columns, interpret=False):
    tiles, planes = stored.shape[:2]
    return pl.pallas_call(
        kernel,
        out_shape=jax.ShapeDtypeStruct((tiles, planes, 256, columns), F32),
        grid_spec=pl.GridSpec(
            grid=(tiles,),
            in_specs=[pl.BlockSpec((1, planes, 256, L), lambda i: (i, 0, 0, 0))]
            + [whole(t.shape) for t in tables],
            out_specs=pl.BlockSpec((1, planes, 256, columns), lambda i: (i, 0, 0, 0)),
        ),
        cost_estimate=pl.CostEstimate(flops=6_000_000 * columns, bytes_accessed=14_000_000, transcendentals=0),
        interpret=interpret,
    )(stored, *tables)


def across(y_ref, first, count, offset, table):
    later = lax.broadcasted_iota(jnp.int32, (A, 256), 0) >= offset
    picked = [jnp.where(later, y_ref[first + k, :A, :], y_ref[first + k, A:, :]) for k in range(count)]
    real = jnp.concatenate([p[:, :128] for p in picked], axis=1)
    imag = jnp.concatenate([p[:, 128:] for p in picked], axis=1)
    return dot3_right(table, jnp.concatenate((real, imag), axis=0))


def send_kernel(count, steps, src_ref, round_ref, tile_ref, off_ref, *refs):
    x_refs, a_ref, outs = refs[:count], refs[count], refs[count + 1 :]
    i = pl.program_id(0)
    later = lax.broadcasted_iota(jnp.int32, (A, 256), 0) >= off_ref[round_ref[i], tile_ref[i]]
    first = 0
    for x_ref in x_refs:
        blocks = x_ref.shape[3] // 256
        picked = [
            jnp.where(later, x_ref[0, p, :A, w * 256 : (w + 1) * 256], x_ref[0, p, A:, w * 256 : (w + 1) * 256])
            for p in range(2)
            for w in range(blocks)
        ]
        real = jnp.concatenate([p[:, :128] for p in picked], axis=1)
        imag = jnp.concatenate([p[:, 128:] for p in picked], axis=1)
        spec = dot3_right(a_ref[0, 0], jnp.concatenate((real, imag), axis=0))
        for step in range(steps):
            @pl.when(i == step)
            def _(step=step, first=first, spec=spec, blocks=blocks):
                for k in range(2 * blocks):
                    outs[step][k // blocks, first + k % blocks] = spec[:, k * 128 : (k + 1) * 128]

        first += blocks


def spectra(xs, sources, rounds, tiles, offs, mats, interpret=False):
    steps = len(sources)
    blocks = sum(x.shape[3] for x in xs) // 256
    shape = (2, blocks, 256, 128)

    def array(values):
        return jnp.stack([jnp.asarray(v, jnp.int32) for v in values])

    return pl.pallas_call(
        functools.partial(send_kernel, len(xs), steps),
        out_shape=(jax.ShapeDtypeStruct(shape, F32),) * steps,
        grid_spec=pltpu.PrefetchScalarGridSpec(
            num_scalar_prefetch=4,
            grid=(steps,),
            in_specs=[
                pl.BlockSpec((1, 2, 256, x.shape[3]), lambda i, s, r, t, o: (s[i], 0, 0, 0)) for x in xs
            ]
            + [pl.BlockSpec((1, 1, 256, 768), lambda i, s, r, t, o: (r[i], t[i], 0, 0))],
            out_specs=(whole(shape),) * steps,
        ),
        cost_estimate=pl.CostEstimate(
            flops=100_000_000 * blocks * steps, bytes_accessed=800_000 * blocks * steps, transcendentals=0
        ),
        interpret=interpret,
    )(array(sources), array(rounds), array(tiles), offs, *xs, mats)


def normalized(p, q, sign):
    real = p[0] * q[0] + p[1] * q[1]
    imag = p[1] * q[0] - p[0] * q[1]
    scale = lax.rsqrt(jnp.maximum(real * real + imag * imag, FLOOR * FLOOR)) * sign
    return (real * scale, imag * scale)


def to_lanes(block_of, part):
    lane = lax.broadcasted_iota(jnp.int32, (A, 128), 1)
    out = jnp.zeros((A, 128), F32)
    for z in range(Z):
        block = block_of(z, slice(part * A, (part + 1) * A))
        if z:
            block = pltpu.roll(block, z, 1)
        out = jnp.where(lane == z, block, out)
    return out


def edge_fix(own_of, far_of, r_ref, ef_ref, er_ref, flip_ref, sign):
    high = lax.Precision.HIGHEST

    def edge(block_of):
        packed = jnp.concatenate([to_lanes(block_of, part) for part in range(2)], axis=1)
        here = jnp.dot(packed, ef_ref[...], precision=high, preferred_element_type=F32)
        turned = jnp.dot(packed, er_ref[...], precision=high, preferred_element_type=F32)
        there = jnp.dot(flip_ref[...], turned, precision=high, preferred_element_type=F32)
        hr, hi = here[:, :128], here[:, 128:]
        tr, ti = there[:, :128], there[:, 128:]
        return ((hr + tr) * 0.5, (hi - ti) * 0.5), ((hi + ti) * 0.5, (tr - hr) * 0.5)

    own_zero, own_last = edge(own_of)
    far_zero, far_last = edge(far_of)
    zero = normalized(own_zero, far_zero, sign)
    last = normalized(own_last, far_last, sign)
    both = jnp.concatenate((zero[0] - last[1], zero[1] + last[0]), axis=1)
    field = jnp.dot(both, er_ref[...], precision=high, preferred_element_type=F32)
    lane = lax.broadcasted_iota(jnp.int32, (A, 128), 1)
    for part in range(2):
        source = field[:, part * 128 : (part + 1) * 128]
        for z in range(Z):
            moved = pltpu.roll(source, 128 - z, 1) if z else source
            place = (slice(part * A, (part + 1) * A), slice(z * 128, (z + 1) * 128))
            r_ref[place] = jnp.where(lane == 0, moved, r_ref[place])


def arrange(slab, far_refs, far_scr):
    for turn in range(4):
        target = lax.rem(slab + turn, 4)
        far_scr[pl.ds(target, 1)] = far_refs[turn][:, 0][None]


def pair_core(offset, slab, y_ref, far_refs, a_ref, own_ref, r_ref, far_scr, valid):
    if far_refs is not None:
        arrange(slab, far_refs, far_scr)
    for half in range(2):
        own_ref[:, half * 512 : (half + 1) * 512] = across(y_ref, half * 4, 4, offset, a_ref[...])

    def own_of(z, rows):
        return own_ref[rows, z * 128 : (z + 1) * 128]

    def far_of(z, rows):
        return far_scr[z // 2, z % 2, rows, :]

    def chunk(i, _):
        up = pl.ds(pl.multiple_of(i * 8, 8), 8)
        down = pl.ds(pl.multiple_of(i * 8 + A, 8), 8)
        own = dft8([(own_of(z, up), own_of(z, down)) for z in range(Z)], -1.0)
        far = dft8([(far_of(z, up), far_of(z, down)) for z in range(Z)], -1.0)
        back = dft8([normalized(own[u], far[u], valid) for u in range(Z)], 1.0)
        for z in range(Z):
            r_ref[up, z * 128 : (z + 1) * 128] = back[z][0]
            r_ref[down, z * 128 : (z + 1) * 128] = back[z][1]
        return 0

    lax.fori_loop(0, A // 8, chunk, 0)
    return own_of, far_of


def parts(ab_ref, r_ref, v_ref):
    for half in range(2):
        q = dot3_right(ab_ref[...], r_ref[:, half * 512 : (half + 1) * 512])
        for k in range(0, 4, 2):
            rows = [
                jnp.concatenate((q[:A, j * 128 : (j + 1) * 128], q[A:, j * 128 : (j + 1) * 128]), axis=1)
                for j in (k, k + 1)
            ]
            yield half * 4 + k, dot3_left(jnp.concatenate(rows, axis=0), v_ref[...])


def large_pair_kernel(
    ints_ref, y_ref, f0_ref, f1_ref, f2_ref, f3_ref, a_ref, ab_ref, v1_ref, v0_ref, ef_ref, er_ref, flip_ref, *refs
):
    odd_ref, fours_ref, own_ref, r_ref, far_scr = refs[-5:]
    step = pl.program_id(0)
    valid = ints_ref[1].astype(F32)
    own_of, far_of = pair_core(
        ints_ref[0], ints_ref[2], y_ref, (f0_ref, f1_ref, f2_ref, f3_ref), a_ref, own_ref, r_ref, far_scr, valid
    )

    @pl.when(step == 0)
    def _():
        for z, part in parts(ab_ref, r_ref, v1_ref.at[0]):
            odd_ref[0, z : z + 2] = part.reshape(2, A, 512)

    @pl.when(step == 1)
    def _():
        for z, part in parts(ab_ref, r_ref, v1_ref.at[0]):
            odd_ref[0, z : z + 2] += part.reshape(2, A, 512)

    @pl.when(step == 2)
    def _():
        edge_fix(own_of, far_of, r_ref, ef_ref, er_ref, flip_ref, valid)
        for z, part in parts(ab_ref, r_ref, v0_ref):
            fours_ref[0, z : z + 2] = part.reshape(2, A, 256)


def small_pair_kernel(own_ref_s, valid_ref, slab_ref, y_ref, *refs):
    zero_refs, one_refs = refs[:4], refs[4:8]
    a_ref, ab_ref, v2_ref, odd_ref, fours_ref, surf_ref, peak_ref, own_ref, r_ref, far_scr = refs[8:]
    rnd = pl.program_id(0)
    valid = valid_ref[rnd].astype(F32)

    @pl.when(rnd == 0)
    def _():
        arrange(slab_ref[0], zero_refs, far_scr)

    @pl.when(rnd == 1)
    def _():
        arrange(slab_ref[0], one_refs, far_scr)

    pair_core(own_ref_s[rnd], None, y_ref, None, a_ref.at[0], own_ref, r_ref, far_scr, valid)
    for z, part in parts(ab_ref, r_ref, v2_ref):
        first = fours_ref[0, z : z + 2].reshape(2 * A, 256)
        odd = odd_ref[0, z : z + 2].reshape(2 * A, 512)
        y = jnp.concatenate((first + part, first - part), axis=1)
        x = jnp.concatenate((y + odd, y - odd), axis=1)
        x = jnp.maximum(x[:A], x[A:])
        if z == 0:
            surf_ref[0, 0] = x
        else:
            surf_ref[0, 0] = jnp.maximum(surf_ref[0, 0], x)
    peak_ref[0, rnd] = jnp.max(surf_ref[0, 0])


SCRATCH = [pltpu.VMEM((256, Z * 128), F32)] * 2 + [pltpu.VMEM((4, 2, 256, 128), F32)]


def large_pair(rnd, ints, y, far, mat, ab, back1, back0, edges, before, interpret=False):
    args = [y, *far, mat, ab, back1, back0, *edges]
    in_specs = [
        pl.BlockSpec((Z, 256, 256), lambda w, *_: (0, 0, w)),
        *[pl.BlockSpec((2, 1, 256, 128), lambda w, *_: (0, w, 0, 0))] * 4,
        whole((256, 768)),
        whole((256, 768)),
        pl.BlockSpec((1, 768, 512), lambda w, *_: (jnp.minimum(w, 1), 0, 0)),
        whole((768, 256)),
        whole((256, 256)),
        whole((256, 256)),
        whole((128, 128)),
    ]
    aliases = {}
    if before is not None:
        aliases = {len(args) + 1: 0, len(args) + 2: 1}
        args += list(before)
        in_specs += [pl.BlockSpec(memory_space=pl.ANY)] * 2
    return pl.pallas_call(
        large_pair_kernel,
        out_shape=(
            jax.ShapeDtypeStruct((ROUNDS, Z, A, 512), F32),
            jax.ShapeDtypeStruct((ROUNDS, Z, A, 256), F32),
        ),
        grid_spec=pltpu.PrefetchScalarGridSpec(
            num_scalar_prefetch=1,
            grid=(3,),
            in_specs=in_specs,
            out_specs=(
                pl.BlockSpec((1, Z, A, 512), lambda w, *_: (rnd, 0, 0, 0)),
                pl.BlockSpec((1, Z, A, 256), lambda w, *_: (rnd, 0, 0, 0)),
            ),
            scratch_shapes=SCRATCH,
        ),
        input_output_aliases=aliases,
        cost_estimate=pl.CostEstimate(flops=6_000_000_000, bytes_accessed=16_000_000, transcendentals=500_000),
        interpret=interpret,
    )(ints, *args)


def small_pair(own, valid, slab, y, far, mats, ab, back2, odd, fours, interpret=False):
    flat = [*far[0], *far[1]]
    return pl.pallas_call(
        small_pair_kernel,
        out_shape=(
            jax.ShapeDtypeStruct((ROUNDS, 1, A, L), F32),
            jax.ShapeDtypeStruct((1, ROUNDS), F32),
        ),
        grid_spec=pltpu.PrefetchScalarGridSpec(
            num_scalar_prefetch=3,
            grid=(ROUNDS,),
            in_specs=[
                whole((Z, 256, 256)),
                *[pl.BlockSpec((2, 1, 256, 128), lambda r, *_, last=x.shape[1] - 1: (0, last, 0, 0)) for x in flat],
                pl.BlockSpec((1, 256, 768), lambda r, *_: (r, 0, 0)),
                whole((256, 768)),
                whole((768, 256)),
                pl.BlockSpec((1, Z, A, 512), lambda r, *_: (r, 0, 0, 0)),
                pl.BlockSpec((1, Z, A, 256), lambda r, *_: (r, 0, 0, 0)),
            ],
            out_specs=(
                pl.BlockSpec((1, 1, A, L), lambda r, *_: (r, 0, 0, 0)),
                pl.BlockSpec(memory_space=pltpu.SMEM),
            ),
            scratch_shapes=SCRATCH,
        ),
        cost_estimate=pl.CostEstimate(flops=4_000_000_000, bytes_accessed=16_000_000, transcendentals=500_000),
        interpret=interpret,
        name="small_pairs",
    )(own, valid, slab, y, *flat, mats, ab, back2, odd, fours)


def after(*values):
    return lax.optimization_barrier(values)


DIRECT = (0, 1, 3)


def routes(groups, slabs, rnd, tile_of):
    pairs = []
    for g in range(groups):
        for s in range(slabs):
            i = tile_of(s)
            if rnd == 0:
                to, j = g - (i == 0), (i - 1) % slabs
            else:
                to, j = g - (1 if i == slabs - 1 else 2), (i + 1) % slabs
            if to >= 0:
                pairs.append((slabs * g + s, slabs * to + j))
    return pairs


def register(stored, offsets):
    size = lax.axis_size(("tile", "slab"))
    groups = lax.axis_size("tile")
    slabs = lax.axis_size("slab")
    slab = lax.axis_index("slab")
    place = lax.axis_index(("tile", "slab"))

    def gather(x):
        return lax.all_to_all(x, "slab", split_axis=0, concat_axis=1, tiled=True)[0]

    def send(x, rnd, tile_of):
        return lax.ppermute(x, ("tile", "slab"), routes(groups, slabs, rnd, tile_of))

    large_src = along(large_kernel, stored, (odd_table(), fours_table()), 768)
    large_all = gather(large_src)
    mine = offsets[:, 1, 0]
    turns = [mine] + [lax.ppermute(mine, "slab", [((i + k) % slabs, i) for i in range(slabs)]) for k in range(1, slabs)]
    small_src = along(small_kernel, stored, (twos_table(),), 256)
    base = lax.optimization_barrier(across_base())
    given = jnp.roll(jnp.stack(turns, axis=1), slab, axis=1)
    mats = jnp.stack(
        [jnp.stack([across_forward(given[r, j], base) for j in range(slabs)]) for r in range(ROUNDS)]
    )

    def shift_of(rnd, k):
        return 1 - k if rnd == 0 else -1 - k

    far = [[None] * slabs for _ in range(ROUNDS)]
    two_tiles = [(slab + shift_of(r, 2) + slabs) % slabs for r in range(ROUNDS)]
    made = spectra([small_src], two_tiles, [0, 1], two_tiles, given, mats)
    small_two = [
        send(x, r, lambda s, r=r: (s + shift_of(r, 2)) % slabs) for r, x in enumerate(made)
    ]
    for r in range(ROUNDS):
        tiles = [(slab + shift_of(r, k) + slabs) % slabs for k in DIRECT]
        made = spectra([large_src, small_src], tiles, [r] * 3, tiles, given, mats)
        for k, x in zip(DIRECT, made, strict=True):
            far[r][k] = send(x, r, lambda s, r=r, k=k: (s + shift_of(r, k)) % slabs)
    SEEDS.append(made[0])
    valid = (
        jnp.logical_and(place % GC != GC - 1, place + 1 < size),
        place + GC < size,
    )
    own = [offsets[r, 0, 0] for r in range(ROUNDS)]
    ints = [jnp.stack((own[r], valid[r].astype(jnp.int32), slab)) for r in range(ROUNDS)]
    own_mats = [across_forward(o, base) for o in own]
    ab = across_back()
    edges = edge_tables()
    back1, back0, back2 = odd_back(), fours_back(), twos_back()
    SEEDS.clear()
    large_all, band_src = after(large_all, small_src)
    small_all = gather(band_src)

    def relayed(x):
        whole_band = x.reshape(slabs, 2, 256, x.shape[2])
        both = spectra(
            [whole_band], [(slab + 1) % slabs, (slab + slabs - 1) % slabs], [0, 1], [slab, slab], given, mats
        )
        return [send(both[r], r, lambda s: s) for r in range(ROUNDS)]

    large_two = relayed(large_all)

    def around(r, two):
        return [far[r][0], far[r][1], two[r], far[r][3]]

    sums = None
    for r in range(ROUNDS):
        sums = large_pair(r, ints[r], large_all, around(r, large_two), own_mats[r], ab, back1, back0, edges, sums)
    surface, peak = small_pair(
        jnp.stack(own),
        jnp.stack([v.astype(jnp.int32) for v in valid]),
        jnp.stack([slab]),
        small_all,
        [around(r, small_two) for r in range(ROUNDS)],
        jnp.stack(own_mats),
        ab,
        back2,
        *sums,
    )
    return surface, peak.reshape(ROUNDS, 1)


def solution(mesh):
    return jax.shard_map(
        register,
        mesh=mesh,
        in_specs=(P("tile", "slab", None, None), P(None, None, ("tile", "slab"))),
        out_specs=(P(None, ("tile", "slab"), None, None), P(None, ("tile", "slab"))),
        check_vma=False,
    )
```

```python
import functools
import math

import jax
import jax.numpy as jnp
from jax import lax
from jax.experimental import pallas as pl
from jax.experimental.pallas import tpu as pltpu
from jax.sharding import PartitionSpec as P


GC = 7
ROUNDS = 2
A = 128
L = 1024
Z = 8
FLOOR = 0.25
BF = jnp.bfloat16
F32 = jnp.float32
HALF = math.sqrt(0.5)


def split(x):
    hi = x.astype(BF)
    lo = (x - hi.astype(F32)).astype(BF)
    return hi, lo


def split_table(x):
    hi = lax.reduce_precision(x, exponent_bits=8, mantissa_bits=7)
    return hi.astype(BF), (x - hi).astype(BF)


def three_rows(x):
    hi, lo = split_table(x)
    return jnp.concatenate((hi, hi, lo), axis=0)


def three_cols(x):
    hi, lo = split_table(x)
    return jnp.concatenate((hi, hi, lo), axis=1)


def trig(index, total):
    angle = (index % total).astype(F32) * (2.0 * math.pi / total)
    return jnp.cos(angle), jnp.sin(angle)


SEEDS = []


def iota(length):
    return lax.optimization_barrier((jnp.arange(length, dtype=jnp.int32), *SEEDS))[0]


def odd_table():
    rows = iota(512)[:, None]
    m = iota(256)[None, :]
    c, s = trig(rows * (2 * m + 1), L)
    scale = 1.0 / L
    return three_rows(
        scale * jnp.concatenate((c[:, :128], -s[:, :128], c[:, 128:], -s[:, 128:]), axis=1)
    )


def fours_table():
    n = iota(256)[:, None]
    m = iota(A)[None, :]
    c, s = trig(n * (4 * m), L)
    last = (1 - 2 * (n % 2)).astype(F32)
    return three_rows((1.0 / L) * jnp.concatenate((c, jnp.where(m == 0, last, -s)), axis=1))


def twos_table():
    n = iota(256)[:, None]
    m = iota(A)[None, :]
    c, s = trig(n * (4 * m + 2), L)
    return three_rows((1.0 / L) * jnp.concatenate((c, -s), axis=1))


def odd_back():
    cols = iota(512)[None, :]
    m = iota(256)[:, None]
    c, s = trig(cols * (2 * m + 1), L)
    scale = 2.0 / L
    return jnp.stack(
        [three_rows(scale * jnp.concatenate((c[b : b + A], -s[b : b + A]), axis=0)) for b in (0, A)]
    )


def fours_back():
    cols = iota(256)[None, :]
    m = iota(A)[:, None]
    c, s = trig(cols * (4 * m), L)
    last = (1 - 2 * (cols % 2)).astype(F32)
    scale = 2.0 / L
    real = jnp.where(m == 0, 0.5 * scale, scale * c)
    imag = jnp.where(m == 0, 0.5 * scale * last, -scale * s)
    return three_rows(jnp.concatenate((real, imag), axis=0))


def twos_back():
    cols = iota(256)[None, :]
    m = iota(A)[:, None]
    c, s = trig(cols * (4 * m + 2), L)
    return three_rows((2.0 / L) * jnp.concatenate((c, -s), axis=0))


def across_base():
    v = iota(A)
    return trig(v[:, None] * v[None, :], A)


def across_forward(offset, base):
    c0, s0 = base
    cv, sv = trig(offset * iota(A)[:, None], A)
    c = c0 * cv + s0 * sv
    s = s0 * cv - c0 * sv
    top = jnp.concatenate((c, s), axis=1)
    low = jnp.concatenate((-s, c), axis=1)
    return three_cols(jnp.concatenate((top, low), axis=0))


def across_back():
    v = iota(A)[None, :]
    a = iota(A)[:, None]
    c, s = trig(a * v, A)
    top = jnp.concatenate((c, -s), axis=1)
    low = jnp.concatenate((s, c), axis=1)
    return three_cols(jnp.concatenate((top, low), axis=0))


def edge_tables():
    lane = iota(A)
    i = lane[:, None]
    j = lane[None, :]
    inside = jnp.logical_and(i < Z, j < Z)
    c, s = trig(i * j, Z)
    c = jnp.where(inside, c, 0.0)
    s = jnp.where(inside, s, 0.0)
    fwd = jnp.concatenate(
        (jnp.concatenate((c, -s), axis=1), jnp.concatenate((s, c), axis=1)), axis=0
    )
    rev = jnp.concatenate(
        (jnp.concatenate((c, s), axis=1), jnp.concatenate((-s, c), axis=1)), axis=0
    )
    flip = ((i + j) % A == 0).astype(F32)
    return fwd, rev, flip


def dot3_left(x, table):
    hi, lo = split(x)
    return jnp.dot(jnp.concatenate((hi, lo, hi), axis=1), table, preferred_element_type=F32)


def dot3_right(table, x):
    hi, lo = split(x)
    return jnp.dot(table, jnp.concatenate((hi, lo, hi), axis=0), preferred_element_type=F32)


def whole(shape):
    return pl.BlockSpec(shape, lambda *_: (0,) * len(shape))


def times_i(x, sign):
    return (-sign * x[1], sign * x[0])


def cadd(x, y):
    return (x[0] + y[0], x[1] + y[1])


def csub(x, y):
    return (x[0] - y[0], x[1] - y[1])


def eighth(x, sign):
    return ((x[0] - sign * x[1]) * HALF, (x[1] + sign * x[0]) * HALF)


def dft4(x, sign):
    a = cadd(x[0], x[2])
    b = csub(x[0], x[2])
    c = cadd(x[1], x[3])
    d = times_i(csub(x[1], x[3]), sign)
    return [cadd(a, c), cadd(b, d), csub(a, c), csub(b, d)]


def dft8(x, sign):
    even = dft4([x[0], x[2], x[4], x[6]], sign)
    odd = dft4([x[1], x[3], x[5], x[7]], sign)
    odd = [odd[0], eighth(odd[1], sign), times_i(odd[2], sign), times_i(eighth(odd[3], sign), sign)]
    return [cadd(even[k], odd[k]) for k in range(4)] + [csub(even[k], odd[k]) for k in range(4)]


def large_kernel(x_ref, w1_ref, w0_ref, out_ref):
    x = x_ref[0].reshape(512, L)
    out_ref[0, :, :, :512] = dot3_left(x[:, :512] - x[:, 512:], w1_ref[...]).reshape(2, 256, 512)
    y = x[:, :512] + x[:, 512:]
    out_ref[0, :, :, 512:] = dot3_left(y[:, :256] + y[:, 256:], w0_ref[...]).reshape(2, 256, 256)


def small_kernel(x_ref, w2_ref, out_ref):
    x = x_ref[0].reshape(512, L)
    y = x[:, :512] + x[:, 512:]
    out_ref[0] = dot3_left(y[:, :256] - y[:, 256:], w2_ref[...]).reshape(2, 256, 256)


def along(kernel, stored, tables, columns, interpret=False):
    tiles, planes = stored.shape[:2]
    return pl.pallas_call(
        kernel,
        out_shape=jax.ShapeDtypeStruct((tiles, planes, 256, columns), F32),
        grid_spec=pl.GridSpec(
            grid=(tiles,),
            in_specs=[pl.BlockSpec((1, planes, 256, L), lambda i: (i, 0, 0, 0))]
            + [whole(t.shape) for t in tables],
            out_specs=pl.BlockSpec((1, planes, 256, columns), lambda i: (i, 0, 0, 0)),
        ),
        cost_estimate=pl.CostEstimate(flops=6_000_000 * columns, bytes_accessed=14_000_000, transcendentals=0),
        interpret=interpret,
    )(stored, *tables)


def across(y_ref, first, count, offset, table):
    later = lax.broadcasted_iota(jnp.int32, (A, 256), 0) >= offset
    picked = [jnp.where(later, y_ref[first + k, :A, :], y_ref[first + k, A:, :]) for k in range(count)]
    real = jnp.concatenate([p[:, :128] for p in picked], axis=1)
    imag = jnp.concatenate([p[:, 128:] for p in picked], axis=1)
    return dot3_right(table, jnp.concatenate((real, imag), axis=0))


def send_kernel(count, steps, src_ref, round_ref, tile_ref, off_ref, *refs):
    x_refs, a_ref, outs = refs[:count], refs[count], refs[count + 1 :]
    i = pl.program_id(0)
    later = lax.broadcasted_iota(jnp.int32, (A, 256), 0) >= off_ref[round_ref[i], tile_ref[i]]
    first = 0
    for x_ref in x_refs:
        blocks = x_ref.shape[3] // 256
        picked = [
            jnp.where(later, x_ref[0, p, :A, w * 256 : (w + 1) * 256], x_ref[0, p, A:, w * 256 : (w + 1) * 256])
            for p in range(2)
            for w in range(blocks)
        ]
        real = jnp.concatenate([p[:, :128] for p in picked], axis=1)
        imag = jnp.concatenate([p[:, 128:] for p in picked], axis=1)
        spec = dot3_right(a_ref[0, 0], jnp.concatenate((real, imag), axis=0))
        for step in range(steps):
            @pl.when(i == step)
            def _(step=step, first=first, spec=spec, blocks=blocks):
                for k in range(2 * blocks):
                    outs[step][k // blocks, first + k % blocks] = spec[:, k * 128 : (k + 1) * 128]

        first += blocks


def spectra(xs, sources, rounds, tiles, offs, mats, interpret=False):
    steps = len(sources)
    blocks = sum(x.shape[3] for x in xs) // 256
    shape = (2, blocks, 256, 128)

    def array(values):
        return jnp.stack([jnp.asarray(v, jnp.int32) for v in values])

    return pl.pallas_call(
        functools.partial(send_kernel, len(xs), steps),
        out_shape=(jax.ShapeDtypeStruct(shape, F32),) * steps,
        grid_spec=pltpu.PrefetchScalarGridSpec(
            num_scalar_prefetch=4,
            grid=(steps,),
            in_specs=[
                pl.BlockSpec((1, 2, 256, x.shape[3]), lambda i, s, r, t, o: (s[i], 0, 0, 0)) for x in xs
            ]
            + [pl.BlockSpec((1, 1, 256, 768), lambda i, s, r, t, o: (r[i], t[i], 0, 0))],
            out_specs=(whole(shape),) * steps,
        ),
        cost_estimate=pl.CostEstimate(
            flops=100_000_000 * blocks * steps, bytes_accessed=800_000 * blocks * steps, transcendentals=0
        ),
        interpret=interpret,
    )(array(sources), array(rounds), array(tiles), offs, *xs, mats)


def normalized(p, q, sign):
    real = p[0] * q[0] + p[1] * q[1]
    imag = p[1] * q[0] - p[0] * q[1]
    scale = lax.rsqrt(jnp.maximum(real * real + imag * imag, FLOOR * FLOOR)) * sign
    return (real * scale, imag * scale)


def to_lanes(block_of, part):
    lane = lax.broadcasted_iota(jnp.int32, (A, 128), 1)
    out = jnp.zeros((A, 128), F32)
    for z in range(Z):
        block = block_of(z, slice(part * A, (part + 1) * A))
        if z:
            block = pltpu.roll(block, z, 1)
        out = jnp.where(lane == z, block, out)
    return out


def edge_fix(own_of, far_of, r_ref, ef_ref, er_ref, flip_ref, sign):
    high = lax.Precision.HIGHEST

    def edge(block_of):
        packed = jnp.concatenate([to_lanes(block_of, part) for part in range(2)], axis=1)
        here = jnp.dot(packed, ef_ref[...], precision=high, preferred_element_type=F32)
        turned = jnp.dot(packed, er_ref[...], precision=high, preferred_element_type=F32)
        there = jnp.dot(flip_ref[...], turned, precision=high, preferred_element_type=F32)
        hr, hi = here[:, :128], here[:, 128:]
        tr, ti = there[:, :128], there[:, 128:]
        return ((hr + tr) * 0.5, (hi - ti) * 0.5), ((hi + ti) * 0.5, (tr - hr) * 0.5)

    own_zero, own_last = edge(own_of)
    far_zero, far_last = edge(far_of)
    zero = normalized(own_zero, far_zero, sign)
    last = normalized(own_last, far_last, sign)
    both = jnp.concatenate((zero[0] - last[1], zero[1] + last[0]), axis=1)
    field = jnp.dot(both, er_ref[...], precision=high, preferred_element_type=F32)
    lane = lax.broadcasted_iota(jnp.int32, (A, 128), 1)
    for part in range(2):
        source = field[:, part * 128 : (part + 1) * 128]
        for z in range(Z):
            moved = pltpu.roll(source, 128 - z, 1) if z else source
            place = (slice(part * A, (part + 1) * A), slice(z * 128, (z + 1) * 128))
            r_ref[place] = jnp.where(lane == 0, moved, r_ref[place])


def arrange(slab, far_refs, far_scr):
    for turn in range(4):
        target = lax.rem(slab + turn, 4)
        far_scr[pl.ds(target, 1)] = far_refs[turn][:, 0][None]


def pair_core(offset, slab, y_ref, far_refs, a_ref, own_ref, r_ref, far_scr, valid):
    if far_refs is not None:
        arrange(slab, far_refs, far_scr)
    for half in range(2):
        own_ref[:, half * 512 : (half + 1) * 512] = across(y_ref, half * 4, 4, offset, a_ref[...])

    def own_of(z, rows):
        return own_ref[rows, z * 128 : (z + 1) * 128]

    def far_of(z, rows):
        return far_scr[z // 2, z % 2, rows, :]

    def chunk(i, _):
        up = pl.ds(pl.multiple_of(i * 8, 8), 8)
        down = pl.ds(pl.multiple_of(i * 8 + A, 8), 8)
        own = dft8([(own_of(z, up), own_of(z, down)) for z in range(Z)], -1.0)
        far = dft8([(far_of(z, up), far_of(z, down)) for z in range(Z)], -1.0)
        back = dft8([normalized(own[u], far[u], valid) for u in range(Z)], 1.0)
        for z in range(Z):
            r_ref[up, z * 128 : (z + 1) * 128] = back[z][0]
            r_ref[down, z * 128 : (z + 1) * 128] = back[z][1]
        return 0

    lax.fori_loop(0, A // 8, chunk, 0)
    return own_of, far_of


def parts(ab_ref, r_ref, v_ref):
    for half in range(2):
        q = dot3_right(ab_ref[...], r_ref[:, half * 512 : (half + 1) * 512])
        for k in range(0, 4, 2):
            rows = [
                jnp.concatenate((q[:A, j * 128 : (j + 1) * 128], q[A:, j * 128 : (j + 1) * 128]), axis=1)
                for j in (k, k + 1)
            ]
            yield half * 4 + k, dot3_left(jnp.concatenate(rows, axis=0), v_ref[...])


def large_pair_kernel(
    ints_ref, y_ref, f0_ref, f1_ref, f2_ref, f3_ref, a_ref, ab_ref, v1_ref, v0_ref, ef_ref, er_ref, flip_ref, *refs
):
    odd_ref, fours_ref, own_ref, r_ref, far_scr = refs[-5:]
    step = pl.program_id(0)
    valid = ints_ref[1].astype(F32)
    own_of, far_of = pair_core(
        ints_ref[0], ints_ref[2], y_ref, (f0_ref, f1_ref, f2_ref, f3_ref), a_ref, own_ref, r_ref, far_scr, valid
    )

    @pl.when(step == 0)
    def _():
        for z, part in parts(ab_ref, r_ref, v1_ref.at[0]):
            odd_ref[0, z : z + 2] = part.reshape(2, A, 512)

    @pl.when(step == 1)
    def _():
        for z, part in parts(ab_ref, r_ref, v1_ref.at[0]):
            odd_ref[0, z : z + 2] += part.reshape(2, A, 512)

    @pl.when(step == 2)
    def _():
        edge_fix(own_of, far_of, r_ref, ef_ref, er_ref, flip_ref, valid)
        for z, part in parts(ab_ref, r_ref, v0_ref):
            fours_ref[0, z : z + 2] = part.reshape(2, A, 256)


def small_pair_kernel(own_ref_s, valid_ref, slab_ref, y_ref, *refs):
    zero_refs, one_refs = refs[:4], refs[4:8]
    a_ref, ab_ref, v2_ref, odd_ref, fours_ref, surf_ref, peak_ref, own_ref, r_ref, far_scr = refs[8:]
    rnd = pl.program_id(0)
    valid = valid_ref[rnd].astype(F32)

    @pl.when(rnd == 0)
    def _():
        arrange(slab_ref[0], zero_refs, far_scr)

    @pl.when(rnd == 1)
    def _():
        arrange(slab_ref[0], one_refs, far_scr)

    pair_core(own_ref_s[rnd], None, y_ref, None, a_ref.at[0], own_ref, r_ref, far_scr, valid)
    for z, part in parts(ab_ref, r_ref, v2_ref):
        first = fours_ref[0, z : z + 2].reshape(2 * A, 256)
        odd = odd_ref[0, z : z + 2].reshape(2 * A, 512)
        y = jnp.concatenate((first + part, first - part), axis=1)
        x = jnp.concatenate((y + odd, y - odd), axis=1)
        x = jnp.maximum(x[:A], x[A:])
        if z == 0:
            surf_ref[0, 0] = x
        else:
            surf_ref[0, 0] = jnp.maximum(surf_ref[0, 0], x)
    peak_ref[0, rnd] = jnp.max(surf_ref[0, 0])


SCRATCH = [pltpu.VMEM((256, Z * 128), F32)] * 2 + [pltpu.VMEM((4, 2, 256, 128), F32)]


def large_pair(rnd, ints, y, far, mat, ab, back1, back0, edges, before, interpret=False):
    args = [y, *far, mat, ab, back1, back0, *edges]
    in_specs = [
        pl.BlockSpec((Z, 256, 256), lambda w, *_: (0, 0, w)),
        *[pl.BlockSpec((2, 1, 256, 128), lambda w, *_: (0, w, 0, 0))] * 4,
        whole((256, 768)),
        whole((256, 768)),
        pl.BlockSpec((1, 768, 512), lambda w, *_: (jnp.minimum(w, 1), 0, 0)),
        whole((768, 256)),
        whole((256, 256)),
        whole((256, 256)),
        whole((128, 128)),
    ]
    aliases = {}
    if before is not None:
        aliases = {len(args) + 1: 0, len(args) + 2: 1}
        args += list(before)
        in_specs += [pl.BlockSpec(memory_space=pl.ANY)] * 2
    return pl.pallas_call(
        large_pair_kernel,
        out_shape=(
            jax.ShapeDtypeStruct((ROUNDS, Z, A, 512), F32),
            jax.ShapeDtypeStruct((ROUNDS, Z, A, 256), F32),
        ),
        grid_spec=pltpu.PrefetchScalarGridSpec(
            num_scalar_prefetch=1,
            grid=(3,),
            in_specs=in_specs,
            out_specs=(
                pl.BlockSpec((1, Z, A, 512), lambda w, *_: (rnd, 0, 0, 0)),
                pl.BlockSpec((1, Z, A, 256), lambda w, *_: (rnd, 0, 0, 0)),
            ),
            scratch_shapes=SCRATCH,
        ),
        input_output_aliases=aliases,
        cost_estimate=pl.CostEstimate(flops=6_000_000_000, bytes_accessed=16_000_000, transcendentals=500_000),
        interpret=interpret,
    )(ints, *args)


def small_pair(own, valid, slab, y, far, mats, ab, back2, odd, fours, interpret=False):
    flat = [*far[0], *far[1]]
    return pl.pallas_call(
        small_pair_kernel,
        out_shape=(
            jax.ShapeDtypeStruct((ROUNDS, 1, A, L), F32),
            jax.ShapeDtypeStruct((1, ROUNDS), F32),
        ),
        grid_spec=pltpu.PrefetchScalarGridSpec(
            num_scalar_prefetch=3,
            grid=(ROUNDS,),
            in_specs=[
                whole((Z, 256, 256)),
                *[pl.BlockSpec((2, 1, 256, 128), lambda r, *_, last=x.shape[1] - 1: (0, last, 0, 0)) for x in flat],
                pl.BlockSpec((1, 256, 768), lambda r, *_: (r, 0, 0)),
                whole((256, 768)),
                whole((768, 256)),
                pl.BlockSpec((1, Z, A, 512), lambda r, *_: (r, 0, 0, 0)),
                pl.BlockSpec((1, Z, A, 256), lambda r, *_: (r, 0, 0, 0)),
            ],
            out_specs=(
                pl.BlockSpec((1, 1, A, L), lambda r, *_: (r, 0, 0, 0)),
                pl.BlockSpec(memory_space=pltpu.SMEM),
            ),
            scratch_shapes=SCRATCH,
        ),
        cost_estimate=pl.CostEstimate(flops=4_000_000_000, bytes_accessed=16_000_000, transcendentals=500_000),
        interpret=interpret,
        name="small_pairs",
    )(own, valid, slab, y, *flat, mats, ab, back2, odd, fours)


def after(*values):
    return lax.optimization_barrier(values)


DIRECT = (0, 1, 3)


def routes(groups, slabs, rnd, tile_of):
    pairs = []
    for g in range(groups):
        for s in range(slabs):
            i = tile_of(s)
            if rnd == 0:
                to, j = g - (i == 0), (i - 1) % slabs
            else:
                to, j = g - (1 if i == slabs - 1 else 2), (i + 1) % slabs
            if to >= 0:
                pairs.append((slabs * g + s, slabs * to + j))
    return pairs


def register(stored, offsets):
    size = lax.axis_size(("tile", "slab"))
    groups = lax.axis_size("tile")
    slabs = lax.axis_size("slab")
    slab = lax.axis_index("slab")
    place = lax.axis_index(("tile", "slab"))

    def gather(x):
        return lax.all_to_all(x, "slab", split_axis=0, concat_axis=1, tiled=True)[0]

    def send(x, rnd, tile_of):
        return lax.ppermute(x, ("tile", "slab"), routes(groups, slabs, rnd, tile_of))

    large_src = along(large_kernel, stored, (odd_table(), fours_table()), 768)
    large_all = gather(large_src)
    mine = offsets[:, 1, 0]
    turns = [mine] + [lax.ppermute(mine, "slab", [((i + k) % slabs, i) for i in range(slabs)]) for k in range(1, slabs)]
    small_src = along(small_kernel, stored, (twos_table(),), 256)
    base = lax.optimization_barrier(across_base())
    given = jnp.roll(jnp.stack(turns, axis=1), slab, axis=1)
    mats = jnp.stack(
        [jnp.stack([across_forward(given[r, j], base) for j in range(slabs)]) for r in range(ROUNDS)]
    )

    def shift_of(rnd, k):
        return 1 - k if rnd == 0 else -1 - k

    far = [[None] * slabs for _ in range(ROUNDS)]
    two_tiles = [(slab + shift_of(r, 2) + slabs) % slabs for r in range(ROUNDS)]
    made = spectra([small_src], two_tiles, [0, 1], two_tiles, given, mats)
    small_two = [
        send(x, r, lambda s, r=r: (s + shift_of(r, 2)) % slabs) for r, x in enumerate(made)
    ]
    for r in range(ROUNDS):
        tiles = [(slab + shift_of(r, k) + slabs) % slabs for k in DIRECT]
        made = spectra([large_src, small_src], tiles, [r] * 3, tiles, given, mats)
        for k, x in zip(DIRECT, made, strict=True):
            far[r][k] = send(x, r, lambda s, r=r, k=k: (s + shift_of(r, k)) % slabs)
    SEEDS.append(made[0])
    valid = (
        jnp.logical_and(place % GC != GC - 1, place + 1 < size),
        place + GC < size,
    )
    own = [offsets[r, 0, 0] for r in range(ROUNDS)]
    ints = [jnp.stack((own[r], valid[r].astype(jnp.int32), slab)) for r in range(ROUNDS)]
    own_mats = [across_forward(o, base) for o in own]
    ab = across_back()
    edges = edge_tables()
    back1, back0, back2 = odd_back(), fours_back(), twos_back()
    SEEDS.clear()

    def relayed(x):
        whole_band = x.reshape(slabs, 2, 256, x.shape[2])
        both = spectra(
            [whole_band], [(slab + 1) % slabs, (slab + slabs - 1) % slabs], [0, 1], [slab, slab], given, mats
        )
        out = []
        for r in range(ROUNDS):
            out.append(send(both[r], r, lambda s: s))
        return out

    large_two = relayed(large_all)
    large_two[0], band_src = after(large_two[0], small_src)
    small_all = gather(band_src)

    def around(r, two):
        return [far[r][0], far[r][1], two[r], far[r][3]]

    sums = None
    for r in range(ROUNDS):
        sums = large_pair(r, ints[r], large_all, around(r, large_two), own_mats[r], ab, back1, back0, edges, sums)
    surface, peak = small_pair(
        jnp.stack(own),
        jnp.stack([v.astype(jnp.int32) for v in valid]),
        jnp.stack([slab]),
        small_all,
        [around(r, small_two) for r in range(ROUNDS)],
        jnp.stack(own_mats),
        ab,
        back2,
        *sums,
    )
    return surface, peak.reshape(ROUNDS, 1)


def solution(mesh):
    return jax.shard_map(
        register,
        mesh=mesh,
        in_specs=(P("tile", "slab", None, None), P(None, None, ("tile", "slab"))),
        out_specs=(P(None, ("tile", "slab"), None, None), P(None, ("tile", "slab"))),
        check_vma=False,
    )
```
